32 devices in a mesh: ctx: 8 (over y, x, core), head: 4 (over z).
Axes of the slice: x: 2, y: 2, z: 4, core: 2. Of those that a mesh axis runs over, the one named last changes fastest.
Arguments:
- token_ids: int32 [2048], P('ctx'), may hold values from 0 to 31999
- labels: int32 [2048], P('ctx'), may hold values from 0 to 31999
- answer_mask: int32 [2048], P('ctx'), may hold values 0 or 1
- pair_map: int32 [8], replicated, may hold values from 0 to 7, each once
- w_layer: float32 [2048, 21504], P('ctx', 'head')
- w_vocab: float32 [2048, 64000], P('ctx', 'head')
- gains: float32 [2048, 3], P('ctx'), may hold values from 0.5 to 1.5
- mom_layer: float32 [2048, 21504], P('ctx', 'head'), may hold values from -1.1444092e-05 to 1.1444092e-05
- mom_vocab: float32 [2048, 64000], P('ctx', 'head'), may hold values from -1.1444092e-05 to 1.1444092e-05
- mom_gains: float32 [2048, 3], P('ctx'), may hold values from -1.1444092e-05 to 1.1444092e-05
- avg_layer: float32 [2048, 21504], P('ctx', 'head')
- avg_vocab: float32 [2048, 64000], P('ctx', 'head')
- avg_gains: float32 [2048, 3], P('ctx'), may hold values from 0.5 to 1.5
Outputs:
- layer_new: float32 [2048, 21504], P('ctx', 'head')
- layer_moment: float32 [2048, 21504], P('ctx', 'head')
- layer_average: float32 [2048, 21504], P('ctx', 'head')
- layer_copy: bfloat16 [2048, 21504], P('ctx', 'head')
- vocab_new: float32 [2048, 64000], P('ctx', 'head')
- vocab_moment: float32 [2048, 64000], P('ctx', 'head')
- vocab_average: float32 [2048, 64000], P('ctx', 'head')
- vocab_copy: bfloat16 [2048, 64000], P('ctx', 'head')
- gains_new: float32 [2048, 3], P('ctx')
- gains_moment: float32 [2048, 3], P('ctx')
- gains_average: float32 [2048, 3], P('ctx')
- gains_copy: bfloat16 [2048, 3], P('ctx')
- loss: float32 [], replicated
- grad_norm: float32 [], replicated
The draws below stay inside these ranges and needn't reach their ends.
Inputs may be any that keep to these rules, and one draw needn't show every extreme that they name: `pair_map`: each index of ctx appears once.
All inputs are finite; a program needn't handle non-finite values. No bound on the sum of `answer_mask` on one device may be relied on, other than what follows from the above.
Results may differ from the reference program's by a relative error of at most 0.015.
The reference program's roundings to bfloat16 on the way count: a program that leaves them out, or rounds other values in their place, can miss the bound.
Values may be sent and summed in bfloat16 or wider, within the bound.
No kernel may reach another device: no remote copies, remote signals or barrier semaphores. Data moves between devices by JAX's collectives and lax.ppermute only.
A program may use at most 832 MiB of HBM per device.

```python
import math
import jax
import jax.numpy as jnp
import numpy as np
from jax import lax

D = 2048
HEADS = 32
KV = 4
HD = 64
FF = 5632
V = 32000
TOK_DEV = 256
SEQS = 2
TOKENS = 2048
LENGTH = 1024
NPARAM = 175118336
N_CTX = 8


def layer_std():
    qg = HEADS // KV * HD
    ffg = FF // KV
    attn_in = qg + 2 * HD
    width = attn_in + qg + 3 * ffg
    column = jnp.arange(KV * width) % width
    return jnp.where(column < attn_in, D ** (-0.5), jnp.where(column < attn_in + qg, (LENGTH / (4.0 * HEADS * HD)) ** 0.5, jnp.where(column < attn_in + qg + 2 * ffg, D ** (-0.5), FF ** (-0.5)))).astype(jnp.float32)


def vocab_std():
    vg = V // KV
    column = jnp.arange(2 * V)
    within = column % (2 * vg)
    slot = (column // (2 * vg)).astype(jnp.float32) / max(KV - 1, 1)
    rise = 3.0 ** slot / 1.5
    return jnp.where(within < vg, 1.5 * D ** (-0.5) * rise, 1.0).astype(jnp.float32)


def unit_noise(key, shape):
    return jax.random.normal(key, shape, jnp.float32)


def draw_w_layer(key, part):
    spread = layer_std()
    return unit_noise(jax.random.fold_in(key, 101), (D, spread.shape[0])) * spread[None, :]


def draw_avg_layer(key, part):
    spread = layer_std()
    return unit_noise(jax.random.fold_in(key, 202), (D, spread.shape[0])) * spread[None, :]


def draw_w_vocab(key, part):
    spread = vocab_std()
    return unit_noise(jax.random.fold_in(key, 303), (D, 2 * V)) * spread[None, :]


def draw_avg_vocab(key, part):
    spread = vocab_std()
    return unit_noise(jax.random.fold_in(key, 404), (D, 2 * V)) * spread[None, :]


def set_ends(array, stream_key, low, high):
    shape = array.shape
    index_at = [jax.random.randint(jax.random.fold_in(stream_key, axis), (), 0, shape[axis]) for axis in range(len(shape))]
    array = array.at[tuple(index_at)].set(low)
    longest = shape.index(max(shape))
    index_at[longest] = (index_at[longest] + 1) % shape[longest]
    return array.at[tuple(index_at)].set(high)


def block_scale(key, dims, pieces, smallest, top_value):
    def one(dim, blocks):
        heights = jax.random.uniform(jax.random.fold_in(jax.random.fold_in(key, 6), dim), (blocks,), jnp.float32, smallest / len(pieces), top_value / len(pieces))
        return jnp.repeat(jnp.exp(heights), dims[dim] // blocks).reshape((-1,) + (1,) * (len(dims) - dim - 1))

    loudness = one(*pieces[0])
    for cut in pieces[1:]:
        loudness = loudness * one(*cut)
    return loudness


def rank_table(count, lean):
    weights = [(1 << 20) // math.isqrt(grade ** lean) + 1 for grade in range(1, count + 1)]
    scale = 1 + sum(weights) // (1 << 30)
    return np.cumsum(np.array([max(1, weight // scale) for weight in weights]))


def ranked(key, shape, amount, skew):
    listing = rank_table(amount, skew)
    ticket = jax.random.randint(jax.random.fold_in(key, 1), shape, 0, int(listing[amount - 1]))
    grade = jnp.searchsorted(jnp.asarray(listing, jnp.int32), ticket, side="right")
    return jax.random.permutation(jax.random.fold_in(key, 2), amount)[grade].astype(jnp.int32)


def normal_values(stream_key, shape, scale, reach, shards=(), kind=jnp.bfloat16):
    drawn = scale * jax.random.normal(stream_key, shape, jnp.float32)
    if shards:
        drawn = drawn * block_scale(stream_key, shape, shards, -0.22, 0.18)
    return jnp.clip(drawn, -reach, reach).astype(kind)


def setup_inputs(seed: int = 0) -> dict:
    arg_keys = jax.random.split(jax.random.key(seed), 14)
    token_ids = set_ends(ranked(arg_keys[0], (TOKENS,), V, 2), jax.random.fold_in(arg_keys[0], 3), 0, V - 1).astype(jnp.int32)
    labels = set_ends(ranked(arg_keys[1], (TOKENS,), V, 2), jax.random.fold_in(arg_keys[1], 3), 0, V - 1).astype(jnp.int32)
    answer_mask = set_ends((jax.random.randint(arg_keys[2], (TOKENS,), 0, 2) < 1).astype(jnp.int32), jax.random.fold_in(arg_keys[2], 1), 0, 1)
    pair_map = jax.random.permutation(arg_keys[3], N_CTX).astype(jnp.int32)
    w_layer = draw_w_layer(jax.random.fold_in(arg_keys[13], 71), 0)
    w_vocab = draw_w_vocab(jax.random.fold_in(arg_keys[13], 71), 0)
    gains = jnp.clip(1.0 + 0.1 * jax.random.normal(arg_keys[6], (D, 3), jnp.float32), 0.5, 1.5)
    mom_layer = normal_values(arg_keys[7], (D, KV * (2 * (HEADS // KV) * HD + 2 * HD + 3 * (FF // KV))), (0.01 / NPARAM ** 0.5), 1.1444091796875e-05, ((0, 8), (1, 4)), jnp.float32)
    mom_vocab = normal_values(arg_keys[8], (D, 2 * V), (0.01 / NPARAM ** 0.5), 1.1444091796875e-05, ((0, 8), (1, 4)), jnp.float32)
    mom_gains = normal_values(arg_keys[9], (D, 3), (0.01 / NPARAM ** 0.5), 1.1444091796875e-05, ((0, 8),), jnp.float32)
    avg_layer = draw_avg_layer(jax.random.fold_in(arg_keys[13], 71), 0)
    avg_vocab = draw_avg_vocab(jax.random.fold_in(arg_keys[13], 71), 0)
    avg_gains = jnp.clip(1.0 + 0.1 * jax.random.normal(arg_keys[12], (D, 3), jnp.float32), 0.5, 1.5)
    return dict(token_ids=token_ids, labels=labels, answer_mask=answer_mask, pair_map=pair_map, w_layer=w_layer, w_vocab=w_vocab, gains=gains, mom_layer=mom_layer, mom_vocab=mom_vocab, mom_gains=mom_gains, avg_layer=avg_layer, avg_vocab=avg_vocab, avg_gains=avg_gains)


eps = 1e-05
z_weight = 0.0001
momentum_rate = 0.5
average_rate = 0.5
clip_level = 0.01
highest = lax.Precision.HIGHEST

@jax.custom_vjp
def low(v):
    return lax.optimization_barrier(v.astype(jnp.bfloat16)).astype(jnp.float32)

@jax.custom_vjp
def low_back(v):
    return v

def low_keep(v):
    return (low(v), None)

def low_pass(kept, grad):
    return (grad,)

def back_keep(v):
    return (v, None)

def back_low(kept, grad):
    return (low(grad),)
low.defvjp(low_keep, low_pass)
low_back.defvjp(back_keep, back_low)

def widths():
    group = HEADS // KV
    return (group, group * HD, FF // KV, V // KV)

def layer_spread(length):
    group, qg, ffg, vg = widths()
    attn_in = qg + 2 * HD
    column = jnp.arange(attn_in + qg + 3 * ffg)
    return jnp.where(column < attn_in, D ** (-0.5), jnp.where(column < attn_in + qg, (length / (4.0 * HEADS * HD)) ** 0.5, jnp.where(column < attn_in + qg + 2 * ffg, D ** (-0.5), FF ** (-0.5)))).astype(jnp.float32)

def vocab_spread():
    vg = V // KV
    column = jnp.arange(2 * vg)
    return jnp.where(column < vg, 2.0 * D ** (-0.5), 1.0).astype(jnp.float32)

def total_params():
    return D * (2 * HEADS * HD + 2 * KV * HD + 3 * FF + 2 * V + 3)

def yarn_tables(positions, head_dim):
    half = head_dim // 2
    index = jnp.arange(half, dtype=jnp.float32)
    inverse = 10000.0 ** (-2.0 * index / head_dim)
    ratio = 2048.0 * inverse / (2.0 * math.pi)
    ramp = jnp.clip((ratio - 1.0) / 31.0, 0.0, 1.0)
    freq = (1.0 - ramp) * inverse / 4.0 + ramp * inverse
    angle = positions[:, None] * freq[None, :]
    mscale = 0.1 * math.log(4.0) + 1.0
    return (jnp.cos(angle) * mscale, jnp.sin(angle) * mscale)

def rope(x, cosine, sine):
    half = x.shape[-1] // 2
    first = x[..., :half]
    second = x[..., half:]
    return jnp.concatenate([first * cosine - second * sine, second * cosine + first * sine], axis=-1)

def norm(x, gain):
    return x * lax.rsqrt(lax.optimization_barrier(jnp.mean(x * x, axis=-1, keepdims=True)) + eps) * gain

def update(weight, moment, average, grad, rate):
    moment_new = momentum_rate * moment + grad
    weight_new = weight - rate * (grad + momentum_rate * moment_new)
    average_new = average_rate * average + (1.0 - average_rate) * weight_new
    return (weight_new, moment_new, average_new)

def attend(q, k, v, qblock):
    length = q.shape[0]
    positions = jnp.arange(length, dtype=jnp.int32)
    scale = HD ** (-0.5)

    def block(args):
        q_block, start = args
        scores = jnp.einsum('qgid,kgd->giqk', q_block, k, precision=highest) * scale
        scores = low_back(scores)
        rows = start + jnp.arange(q_block.shape[0], dtype=jnp.int32)
        allowed = positions[None, :] <= rows[:, None]
        weights = jax.nn.softmax(jnp.where(allowed, scores, -jnp.inf), axis=-1)
        return jnp.einsum('giqk,kgd->qgid', low(weights), v, precision=highest)
    blocks = q.reshape((length // qblock, qblock) + q.shape[1:])
    starts = jnp.arange(length // qblock, dtype=jnp.int32) * qblock
    result = lax.map(jax.checkpoint(block), (blocks, starts))
    return result.reshape(q.shape)

def reference(token_ids, labels, answer_mask, pair_map, w_layer, w_vocab, gains, mom_layer, mom_vocab, mom_gains, avg_layer, avg_vocab, avg_gains):
    group, qg, ffg, vg = widths()
    attn_in = qg + 2 * HD
    span = TOK_DEV // (2 * SEQS)
    rows = jnp.arange(TOKENS, dtype=jnp.int32)
    device = rows // TOK_DEV
    local = rows % TOK_DEV
    first = pair_map[device]
    index = jnp.where(local // span % 2 == 0, first, 2 * N_CTX - 1 - first)
    dest = local // (2 * span) * LENGTH + index * span + local % span
    order = jnp.zeros((TOKENS,), jnp.int32).at[dest].set(rows)
    ids = token_ids[order]
    answers = labels[order]
    valid = answer_mask[order].astype(jnp.float32)
    count = jnp.sum(valid)
    cosine, sine = yarn_tables(jnp.tile(jnp.arange(LENGTH, dtype=jnp.float32), SEQS), HD)

    def loss_fn(layer, vocab, gain):
        layer = low(layer).reshape(D, KV, attn_in + qg + 3 * ffg)
        vocab = low(vocab).reshape(D, KV, 2 * vg)
        gain = low(gain)
        w_in = layer[:, :, :attn_in].reshape(D, KV * attn_in)
        w_out = layer[:, :, attn_in:attn_in + qg].reshape(D, HEADS * HD)
        w_gu = layer[:, :, attn_in + qg:attn_in + qg + 2 * ffg].reshape(D, KV * 2 * ffg)
        w_down = layer[:, :, attn_in + qg + 2 * ffg:].reshape(D, FF)
        w_head = vocab[:, :, :vg].reshape(D, V)
        w_embed = vocab[:, :, vg:].reshape(D, V)
        x0 = jnp.take(w_embed, ids, axis=1).T
        a1 = low(norm(x0, gain[:, 0]))
        raw = low_back(jnp.dot(a1, w_in, precision=highest)).reshape(TOKENS, KV, attn_in)
        q = raw[:, :, :qg].reshape(TOKENS, KV, group, HD)
        k = raw[:, :, qg:qg + HD]
        v = low(raw[:, :, qg + HD:])
        q = low(rope(q, cosine[:, None, None, :], sine[:, None, None, :]))
        k = low(rope(k, cosine[:, None, :], sine[:, None, :]))
        qblock = min(512, LENGTH)
        outs = [attend(q[s * LENGTH:(s + 1) * LENGTH], k[s * LENGTH:(s + 1) * LENGTH], v[s * LENGTH:(s + 1) * LENGTH], qblock) for s in range(SEQS)]
        attn = low(low_back(jnp.concatenate(outs, axis=0).reshape(TOKENS, HEADS * HD)))
        x1 = x0 + low_back(jnp.dot(attn, w_out.T, precision=highest))
        a2 = low(norm(x1, gain[:, 1]))
        gate_up = low_back(jnp.dot(a2, w_gu, precision=highest)).reshape(TOKENS, KV, 2 * ffg)
        hidden = low((jax.nn.silu(gate_up[:, :, :ffg]) * gate_up[:, :, ffg:]).reshape(TOKENS, FF))
        x2 = x1 + low_back(jnp.dot(hidden, w_down.T, precision=highest))
        final = low(norm(x2, gain[:, 2]))

        def head_block(args):
            rows_block, target, weight = args
            logits = low_back(jnp.dot(rows_block, w_head, precision=highest))
            top = lax.optimization_barrier(jnp.max(logits, axis=-1, keepdims=True))
            lse = top[:, 0] + jnp.log(lax.optimization_barrier(jnp.sum(jnp.exp(logits - top), axis=-1)))
            picked = jnp.take_along_axis(logits, target[:, None], axis=1)[:, 0]
            return jnp.sum(weight * (lse - picked + z_weight * lse * lse))
        blocks = TOKENS // TOK_DEV
        terms = lax.map(jax.checkpoint(head_block), (final.reshape(blocks, TOK_DEV, D), answers.reshape(blocks, TOK_DEV), valid.reshape(blocks, TOK_DEV)))
        return jnp.sum(terms) / count
    loss, back = jax.vjp(loss_fn, w_layer, w_vocab, gains)
    grad_layer, grad_vocab, grad_gain = back(jnp.ones_like(loss))
    squares = jnp.sum(grad_layer * grad_layer) + jnp.sum(grad_vocab * grad_vocab) + jnp.sum(grad_gain * grad_gain)
    grad_norm = jnp.sqrt(squares)
    factor = jnp.minimum(1.0, clip_level / grad_norm)
    base = 1.5 * math.sqrt(total_params()) / clip_level
    layer_rate = base * jnp.tile(layer_spread(LENGTH), KV)
    vocab_rate = base * jnp.tile(vocab_spread(), KV)
    layer_new, layer_moment, layer_average = update(w_layer, mom_layer, avg_layer, factor * grad_layer, layer_rate)
    vocab_new, vocab_moment, vocab_average = update(w_vocab, mom_vocab, avg_vocab, factor * grad_vocab, vocab_rate)
    gains_new, gains_moment, gains_average = update(gains, mom_gains, avg_gains, factor * grad_gain, base * 0.1)
    return (layer_new, layer_moment, layer_average, layer_new.astype(jnp.bfloat16), vocab_new, vocab_moment, vocab_average, vocab_new.astype(jnp.bfloat16), gains_new, gains_moment, gains_average, gains_new.astype(jnp.bfloat16), loss, grad_norm)
```

```python
import functools
import math

import jax
import jax.numpy as jnp
import numpy as np
from jax import lax
from jax.experimental import pallas as pl
from jax.experimental.pallas import tpu as pltpu
from jax.sharding import PartitionSpec as P

D = 2048
HEADS = 32
KV = 4
HD = 64
FF = 5632
V = 32000
SEQS = 2

eps = 1e-05
z_weight = 0.0001
momentum_rate = 0.5
average_rate = 0.5
clip_level = 0.01

GROUP = HEADS // KV
QG = GROUP * HD
FFG = FF // KV
VG = V // KV
ATTN_IN = QG + 2 * HD
NPARAM = D * (2 * HEADS * HD + 2 * KV * HD + 3 * FF + 2 * V + 3)
BASE = 1.5 * math.sqrt(NPARAM) / clip_level
EMB_AT = VG // 128 * 128
EMB_W = 2 * VG - EMB_AT
EMB_STEPS = 7
EMB_BLOCK = EMB_W // EMB_STEPS

f32 = jnp.float32
bf16 = jnp.bfloat16
NEG = -1e30


def dot_nn(a, b):
    return lax.dot_general(a, b, (((1,), (0,)), ((), ())), preferred_element_type=f32)


def dot_nt(a, b):
    return lax.dot_general(a, b, (((1,), (1,)), ((), ())), preferred_element_type=f32)


def dot_tn(a, b):
    return lax.dot_general(a, b, (((0,), (0,)), ((), ())), preferred_element_type=f32)


def cost(flops, nbytes, trans=0):
    return pl.CostEstimate(flops=int(flops), bytes_accessed=int(nbytes), transcendentals=int(trans))


def params(**kw):
    return pltpu.CompilerParams(vmem_limit_bytes=56 * 1024 * 1024, **kw)


def one_hot(ids, base, width):
    column = lax.broadcasted_iota(jnp.int32, (ids.shape[0], width), 1) + base
    return jnp.where(ids == column, jnp.float32(1.0), jnp.float32(0.0)).astype(bf16)


def lookup_kernel(rows, ids_ref, w_ref, out_ref, acc_ref):
    step = pl.program_id(0)
    w = w_ref[...].astype(bf16)
    total = ids_ref.shape[0]

    @pl.when(step == 0)
    def _():
        acc_ref[...] = jnp.zeros_like(acc_ref)

    for r in range(0, total, rows):
        part = pl.ds(r, rows)
        acc_ref[part, :] += dot_nt(one_hot(ids_ref[part, :], step * EMB_BLOCK, EMB_BLOCK), w)

    @pl.when(step == EMB_STEPS - 1)
    def _():
        out_ref[...] = acc_ref[...].astype(bf16)


def lookup(ids, w_vocab):
    total, rows = ids.shape[0], w_vocab.shape[0]
    return pl.pallas_call(
        functools.partial(lookup_kernel, min(512, total)),
        grid=(EMB_STEPS,),
        in_specs=[
            pl.BlockSpec((total, 1), lambda i: (0, 0)),
            pl.BlockSpec((pl.Element(rows), pl.Element(EMB_BLOCK)), lambda i: (0, (EMB_AT // 128 + EMB_BLOCK // 128 * i) * 128)),
        ],
        out_specs=pl.BlockSpec((total, rows), lambda i: (0, 0)),
        out_shape=jax.ShapeDtypeStruct((total, rows), bf16),
        scratch_shapes=[pltpu.VMEM((total, rows), f32)],
        compiler_params=params(),
        cost_estimate=cost(2 * total * rows * EMB_W, rows * EMB_W * 4),
        name="embed_lookup",
    )(ids, w_vocab)


def embed_grad_kernel(rows, ids_ref, dxt_ref, out_ref, sq_ref):
    step = pl.program_id(0)
    total = ids_ref.shape[0]
    acc = jnp.zeros(out_ref.shape, f32)
    for r in range(0, total, rows):
        hot = one_hot(ids_ref[pl.ds(r, rows), :], step * EMB_BLOCK, EMB_BLOCK)
        acc = acc + dot_nn(dxt_ref[:, pl.ds(r, rows)], hot)
    out_ref[...] = acc.astype(bf16)
    square = acc * acc
    lanes = sum(square[:, k : k + 128] for k in range(0, EMB_BLOCK, 128))
    part = sum(lanes[k : k + 8] for k in range(0, lanes.shape[0], 8))

    @pl.when(step == 0)
    def _():
        sq_ref[...] = jnp.zeros_like(sq_ref)

    sq_ref[...] += part


def embed_grad(ids, dxt):
    rows, total = dxt.shape
    return pl.pallas_call(
        functools.partial(embed_grad_kernel, min(512, total)),
        grid=(EMB_STEPS,),
        in_specs=[
            pl.BlockSpec((total, 1), lambda i: (0, 0)),
            pl.BlockSpec((rows, total), lambda i: (0, 0)),
        ],
        out_specs=[
            pl.BlockSpec((rows, EMB_BLOCK), lambda i: (0, i)),
            pl.BlockSpec((8, 128), lambda i: (0, 0)),
        ],
        out_shape=[
            jax.ShapeDtypeStruct((rows, EMB_W), bf16),
            jax.ShapeDtypeStruct((8, 128), f32),
        ],
        compiler_params=params(),
        cost_estimate=cost(2 * total * rows * EMB_W, rows * EMB_W * 2),
        name="embed_grad",
    )(ids, dxt)


def partner(x):
    width = x.shape[1]
    lane = lax.broadcasted_iota(jnp.int32, x.shape, 1)
    return jnp.where(lane % HD < HD // 2, pltpu.roll(x, width - HD // 2, 1), pltpu.roll(x, HD // 2, 1))


def qkv_kernel(a_ref, w_ref, cos_ref, sin_ref, q_ref, kv_ref):
    raw = dot_nn(a_ref[...], w_ref[...])
    cosine, sine = cos_ref[...], sin_ref[...]
    for j in range(0, QG, 128):
        x = raw[:, j : j + 128]
        rot = (x * cosine + partner(x) * sine).astype(bf16)
        q_ref[:, j : j + 128] = rot * jnp.asarray(HD**-0.5, bf16)
    x = raw[:, QG:]
    lane = lax.broadcasted_iota(jnp.int32, x.shape, 1)
    kv_ref[...] = jnp.where(lane < HD, x * cosine + partner(x) * sine, x).astype(bf16)


def qkv(a1, w_in, cosine, sine):
    tok = a1.shape[0]
    return pl.pallas_call(
        qkv_kernel,
        out_shape=[
            jax.ShapeDtypeStruct((tok, QG), bf16),
            jax.ShapeDtypeStruct((tok, 2 * HD), bf16),
        ],
        compiler_params=params(),
        cost_estimate=cost(2 * tok * D * ATTN_IN, 2 * D * ATTN_IN + 2 * tok * D),
        name="qkv",
    )(a1, w_in, cosine, sine)


def split_kv(kv_ref, parts_ref):
    kv = kv_ref[...].reshape(-1, 2 * HD).astype(f32)
    lane = lax.broadcasted_iota(jnp.int32, kv.shape, 1)
    swapped = pltpu.roll(kv, HD, 1)
    zero = jnp.zeros_like(kv)
    low = lane < HD
    parts_ref[0] = jnp.where(low, kv, zero).astype(bf16)
    parts_ref[1] = jnp.where(low, zero, swapped).astype(bf16)
    parts_ref[2] = jnp.where(low, swapped, zero).astype(bf16)
    parts_ref[3] = jnp.where(low, zero, kv).astype(bf16)


def attn_kernel(q_ref, kv_ref, qpos_ref, kpos_ref, o_ref, parts_ref):
    @pl.when(pl.program_id(1) == 0)
    def _():
        split_kv(kv_ref, parts_ref)

    q = q_ref[...]
    allowed = kpos_ref[...] <= qpos_ref[...]
    out = None
    for g in range(2):
        s = jnp.where(allowed, dot_nt(q, parts_ref[g]), NEG)
        p = jnp.exp(s - jnp.max(s, axis=1, keepdims=True))
        p = p * (1.0 / jnp.sum(p, axis=1, keepdims=True))
        part = dot_nn(p.astype(bf16), parts_ref[2 + g])
        out = part if out is None else out + part
    o_ref[...] = out.astype(bf16)


def attn(q, kv_every, qpos, kpos):
    n_ctx, _, seq_tok, _ = kv_every.shape
    keys = n_ctx * seq_tok
    pairs = QG // 128
    return pl.pallas_call(
        attn_kernel,
        grid=(SEQS, pairs),
        in_specs=[
            pl.BlockSpec((seq_tok, 128), lambda s, p: (s, p)),
            pl.BlockSpec((n_ctx, 1, seq_tok, 2 * HD), lambda s, p: (0, s, 0, 0)),
            pl.BlockSpec((seq_tok, 1), lambda s, p: (0, 0)),
            pl.BlockSpec((1, keys), lambda s, p: (0, 0)),
        ],
        out_specs=pl.BlockSpec((seq_tok, 128), lambda s, p: (s, p)),
        out_shape=jax.ShapeDtypeStruct((SEQS * seq_tok, QG), bf16),
        scratch_shapes=[pltpu.VMEM((4, keys, 2 * HD), bf16)],
        compiler_params=params(),
        cost_estimate=cost(
            8 * SEQS * seq_tok * keys * QG, 4 * SEQS * seq_tok * QG, SEQS * GROUP * seq_tok * keys
        ),
        name="attn_fwd",
    )(q, kv_every, qpos.reshape(seq_tok, 1), kpos.reshape(1, keys))


def attn_back_kernel(
    pairs, q_ref, do_ref, kv_ref, qpos_ref, kpos_ref, cos_ref, sin_ref, dq_ref, dkv_ref, parts_ref, acc_ref
):
    pair = pl.program_id(1)

    @pl.when(pair == 0)
    def _():
        split_kv(kv_ref, parts_ref)
        acc_ref[...] = jnp.zeros_like(acc_ref)

    q = q_ref[...]
    do = do_ref[...]
    allowed = kpos_ref[...] <= qpos_ref[...]
    dq = None
    for g in range(2):
        s = jnp.where(allowed, dot_nt(parts_ref[g], q), NEG)
        p = jnp.exp(s - jnp.max(s, axis=0, keepdims=True))
        p = p * (1.0 / jnp.sum(p, axis=0, keepdims=True))
        dp = dot_nt(parts_ref[2 + g], do)
        delta = jnp.sum(p * dp, axis=0, keepdims=True)
        ds = (p * (dp - delta)).astype(bf16)
        part = dot_tn(ds, parts_ref[g])
        dq = part if dq is None else dq + part
        acc_ref[g] += dot_nn(ds, q)
        acc_ref[2 + g] += dot_nn(p.astype(bf16), do)
    dq = dq * (HD**-0.5)
    dq_ref[...] = (dq * cos_ref[...] - partner(dq) * sin_ref[...]).astype(bf16)

    @pl.when(pair == pairs - 1)
    def _():
        lane = lax.broadcasted_iota(jnp.int32, acc_ref.shape[1:], 1)
        grad_k = acc_ref[0] + pltpu.roll(acc_ref[1], HD, 1)
        grad_v = pltpu.roll(acc_ref[2], HD, 1) + acc_ref[3]
        dkv_ref[...] = jnp.where(lane < HD, grad_k, grad_v).astype(bf16).reshape(dkv_ref.shape)


def attn_back(q, do, kv_every, qpos, kpos, cosine, sine):
    n_ctx, _, seq_tok, _ = kv_every.shape
    keys = n_ctx * seq_tok
    pairs = QG // 128
    return pl.pallas_call(
        functools.partial(attn_back_kernel, pairs),
        grid=(SEQS, pairs),
        in_specs=[
            pl.BlockSpec((seq_tok, 128), lambda s, p: (s, p)),
            pl.BlockSpec((seq_tok, 128), lambda s, p: (s, p)),
            pl.BlockSpec((n_ctx, 1, seq_tok, 2 * HD), lambda s, p: (0, s, 0, 0)),
            pl.BlockSpec((1, seq_tok), lambda s, p: (0, 0)),
            pl.BlockSpec((keys, 1), lambda s, p: (0, 0)),
            pl.BlockSpec((seq_tok, 128), lambda s, p: (s, 0)),
            pl.BlockSpec((seq_tok, 128), lambda s, p: (s, 0)),
        ],
        out_specs=[
            pl.BlockSpec((seq_tok, 128), lambda s, p: (s, p)),
            pl.BlockSpec((n_ctx, 1, seq_tok, 2 * HD), lambda s, p: (0, s, 0, 0)),
        ],
        out_shape=[
            jax.ShapeDtypeStruct((SEQS * seq_tok, QG), bf16),
            jax.ShapeDtypeStruct(kv_every.shape, bf16),
        ],
        scratch_shapes=[
            pltpu.VMEM((4, keys, 2 * HD), bf16),
            pltpu.VMEM((4, keys, 2 * HD), f32),
        ],
        compiler_params=params(),
        cost_estimate=cost(
            20 * SEQS * seq_tok * keys * QG, 8 * SEQS * seq_tok * QG, SEQS * GROUP * seq_tok * keys
        ),
        name="attn_bwd",
    )(q, do, kv_every, qpos.reshape(1, seq_tok), kpos.reshape(keys, 1), cosine, sine)


def kv_back_kernel(parts_ref, cos_ref, sin_ref, out_ref):
    x = parts_ref[0].astype(f32)
    for k in range(1, parts_ref.shape[0]):
        x = x + parts_ref[k].astype(f32)
    lane = lax.broadcasted_iota(jnp.int32, x.shape, 1)
    out_ref[...] = jnp.where(lane < HD, x * cos_ref[...] - partner(x) * sin_ref[...], x).astype(bf16)


def kv_back(parts, cosine, sine):
    return pl.pallas_call(
        kv_back_kernel,
        out_shape=jax.ShapeDtypeStruct(parts.shape[1:], bf16),
        compiler_params=params(),
        name="kv_bwd",
    )(parts, cosine, sine)


def update_piece(factor, rate, grad, w_ref, m_ref, a_ref, outs, columns):
    new_ref, moment_ref, average_ref, copy_ref = outs
    grad = factor * grad
    moment = momentum_rate * m_ref[:, columns] + grad
    new = w_ref[:, columns] - rate * (grad + momentum_rate * moment)
    new_ref[:, columns] = new
    moment_ref[:, columns] = moment
    average_ref[:, columns] = average_rate * a_ref[:, columns] + (1.0 - average_rate) * new
    copy_ref[:, columns] = new.astype(bf16)


def layer_update_kernel(spreads, factor_ref, *refs):
    grads, (w_ref, m_ref, a_ref), outs = refs[:-7], refs[-7:-4], refs[-4:]
    factor = factor_ref[0, 0]
    for source, inner, outer, width, spread in spreads:
        grad = grads[source][:, inner : inner + width].astype(f32)
        update_piece(factor, BASE * spread, grad, w_ref, m_ref, a_ref, outs, slice(outer, outer + width))


def vocab_update_kernel(part, factor_ref, head_ref, embed_ref, w_ref, m_ref, a_ref, *outs):
    factor = factor_ref[0, 0]
    head_rate = BASE * 2.0 * D**-0.5
    for k in range(head_ref.shape[0]):
        low, high = k * part, min((k + 1) * part, EMB_AT)
        if low >= high:
            continue
        grad = head_ref[k, :, : high - low].astype(f32)
        update_piece(factor, head_rate, grad, w_ref, m_ref, a_ref, outs, slice(low, high))
    edge = EMB_AT - EMB_AT // part * part
    grad_head = head_ref[EMB_AT // part, :, edge : edge + 128].astype(f32)
    grad_embed = embed_ref[:, :128].astype(f32)
    own = lax.broadcasted_iota(jnp.int32, grad_head.shape, 1) < VG - EMB_AT
    update_piece(
        factor,
        jnp.where(own, head_rate, BASE),
        jnp.where(own, grad_head, grad_embed),
        w_ref,
        m_ref,
        a_ref,
        outs,
        slice(EMB_AT, EMB_AT + 128),
    )
    for low in range(128, EMB_W, 1024):
        high = min(low + 1024, EMB_W)
        grad = embed_ref[:, low:high].astype(f32)
        update_piece(factor, BASE, grad, w_ref, m_ref, a_ref, outs, slice(EMB_AT + low, EMB_AT + high))


def call_update(kernel, factor, grads, grad_specs, w, m, a, rows, name):
    total, width = w.shape
    block = pl.BlockSpec((rows, width), lambda i: (i, 0))
    return pl.pallas_call(
        kernel,
        grid=(total // rows,),
        in_specs=[pl.BlockSpec(memory_space=pltpu.SMEM)] + grad_specs + [block] * 3,
        out_specs=[block] * 4,
        out_shape=[jax.ShapeDtypeStruct(w.shape, f32)] * 3 + [jax.ShapeDtypeStruct(w.shape, bf16)],
        compiler_params=params(),
        cost_estimate=cost(10 * total * width, 28 * total * width),
        name=name,
    )(factor.reshape(1, 1), *grads, w, m, a)


def norm_parts(x):
    scale = lax.rsqrt(jnp.mean(x * x, axis=-1, keepdims=True) + eps)
    return x * scale, scale


def norm_back(dy, unit, scale, gain):
    scaled = dy * gain
    dx = scale * (scaled - unit * jnp.mean(scaled * unit, axis=-1, keepdims=True))
    return dx, jnp.sum(dy * unit, axis=0)


def local(
    token_ids,
    labels,
    answer_mask,
    pair_map,
    w_layer,
    w_vocab,
    gains,
    mom_layer,
    mom_vocab,
    mom_gains,
    avg_layer,
    avg_vocab,
    avg_gains,
):
    n_ctx = lax.axis_size("ctx")
    n_head = lax.axis_size("head")
    place = lax.axis_index("ctx")
    shard = lax.axis_index("head")
    tok = token_ids.shape[0]
    rows = w_layer.shape[0]
    seq_tok = tok // SEQS
    span = seq_tok // 2
    chunk = seq_tok // n_head
    own = SEQS * chunk
    length = n_ctx * seq_tok
    part = -(-VG // (n_ctx * 128)) * 128

    def turn(x, axis):
        return lax.dynamic_slice_in_dim(
            jnp.concatenate([x, x], axis), shard * chunk, seq_tok, axis
        )

    def turn_back(x, axis):
        return lax.dynamic_slice_in_dim(
            jnp.concatenate([x, x], axis), seq_tok - shard * chunk, seq_tok, axis
        )

    def head_scatter(x):
        sums = x[:, 0].astype(f32)
        for s in range(1, n_head):
            sent = lax.ppermute(x[:, s], "head", [(i, (i + s) % n_head) for i in range(n_head)])
            sums = sums + sent.astype(f32)
        return sums

    def head_gather(x):
        pieces = [x]
        for s in range(1, n_head):
            pieces.append(lax.ppermute(x, "head", [(i, (i - s) % n_head) for i in range(n_head)]))
        return jnp.stack(pieces, axis=1)

    def sum_own(partial):
        split = partial.astype(bf16).reshape(SEQS, n_head, chunk, D)
        return head_scatter(split).reshape(own, D)

    def spread_all(x):
        return head_gather(x.astype(bf16).reshape(SEQS, chunk, D)).reshape(tok, D)

    every = lax.all_gather(jnp.stack([token_ids, labels, answer_mask]), "ctx", axis=1)
    every = every.reshape(3, n_ctx, SEQS, seq_tok)
    turned = turn(every, 3)
    ids_all, labels_all, mask_all = (turned[k].reshape(n_ctx * tok) for k in range(3))
    count = jnp.sum(every[2].astype(f32))

    layer_b = w_layer.astype(bf16)
    ends = np.cumsum([0, ATTN_IN, QG, 2 * FFG, FFG])
    w_in, w_out, w_gu, w_down = (
        lax.all_gather(layer_b[:, ends[k] : ends[k + 1]], "ctx", axis=0, tiled=True) for k in range(4)
    )
    gain_rows = lax.all_gather(gains.astype(bf16).T, "ctx", axis=1, tiled=True).astype(f32)
    head_b = jnp.pad(w_vocab[:, :VG].astype(bf16), ((0, 0), (0, n_ctx * part - VG)))
    w_head = lax.all_to_all(
        head_b.reshape(rows, n_ctx, part).transpose(1, 0, 2), "ctx", 0, 0, tiled=True
    ).reshape(D, part)

    offset_id = shard * VG
    local_ids = ids_all - offset_id
    inside = (local_ids >= 0) & (local_ids < VG)
    slots = jnp.where(inside, local_ids + (VG - EMB_AT), -1).reshape(-1, 1)
    picked = lookup(slots, w_vocab).reshape(n_ctx * SEQS, n_head, chunk, rows)
    picked = head_scatter(picked).astype(bf16).reshape(n_ctx * own, rows)
    x0 = lax.all_to_all(picked, "ctx", 0, 1, tiled=True).astype(f32)

    unit0, scale0 = norm_parts(x0)
    a1 = spread_all(unit0 * gain_rows[0])
    row = (jnp.arange(seq_tok, dtype=jnp.int32) + shard * chunk) % seq_tok

    def positions(index):
        index = index[:, None]
        at = jnp.where(row // span == 0, index, 2 * n_ctx - 1 - index)
        return at * span + row % span

    qpos = positions(pair_map[place][None])[0]
    kpos = positions(pair_map).reshape(length)
    half = HD // 2
    inverse = 10000.0 ** (-2.0 * np.arange(half) / HD)
    ramp = np.clip((2048.0 * inverse / (2.0 * math.pi) - 1.0) / 31.0, 0.0, 1.0)
    freq = np.tile(((1.0 - ramp) * inverse / 4.0 + ramp * inverse).astype(np.float32), 128 // half)
    sign = np.where(np.arange(128) % HD < half, -1.0, 1.0).astype(np.float32)
    mscale = 0.1 * math.log(4.0) + 1.0
    angle = jnp.tile(qpos, SEQS).astype(f32)[:, None] * freq[None, :]
    cosine = jnp.cos(angle) * mscale
    sine = jnp.sin(angle) * (mscale * sign)[None, :]
    q, kv_own = qkv(a1, w_in, cosine, sine)
    kv_every = lax.all_gather(kv_own, "ctx").reshape(n_ctx, SEQS, seq_tok, 2 * HD)
    attn_b = attn(q, kv_every, qpos, kpos)
    x1 = x0 + sum_own(dot_nt(attn_b, w_out))

    unit1, scale1 = norm_parts(x1)
    a2 = spread_all(unit1 * gain_rows[1])
    gate_up = dot_nn(a2, w_gu)

    def glu(values):
        return jax.nn.silu(values[:, :FFG]) * values[:, FFG:]

    hidden_f, glu_back = jax.vjp(glu, gate_up)
    hidden_b = hidden_f.astype(bf16)
    x2 = x1 + sum_own(dot_nt(hidden_b, w_down))

    unit2, scale2 = norm_parts(x2)
    final_b = spread_all(unit2 * gain_rows[2])
    final_all = lax.all_gather(final_b, "ctx", axis=0, tiled=True)
    column = place * part + jnp.arange(part, dtype=jnp.int32)
    logits = jnp.where((column < VG)[None, :], dot_nn(final_all, w_head), NEG)
    row_top = jnp.max(logits, axis=-1)
    row_total = jnp.sum(jnp.exp(logits - row_top[:, None]), axis=-1)
    slot = jnp.where(column < VG, column + offset_id, -1)
    hit = slot[None, :] == labels_all[:, None]
    label_logit = jnp.sum(jnp.where(hit, logits, 0.0), axis=-1)

    def merge(stats):
        top = jnp.max(stats[:, 0], axis=0)
        total = jnp.sum(stats[:, 1] * jnp.exp(stats[:, 0] - top), axis=0)
        return jnp.stack([top, total, jnp.sum(stats[:, 2], axis=0)])

    stats = jnp.stack([row_top, row_total, label_logit])
    stats = merge(lax.all_gather(stats, "ctx"))
    stats = turn_back(stats.reshape(3, n_ctx * SEQS, seq_tok), 2)
    stats = merge(lax.all_gather(stats, "head"))
    lse = stats[0] + jnp.log(stats[1])
    valid = every[2].astype(f32).reshape(n_ctx * SEQS, seq_tok)
    loss = jnp.sum(valid * (lse - stats[2] + z_weight * lse * lse)) / count
    lse = turn(lse, 1).reshape(n_ctx * tok)
    weight = mask_all.astype(f32) / count
    soft = jnp.exp(logits - lse[:, None])
    dlog_b = (
        weight[:, None] * ((1.0 + 2.0 * z_weight * lse)[:, None] * soft - hit.astype(f32))
    ).astype(bf16)
    d_final = lax.psum_scatter(
        dot_nt(dlog_b, w_head).astype(bf16), "ctx", scatter_dimension=0, tiled=True
    )
    d_head = dot_tn(final_all, dlog_b)
    head_sq = jnp.sum(d_head * d_head)
    g_head = lax.all_to_all(d_head.astype(bf16).reshape(n_ctx, rows, part), "ctx", 0, 0, tiled=True)

    dx2, d_gain2 = norm_back(sum_own(d_final), unit2, scale2, gain_rows[2])
    dyf_b = spread_all(dx2)
    d_hidden = dot_nn(dyf_b, w_down)
    d_gate_up_b = glu_back(d_hidden)[0].astype(bf16)
    dx1_norm, d_gain1 = norm_back(sum_own(dot_nt(d_gate_up_b, w_gu)), unit1, scale1, gain_rows[1])
    dx1 = dx2 + dx1_norm
    dya_b = spread_all(dx1)
    d_attn_b = dot_nn(dya_b, w_out).astype(bf16)
    d_q, d_kv = attn_back(q, d_attn_b, kv_every, qpos, kpos, cosine, sine)
    d_kv = lax.all_to_all(d_kv.reshape(n_ctx, tok, 2 * HD), "ctx", 0, 0, tiled=True)
    d_raw_b = jnp.concatenate([d_q, kv_back(d_kv, cosine, sine)], axis=1)
    dx0_norm, d_gain0 = norm_back(sum_own(dot_nt(d_raw_b, w_in)), unit0, scale0, gain_rows[0])
    dx0 = dx1 + dx0_norm

    g_ff = lax.psum_scatter(
        jnp.concatenate([dot_tn(a2, d_gate_up_b), dot_tn(dyf_b, hidden_b)], axis=1).astype(bf16),
        "ctx",
        scatter_dimension=0,
        tiled=True,
    )
    g_at = lax.psum_scatter(
        jnp.concatenate([dot_tn(a1, d_raw_b), dot_tn(dya_b, attn_b)], axis=1).astype(bf16),
        "ctx",
        scatter_dimension=0,
        tiled=True,
    )
    extra = jnp.pad(jnp.stack([d_gain0, d_gain1, d_gain2]), ((0, 13), (0, 0)))
    moved = lax.all_to_all(jnp.concatenate([dx0, extra]).astype(bf16), "ctx", 1, 0, tiled=True)
    moved = moved.reshape(n_ctx, own + 16, rows)
    gain_part = jnp.sum(moved[:, own : own + 8].astype(f32), axis=0)
    gain_all = lax.all_gather(gain_part, "head")
    grad_gain = jnp.sum(gain_all, axis=0)[:3].T
    dx0_all = head_gather(moved[:, :own].reshape(n_ctx * SEQS, chunk, rows)).reshape(n_ctx * tok, rows)
    g_embed, embed_sq = embed_grad(slots, dx0_all.T)

    squares = (
        jnp.sum(jnp.square(g_ff.astype(f32)))
        + jnp.sum(jnp.square(g_at.astype(f32)))
        + head_sq
        + jnp.sum(embed_sq)
        + jnp.sum(grad_gain * grad_gain) / n_head
    )
    squares = jnp.sum(lax.all_gather(jnp.broadcast_to(squares, (8, 128)), "head"), axis=0)
    total_sq = jnp.sum(lax.all_gather(squares, "ctx"), axis=0)[0, 0]
    grad_norm = jnp.sqrt(total_sq)
    factor = jnp.minimum(1.0, clip_level / grad_norm)

    wide = 16
    spreads = (
        (1, 0, 0, ATTN_IN, D**-0.5),
        (1, ATTN_IN, ATTN_IN, QG, (length / (4.0 * HEADS * HD)) ** 0.5),
        (0, 0, ATTN_IN + QG, 2 * FFG, D**-0.5),
        (0, 2 * FFG, ATTN_IN + QG + 2 * FFG, FFG, FF**-0.5),
    )
    layer = call_update(
        functools.partial(layer_update_kernel, spreads),
        factor,
        (g_ff, g_at),
        [
            pl.BlockSpec((wide, g_ff.shape[1]), lambda i: (i, 0)),
            pl.BlockSpec((wide, g_at.shape[1]), lambda i: (i, 0)),
        ],
        w_layer,
        mom_layer,
        avg_layer,
        wide,
        "layer_update",
    )
    vocab = call_update(
        functools.partial(vocab_update_kernel, part),
        factor,
        (g_head, g_embed),
        [
            pl.BlockSpec((n_ctx, wide, part), lambda i: (0, i, 0)),
            pl.BlockSpec((wide, EMB_W), lambda i: (i, 0)),
        ],
        w_vocab,
        mom_vocab,
        avg_vocab,
        wide,
        "vocab_update",
    )
    grad = factor * grad_gain
    gains_moment = momentum_rate * mom_gains + grad
    gains_new = gains - BASE * 0.1 * (grad + momentum_rate * gains_moment)
    gains_average = average_rate * avg_gains + (1.0 - average_rate) * gains_new
    return (
        *layer,
        *vocab,
        gains_new,
        gains_moment,
        gains_average,
        gains_new.astype(bf16),
        loss,
        grad_norm,
    )


def solution(mesh):
    token, split, gain = P("ctx"), P("ctx", "head"), P("ctx", None)
    in_specs = (token, token, token, P()) + (split, split, gain) * 3
    out_specs = (split,) * 8 + (gain,) * 4 + (P(), P())
    return jax.shard_map(local, mesh=mesh, in_specs=in_specs, out_specs=out_specs, check_vma=False)
```

```python
import functools
import math

import jax
import jax.numpy as jnp
import numpy as np
from jax import lax
from jax.experimental import pallas as pl
from jax.experimental.pallas import tpu as pltpu
from jax.sharding import PartitionSpec as P

D = 2048
HEADS = 32
KV = 4
HD = 64
FF = 5632
V = 32000
SEQS = 2

eps = 1e-05
z_weight = 0.0001
momentum_rate = 0.5
average_rate = 0.5
clip_level = 0.01

GROUP = HEADS // KV
QG = GROUP * HD
FFG = FF // KV
VG = V // KV
ATTN_IN = QG + 2 * HD
NPARAM = D * (2 * HEADS * HD + 2 * KV * HD + 3 * FF + 2 * V + 3)
BASE = 1.5 * math.sqrt(NPARAM) / clip_level
EMB_AT = VG // 128 * 128
EMB_W = 2 * VG - EMB_AT
EMB_STEPS = 7
EMB_BLOCK = EMB_W // EMB_STEPS

f32 = jnp.float32
bf16 = jnp.bfloat16
NEG = -1e30


def dot_nn(a, b):
    return lax.dot_general(a, b, (((1,), (0,)), ((), ())), preferred_element_type=f32)


def dot_nt(a, b):
    return lax.dot_general(a, b, (((1,), (1,)), ((), ())), preferred_element_type=f32)


def dot_tn(a, b):
    return lax.dot_general(a, b, (((0,), (0,)), ((), ())), preferred_element_type=f32)


def cost(flops, nbytes, trans=0):
    return pl.CostEstimate(flops=int(flops), bytes_accessed=int(nbytes), transcendentals=int(trans))


def params(**kw):
    return pltpu.CompilerParams(vmem_limit_bytes=56 * 1024 * 1024, **kw)


def one_hot(ids, base, width):
    column = lax.broadcasted_iota(jnp.int32, (ids.shape[0], width), 1) + base
    return jnp.where(ids == column, jnp.float32(1.0), jnp.float32(0.0)).astype(bf16)


def lookup_kernel(rows, ids_ref, w_ref, out_ref, acc_ref):
    step = pl.program_id(0)
    w = w_ref[...].astype(bf16)
    total = ids_ref.shape[0]

    @pl.when(step == 0)
    def _():
        acc_ref[...] = jnp.zeros_like(acc_ref)

    for r in range(0, total, rows):
        part = pl.ds(r, rows)
        acc_ref[part, :] += dot_nt(one_hot(ids_ref[part, :], step * EMB_BLOCK, EMB_BLOCK), w)

    @pl.when(step == EMB_STEPS - 1)
    def _():
        out_ref[...] = acc_ref[...].astype(bf16)


def lookup(ids, w_vocab):
    total, rows = ids.shape[0], w_vocab.shape[0]
    return pl.pallas_call(
        functools.partial(lookup_kernel, min(512, total)),
        grid=(EMB_STEPS,),
        in_specs=[
            pl.BlockSpec((total, 1), lambda i: (0, 0)),
            pl.BlockSpec((pl.Element(rows), pl.Element(EMB_BLOCK)), lambda i: (0, (EMB_AT // 128 + EMB_BLOCK // 128 * i) * 128)),
        ],
        out_specs=pl.BlockSpec((total, rows), lambda i: (0, 0)),
        out_shape=jax.ShapeDtypeStruct((total, rows), bf16),
        scratch_shapes=[pltpu.VMEM((total, rows), f32)],
        compiler_params=params(),
        cost_estimate=cost(2 * total * rows * EMB_W, rows * EMB_W * 4),
        name="embed_lookup",
    )(ids, w_vocab)


def embed_grad_kernel(rows, ids_ref, dxt_ref, out_ref, sq_ref):
    step = pl.program_id(0)
    total = ids_ref.shape[0]
    acc = jnp.zeros(out_ref.shape, f32)
    for r in range(0, total, rows):
        hot = one_hot(ids_ref[pl.ds(r, rows), :], step * EMB_BLOCK, EMB_BLOCK)
        acc = acc + dot_nn(dxt_ref[:, pl.ds(r, rows)], hot)
    out_ref[...] = acc.astype(bf16)
    square = acc * acc
    lanes = sum(square[:, k : k + 128] for k in range(0, EMB_BLOCK, 128))
    part = sum(lanes[k : k + 8] for k in range(0, lanes.shape[0], 8))

    @pl.when(step == 0)
    def _():
        sq_ref[...] = jnp.zeros_like(sq_ref)

    sq_ref[...] += part


def embed_grad(ids, dxt):
    rows, total = dxt.shape
    return pl.pallas_call(
        functools.partial(embed_grad_kernel, min(512, total)),
        grid=(EMB_STEPS,),
        in_specs=[
            pl.BlockSpec((total, 1), lambda i: (0, 0)),
            pl.BlockSpec((rows, total), lambda i: (0, 0)),
        ],
        out_specs=[
            pl.BlockSpec((rows, EMB_BLOCK), lambda i: (0, i)),
            pl.BlockSpec((8, 128), lambda i: (0, 0)),
        ],
        out_shape=[
            jax.ShapeDtypeStruct((rows, EMB_W), bf16),
            jax.ShapeDtypeStruct((8, 128), f32),
        ],
        compiler_params=params(),
        cost_estimate=cost(2 * total * rows * EMB_W, rows * EMB_W * 2),
        name="embed_grad",
    )(ids, dxt)


def partner(x):
    width = x.shape[1]
    lane = lax.broadcasted_iota(jnp.int32, x.shape, 1)
    return jnp.where(lane % HD < HD // 2, pltpu.roll(x, width - HD // 2, 1), pltpu.roll(x, HD // 2, 1))


def qkv_kernel(a_ref, w_ref, cos_ref, sin_ref, q_ref, kv_ref):
    raw = dot_nn(a_ref[...], w_ref[...])
    cosine, sine = cos_ref[...], sin_ref[...]
    for j in range(0, QG, 128):
        x = raw[:, j : j + 128]
        rot = (x * cosine + partner(x) * sine).astype(bf16)
        q_ref[:, j : j + 128] = rot * jnp.asarray(HD**-0.5, bf16)
    x = raw[:, QG:]
    lane = lax.broadcasted_iota(jnp.int32, x.shape, 1)
    kv_ref[...] = jnp.where(lane < HD, x * cosine + partner(x) * sine, x).astype(bf16)


def qkv(a1, w_in, cosine, sine):
    tok = a1.shape[0]
    return pl.pallas_call(
        qkv_kernel,
        grid=(1,),
        in_specs=[
            pl.BlockSpec((tok, D), lambda i: (0, 0)),
            pl.BlockSpec((D, ATTN_IN), lambda i: (0, 0)),
            pl.BlockSpec((tok, 128), lambda i: (0, 0)),
            pl.BlockSpec((tok, 128), lambda i: (0, 0)),
        ],
        out_specs=[
            pl.BlockSpec((tok, QG), lambda i: (0, 0)),
            pl.BlockSpec((tok, 2 * HD), lambda i: (0, 0)),
        ],
        out_shape=[
            jax.ShapeDtypeStruct((tok, QG), bf16),
            jax.ShapeDtypeStruct((tok, 2 * HD), bf16),
        ],
        compiler_params=params(),
        cost_estimate=cost(2 * tok * D * ATTN_IN, 2 * D * ATTN_IN + 2 * tok * D),
        name="qkv",
    )(a1, w_in, cosine, sine)


def split_kv(kv_ref, parts_ref):
    kv = kv_ref[...].reshape(-1, 2 * HD).astype(f32)
    lane = lax.broadcasted_iota(jnp.int32, kv.shape, 1)
    swapped = pltpu.roll(kv, HD, 1)
    zero = jnp.zeros_like(kv)
    low = lane < HD
    parts_ref[0] = jnp.where(low, kv, zero).astype(bf16)
    parts_ref[1] = jnp.where(low, zero, swapped).astype(bf16)
    parts_ref[2] = jnp.where(low, swapped, zero).astype(bf16)
    parts_ref[3] = jnp.where(low, zero, kv).astype(bf16)


def attn_kernel(q_ref, kv_ref, qpos_ref, kpos_ref, o_ref, parts_ref):
    @pl.when(pl.program_id(1) == 0)
    def _():
        split_kv(kv_ref, parts_ref)

    q = q_ref[...]
    allowed = kpos_ref[...] <= qpos_ref[...]
    out = None
    for g in range(2):
        s = jnp.where(allowed, dot_nt(q, parts_ref[g]), NEG)
        p = jnp.exp(s - jnp.max(s, axis=1, keepdims=True))
        p = p * (1.0 / jnp.sum(p, axis=1, keepdims=True))
        part = dot_nn(p.astype(bf16), parts_ref[2 + g])
        out = part if out is None else out + part
    o_ref[...] = out.astype(bf16)


def attn(q, kv_every, qpos, kpos):
    n_ctx, _, seq_tok, _ = kv_every.shape
    keys = n_ctx * seq_tok
    pairs = QG // 128
    return pl.pallas_call(
        attn_kernel,
        grid=(SEQS, pairs),
        in_specs=[
            pl.BlockSpec((seq_tok, 128), lambda s, p: (s, p)),
            pl.BlockSpec((n_ctx, 1, seq_tok, 2 * HD), lambda s, p: (0, s, 0, 0)),
            pl.BlockSpec((seq_tok, 1), lambda s, p: (0, 0)),
            pl.BlockSpec((1, keys), lambda s, p: (0, 0)),
        ],
        out_specs=pl.BlockSpec((seq_tok, 128), lambda s, p: (s, p)),
        out_shape=jax.ShapeDtypeStruct((SEQS * seq_tok, QG), bf16),
        scratch_shapes=[pltpu.VMEM((4, keys, 2 * HD), bf16)],
        compiler_params=params(),
        cost_estimate=cost(
            8 * SEQS * seq_tok * keys * QG, 4 * SEQS * seq_tok * QG, SEQS * GROUP * seq_tok * keys
        ),
        name="attn_fwd",
    )(q, kv_every, qpos.reshape(seq_tok, 1), kpos.reshape(1, keys))


def attn_back_kernel(
    pairs, q_ref, do_ref, kv_ref, qpos_ref, kpos_ref, cos_ref, sin_ref, dq_ref, dkv_ref, parts_ref, acc_ref
):
    pair = pl.program_id(1)

    @pl.when(pair == 0)
    def _():
        split_kv(kv_ref, parts_ref)
        acc_ref[...] = jnp.zeros_like(acc_ref)

    q = q_ref[...]
    do = do_ref[...]
    allowed = kpos_ref[...] <= qpos_ref[...]
    dq = None
    for g in range(2):
        s = jnp.where(allowed, dot_nt(parts_ref[g], q), NEG)
        p = jnp.exp(s - jnp.max(s, axis=0, keepdims=True))
        p = p * (1.0 / jnp.sum(p, axis=0, keepdims=True))
        dp = dot_nt(parts_ref[2 + g], do)
        delta = jnp.sum(p * dp, axis=0, keepdims=True)
        ds = (p * (dp - delta)).astype(bf16)
        part = dot_tn(ds, parts_ref[g])
        dq = part if dq is None else dq + part
        acc_ref[g] += dot_nn(ds, q)
        acc_ref[2 + g] += dot_nn(p.astype(bf16), do)
    dq = dq * (HD**-0.5)
    dq_ref[...] = (dq * cos_ref[...] - partner(dq) * sin_ref[...]).astype(bf16)

    @pl.when(pair == pairs - 1)
    def _():
        lane = lax.broadcasted_iota(jnp.int32, acc_ref.shape[1:], 1)
        grad_k = acc_ref[0] + pltpu.roll(acc_ref[1], HD, 1)
        grad_v = pltpu.roll(acc_ref[2], HD, 1) + acc_ref[3]
        dkv_ref[...] = jnp.where(lane < HD, grad_k, grad_v).astype(bf16).reshape(dkv_ref.shape)


def attn_back(q, do, kv_every, qpos, kpos, cosine, sine):
    n_ctx, _, seq_tok, _ = kv_every.shape
    keys = n_ctx * seq_tok
    pairs = QG // 128
    return pl.pallas_call(
        functools.partial(attn_back_kernel, pairs),
        grid=(SEQS, pairs),
        in_specs=[
            pl.BlockSpec((seq_tok, 128), lambda s, p: (s, p)),
            pl.BlockSpec((seq_tok, 128), lambda s, p: (s, p)),
            pl.BlockSpec((n_ctx, 1, seq_tok, 2 * HD), lambda s, p: (0, s, 0, 0)),
            pl.BlockSpec((1, seq_tok), lambda s, p: (0, 0)),
            pl.BlockSpec((keys, 1), lambda s, p: (0, 0)),
            pl.BlockSpec((seq_tok, 128), lambda s, p: (s, 0)),
            pl.BlockSpec((seq_tok, 128), lambda s, p: (s, 0)),
        ],
        out_specs=[
            pl.BlockSpec((seq_tok, 128), lambda s, p: (s, p)),
            pl.BlockSpec((n_ctx, 1, seq_tok, 2 * HD), lambda s, p: (0, s, 0, 0)),
        ],
        out_shape=[
            jax.ShapeDtypeStruct((SEQS * seq_tok, QG), bf16),
            jax.ShapeDtypeStruct(kv_every.shape, bf16),
        ],
        scratch_shapes=[
            pltpu.VMEM((4, keys, 2 * HD), bf16),
            pltpu.VMEM((4, keys, 2 * HD), f32),
        ],
        compiler_params=params(),
        cost_estimate=cost(
            20 * SEQS * seq_tok * keys * QG, 8 * SEQS * seq_tok * QG, SEQS * GROUP * seq_tok * keys
        ),
        name="attn_bwd",
    )(q, do, kv_every, qpos.reshape(1, seq_tok), kpos.reshape(keys, 1), cosine, sine)


def kv_back_kernel(parts_ref, cos_ref, sin_ref, out_ref):
    x = parts_ref[0].astype(f32)
    for k in range(1, parts_ref.shape[0]):
        x = x + parts_ref[k].astype(f32)
    lane = lax.broadcasted_iota(jnp.int32, x.shape, 1)
    out_ref[...] = jnp.where(lane < HD, x * cos_ref[...] - partner(x) * sin_ref[...], x).astype(bf16)


def kv_back(parts, cosine, sine):
    return pl.pallas_call(
        kv_back_kernel,
        out_shape=jax.ShapeDtypeStruct(parts.shape[1:], bf16),
        compiler_params=params(),
        name="kv_bwd",
    )(parts, cosine, sine)


def head_cast_kernel(block, w_ref, *outs):
    column = lax.broadcasted_iota(jnp.int32, w_ref.shape, 1) + pl.program_id(0) * block
    w = jnp.where(column < VG, w_ref[...], 0.0).astype(bf16)
    count = w.shape[0] // len(outs)
    for k, out_ref in enumerate(outs):
        out_ref[...] = w[k * count : (k + 1) * count]


def head_cast(w_vocab, width, parts):
    rows = w_vocab.shape[0]
    block = 1024
    return pl.pallas_call(
        functools.partial(head_cast_kernel, block),
        grid=(width // block,),
        in_specs=[pl.BlockSpec((rows, block), lambda i: (0, i))],
        out_specs=[pl.BlockSpec((rows // parts, block), lambda i: (0, i))] * parts,
        out_shape=[jax.ShapeDtypeStruct((rows // parts, width), bf16)] * parts,
        compiler_params=params(),
        cost_estimate=cost(rows * width, rows * width * 6),
        name="head_cast",
    )(w_vocab)


def joined(pieces, parts):
    for k in range(0, len(pieces), parts):
        run = [piece[...] for piece in pieces[k : k + parts]]
        yield k // parts, run[0] if parts == 1 else jnp.concatenate(run, axis=0)


def logits_kernel(steps, parts, at_ref, x_ref, slot_ref, *refs):
    pieces, (out_ref, stats_ref, top_ref, total_ref, label_ref) = refs[:-5], refs[-5:]
    step = pl.program_id(0)
    block = out_ref.shape[1]

    @pl.when(step == 0)
    def _():
        top_ref[...] = jnp.full_like(top_ref, NEG)
        total_ref[...] = jnp.zeros_like(total_ref)
        label_ref[...] = jnp.zeros_like(label_ref)

    logits = None
    for k, w in joined(pieces, parts):
        at = pl.multiple_of(at_ref[k], 128)
        term = dot_nn(x_ref[:, pl.ds(at, w.shape[0])], w)
        logits = term if logits is None else logits + term
    column = lax.broadcasted_iota(jnp.int32, logits.shape, 1) + step * block
    logits = jnp.where(column < VG, logits, NEG)
    out_ref[...] = logits
    top = top_ref[...]
    new_top = jnp.maximum(top, jnp.max(logits, axis=1, keepdims=True))
    total_ref[...] = total_ref[...] * jnp.exp(top - new_top) + jnp.sum(
        jnp.exp(logits - new_top), axis=1, keepdims=True
    )
    top_ref[...] = new_top
    label_ref[...] += jnp.sum(jnp.where(column == slot_ref[...], logits, 0.0), axis=1, keepdims=True)

    @pl.when(step == steps - 1)
    def _():
        lane = lax.broadcasted_iota(jnp.int32, (x_ref.shape[0], 128), 1)
        packed = jnp.where(lane == 0, top_ref[...], jnp.where(lane == 1, total_ref[...], label_ref[...]))
        stats_ref[...] = packed.T[:8]


def head_logits(x, slots, pieces, at):
    tok = x.shape[0]
    width = pieces[0].shape[1]
    block = 1024
    steps = width // block
    return pl.pallas_call(
        functools.partial(logits_kernel, steps, len(pieces) // at.shape[0]),
        grid=(steps,),
        in_specs=[
            pl.BlockSpec(memory_space=pltpu.SMEM),
            pl.BlockSpec((tok, D), lambda i: (0, 0)),
            pl.BlockSpec((tok, 1), lambda i: (0, 0)),
        ]
        + [pl.BlockSpec((piece.shape[0], block), lambda i: (0, i)) for piece in pieces],
        out_specs=[
            pl.BlockSpec((tok, block), lambda i: (0, i)),
            pl.BlockSpec((8, tok), lambda i: (0, 0)),
        ],
        out_shape=[
            jax.ShapeDtypeStruct((tok, width), f32),
            jax.ShapeDtypeStruct((8, tok), f32),
        ],
        scratch_shapes=[pltpu.VMEM((tok, 1), f32)] * 3,
        compiler_params=params(),
        cost_estimate=cost(2 * tok * D * width, 2 * D * width + 4 * tok * width, tok * width),
        name="head_logits",
    )(at, x, slots, *pieces)


def dlogits_kernel(steps, parts, at_ref, logits_ref, values_ref, slot_ref, *refs):
    pieces, (dlog_ref, dx_ref, acc_ref) = refs[:-3], refs[-3:]
    step = pl.program_id(0)
    tok, block = logits_ref.shape
    logits = logits_ref[...]
    lse = values_ref[:, 0:1]
    weight = values_ref[:, 1:2]
    column = lax.broadcasted_iota(jnp.int32, logits.shape, 1) + step * block
    hit = jnp.where(column == slot_ref[...], 1.0, 0.0)
    soft = jnp.exp(logits - lse)
    dlog = (weight * ((1.0 + 2.0 * z_weight * lse) * soft - hit)).astype(bf16)
    part = dlog_ref.shape[2]
    for k in range(dlog_ref.shape[0]):
        dlog_ref[k] = dlog[:, k * part : (k + 1) * part]

    @pl.when(step == 0)
    def _():
        acc_ref[...] = jnp.zeros_like(acc_ref)

    for k, w in joined(pieces, parts):
        at = pl.multiple_of(at_ref[k], 128)
        acc_ref[:, pl.ds(at, w.shape[0])] += dot_nt(dlog, w)

    @pl.when(step == steps - 1)
    def _():
        dx_ref[...] = acc_ref[...].astype(bf16)


def head_dlogits(logits, values, slots, pieces, at, part):
    tok, width = logits.shape
    block = 1024
    steps = width // block
    return pl.pallas_call(
        functools.partial(dlogits_kernel, steps, len(pieces) // at.shape[0]),
        grid=(steps,),
        in_specs=[
            pl.BlockSpec(memory_space=pltpu.SMEM),
            pl.BlockSpec((tok, block), lambda i: (0, i)),
            pl.BlockSpec((tok, values.shape[1]), lambda i: (0, 0)),
            pl.BlockSpec((tok, 1), lambda i: (0, 0)),
        ]
        + [pl.BlockSpec((piece.shape[0], block), lambda i: (0, i)) for piece in pieces],
        out_specs=[
            pl.BlockSpec((block // part, tok, part), lambda i: (i, 0, 0)),
            pl.BlockSpec((tok, D), lambda i: (0, 0)),
        ],
        out_shape=[
            jax.ShapeDtypeStruct((width // part, tok, part), bf16),
            jax.ShapeDtypeStruct((tok, D), bf16),
        ],
        scratch_shapes=[pltpu.VMEM((tok, D), f32)],
        compiler_params=params(),
        cost_estimate=cost(2 * tok * D * width, 2 * D * width + 6 * tok * width, tok * width),
        name="head_dlogits",
    )(at, logits, values, slots, *pieces)


def outer_kernel(a_ref, da_ref, b_ref, db_ref, out_ref, *, a_steps):
    step = pl.program_id(0)

    @pl.when(step < a_steps)
    def _():
        out_ref[...] = dot_tn(a_ref[...], da_ref[...]).astype(bf16)

    @pl.when(step >= a_steps)
    def _():
        out_ref[...] = dot_tn(b_ref[...], db_ref[...]).astype(bf16)


def outer_pair(a, da, b, db, block, rows, name):
    tok = a.shape[0]
    a_steps, b_steps = da.shape[1] // block, db.shape[1] // block
    width = da.shape[1] + db.shape[1]
    return pl.pallas_call(
        functools.partial(outer_kernel, a_steps=a_steps),
        grid=(a_steps + b_steps, D // rows),
        in_specs=[
            pl.BlockSpec((tok, rows), lambda i, j: (0, j)),
            pl.BlockSpec((tok, block), lambda i, j: (0, jnp.minimum(i, a_steps - 1))),
            pl.BlockSpec((tok, rows), lambda i, j: (0, j)),
            pl.BlockSpec((tok, block), lambda i, j: (0, jnp.maximum(i - a_steps, 0))),
        ],
        out_specs=pl.BlockSpec((rows, block), lambda i, j: (j, i)),
        out_shape=jax.ShapeDtypeStruct((D, width), bf16),
        compiler_params=params(),
        cost_estimate=cost(2 * tok * D * width, 2 * D * width + 4 * tok * D),
        name=name,
    )(a, da, b, db)


def update_piece(factor, rate, grad, w_ref, m_ref, a_ref, outs, columns):
    new_ref, moment_ref, average_ref, copy_ref = outs
    grad = factor * grad
    moment = momentum_rate * m_ref[:, columns] + grad
    new = w_ref[:, columns] - rate * (grad + momentum_rate * moment)
    new_ref[:, columns] = new
    moment_ref[:, columns] = moment
    average_ref[:, columns] = average_rate * a_ref[:, columns] + (1.0 - average_rate) * new
    copy_ref[:, columns] = new.astype(bf16)


def layer_update_kernel(spreads, factor_ref, *refs):
    grads, (w_ref, m_ref, a_ref), outs = refs[:-7], refs[-7:-4], refs[-4:]
    factor = factor_ref[0, 0]
    for source, inner, outer, width, spread in spreads:
        grad = grads[source][:, inner : inner + width].astype(f32)
        update_piece(factor, BASE * spread, grad, w_ref, m_ref, a_ref, outs, slice(outer, outer + width))


def vocab_update_kernel(part, factor_ref, head_ref, embed_ref, w_ref, m_ref, a_ref, *outs):
    factor = factor_ref[0, 0]
    head_rate = BASE * 2.0 * D**-0.5
    for k in range(head_ref.shape[0]):
        low, high = k * part, min((k + 1) * part, EMB_AT)
        if low >= high:
            continue
        grad = head_ref[k, :, : high - low].astype(f32)
        update_piece(factor, head_rate, grad, w_ref, m_ref, a_ref, outs, slice(low, high))
    edge = EMB_AT - EMB_AT // part * part
    grad_head = head_ref[EMB_AT // part, :, edge : edge + 128].astype(f32)
    grad_embed = embed_ref[:, :128].astype(f32)
    own = lax.broadcasted_iota(jnp.int32, grad_head.shape, 1) < VG - EMB_AT
    update_piece(
        factor,
        jnp.where(own, head_rate, BASE),
        jnp.where(own, grad_head, grad_embed),
        w_ref,
        m_ref,
        a_ref,
        outs,
        slice(EMB_AT, EMB_AT + 128),
    )
    for low in range(128, EMB_W, 1024):
        high = min(low + 1024, EMB_W)
        grad = embed_ref[:, low:high].astype(f32)
        update_piece(factor, BASE, grad, w_ref, m_ref, a_ref, outs, slice(EMB_AT + low, EMB_AT + high))


def call_update(kernel, factor, grads, grad_specs, w, m, a, rows, name):
    total, width = w.shape
    block = pl.BlockSpec((rows, width), lambda i: (i, 0))
    return pl.pallas_call(
        kernel,
        grid=(total // rows,),
        in_specs=[pl.BlockSpec(memory_space=pltpu.SMEM)] + grad_specs + [block] * 3,
        out_specs=[block] * 4,
        out_shape=[jax.ShapeDtypeStruct(w.shape, f32)] * 3 + [jax.ShapeDtypeStruct(w.shape, bf16)],
        compiler_params=params(),
        cost_estimate=cost(10 * total * width, 28 * total * width),
        name=name,
    )(factor.reshape(1, 1), *grads, w, m, a)


def norm_parts(x):
    scale = lax.rsqrt(jnp.mean(x * x, axis=-1, keepdims=True) + eps)
    return x * scale, scale


def norm_back(dy, unit, scale, gain):
    scaled = dy * gain
    dx = scale * (scaled - unit * jnp.mean(scaled * unit, axis=-1, keepdims=True))
    return dx, jnp.sum(dy * unit, axis=0)


def local(
    token_ids,
    labels,
    answer_mask,
    pair_map,
    w_layer,
    w_vocab,
    gains,
    mom_layer,
    mom_vocab,
    mom_gains,
    avg_layer,
    avg_vocab,
    avg_gains,
):
    n_ctx = lax.axis_size("ctx")
    n_head = lax.axis_size("head")
    place = lax.axis_index("ctx")
    shard = lax.axis_index("head")
    tok = token_ids.shape[0]
    rows = w_layer.shape[0]
    seq_tok = tok // SEQS
    span = seq_tok // 2
    chunk = seq_tok // n_head
    own = SEQS * chunk
    length = n_ctx * seq_tok
    part = -(-VG // (n_ctx * 128)) * 128

    def turn(x, axis):
        return lax.dynamic_slice_in_dim(
            jnp.concatenate([x, x], axis), shard * chunk, seq_tok, axis
        )

    def turn_back(x, axis):
        return lax.dynamic_slice_in_dim(
            jnp.concatenate([x, x], axis), seq_tok - shard * chunk, seq_tok, axis
        )

    def head_scatter(x):
        sums = x[:, 0].astype(f32)
        for s in range(1, n_head):
            sent = lax.ppermute(x[:, s], "head", [(i, (i + s) % n_head) for i in range(n_head)])
            sums = sums + sent.astype(f32)
        return sums

    def head_gather(x):
        pieces = [x]
        for s in range(1, n_head):
            pieces.append(lax.ppermute(x, "head", [(i, (i - s) % n_head) for i in range(n_head)]))
        return jnp.stack(pieces, axis=1)

    def sum_own(partial):
        split = partial.astype(bf16).reshape(SEQS, n_head, chunk, D)
        return head_scatter(split).reshape(own, D)

    def spread_all(x):
        return head_gather(x.astype(bf16).reshape(SEQS, chunk, D)).reshape(tok, D)

    layer_b = w_layer.astype(bf16)
    edge = ATTN_IN + QG
    w_attn = lax.all_gather(layer_b[:, :edge], "ctx", axis=0, tiled=True)
    w_ff = lax.all_gather(layer_b[:, edge:], "ctx", axis=0, tiled=True)
    w_out, w_gu, w_down = w_attn[:, ATTN_IN:], w_ff[:, : 2 * FFG], w_ff[:, 2 * FFG :]
    corners = n_ctx == 8
    head_own = head_cast(w_vocab, n_ctx * part, 2 if corners else 1)

    def swap(x, bit):
        return lax.ppermute(x, "ctx", [(i, i ^ bit) for i in range(n_ctx)])

    gain_own = lax.reduce_precision(gains, exponent_bits=8, mantissa_bits=7).T.reshape(3 * rows)
    every = jnp.concatenate([token_ids.astype(f32), answer_mask.astype(f32), gain_own])
    every = lax.all_gather(every, "ctx")
    ids_all = every[:, :tok].astype(jnp.int32).reshape(n_ctx, SEQS, seq_tok)
    ids_all = turn(ids_all, 2).reshape(n_ctx * tok)
    count = jnp.sum(every[:, tok : 2 * tok])
    gain_rows = jnp.moveaxis(every[:, 2 * tok :].reshape(n_ctx, 3, rows), 1, 0).reshape(3, D)
    labels_own = turn(labels.reshape(SEQS, seq_tok), 1).reshape(tok)
    mask_own = turn(answer_mask.reshape(SEQS, seq_tok), 1).reshape(tok)

    offset_id = shard * VG
    local_ids = ids_all - offset_id
    inside = (local_ids >= 0) & (local_ids < VG)
    slots = jnp.where(inside, local_ids + (VG - EMB_AT), -1).reshape(-1, 1)
    picked = lookup(slots, w_vocab).reshape(n_ctx * SEQS, n_head, chunk, rows)
    picked, *head_own = lax.optimization_barrier((picked, *head_own))
    picked = head_scatter(picked).astype(bf16).reshape(n_ctx * own, rows)
    x0 = lax.all_to_all(picked, "ctx", 0, 1, tiled=True).astype(f32)

    unit0, scale0 = norm_parts(x0)
    a1 = spread_all(unit0 * gain_rows[0])
    row = (jnp.arange(seq_tok, dtype=jnp.int32) + shard * chunk) % seq_tok

    def positions(index):
        index = index[:, None]
        at = jnp.where(row // span == 0, index, 2 * n_ctx - 1 - index)
        return at * span + row % span

    qpos = positions(pair_map[place][None])[0]
    kpos = positions(pair_map).reshape(length)
    half = HD // 2
    inverse = 10000.0 ** (-2.0 * np.arange(half) / HD)
    ramp = np.clip((2048.0 * inverse / (2.0 * math.pi) - 1.0) / 31.0, 0.0, 1.0)
    freq = np.tile(((1.0 - ramp) * inverse / 4.0 + ramp * inverse).astype(np.float32), 128 // half)
    sign = np.where(np.arange(128) % HD < half, -1.0, 1.0).astype(np.float32)
    mscale = 0.1 * math.log(4.0) + 1.0
    angle = jnp.tile(qpos, SEQS).astype(f32)[:, None] * freq[None, :]
    cosine = jnp.cos(angle) * mscale
    sine = jnp.sin(angle) * (mscale * sign)[None, :]
    q, kv_own = qkv(a1, w_attn, cosine, sine)
    kv_every = lax.all_gather(kv_own, "ctx").reshape(n_ctx, SEQS, seq_tok, 2 * HD)
    kv_every, *head_own = lax.optimization_barrier((kv_every, *head_own))
    if corners:
        low, high = head_own
        y_low, x_high, x_low, y_high = swap(low, 4), swap(high, 2), swap(low, 2), swap(high, 4)
        near = [low, high, swap(low, 1), swap(high, 1)]
    attn_b = attn(q, kv_every, qpos, kpos)
    x1 = x0 + sum_own(dot_nt(attn_b, w_out))

    unit1, scale1 = norm_parts(x1)
    a2 = spread_all(unit1 * gain_rows[1])
    if corners:
        a2, y_low, x_high = lax.optimization_barrier((a2, y_low, x_high))
        far_low, far_high = swap(y_low, 2), swap(x_high, 4)
        over_y_low, over_x_high = swap(y_low, 1), swap(x_high, 1)
    gate_up = dot_nn(a2, w_gu)

    def glu(values):
        return jax.nn.silu(values[:, :FFG]) * values[:, FFG:]

    hidden_f, glu_back = jax.vjp(glu, gate_up)
    hidden_b = hidden_f.astype(bf16)
    second = sum_own(dot_nt(hidden_b, w_down))
    if corners:
        second, x_low, y_high = lax.optimization_barrier((second, x_low, y_high))
    x2 = x1 + second

    unit2, scale2 = norm_parts(x2)
    final_b = spread_all(unit2 * gain_rows[2])
    label_ids = labels_own - offset_id
    label_slots = jnp.where((label_ids >= 0) & (label_ids < VG), label_ids, -1).reshape(tok, 1)
    if corners:
        over_x_low, over_y_high = swap(x_low, 1), swap(y_high, 1)
        final_b, far_low, far_high = lax.optimization_barrier((final_b, far_low, far_high))
        head_pieces = [*near, x_low, x_high, over_x_low, over_x_high, y_low, y_high, over_y_low, over_y_high]
        head_pieces += [far_low, far_high, swap(far_low, 1), swap(far_high, 1)]
        head_at = jnp.stack([(place ^ bits) * rows for bits in (0, 1, 2, 3, 4, 5, 6, 7)])
    else:
        head_pieces = [lax.all_gather(head_own[0], "ctx", axis=0, tiled=True)]
        head_at = jnp.zeros((1,), jnp.int32)
    logits, stats = head_logits(final_b, label_slots, head_pieces, head_at)
    stats, final_late = lax.optimization_barrier((stats, final_b))
    pieces = [stats]
    for s in range(1, n_head):
        sent = lax.ppermute(stats, "head", [(i, (i - s) % n_head) for i in range(n_head)])
        sent = sent.reshape(8, SEQS, n_head, chunk)
        pieces.append(jnp.roll(sent, s, axis=2).reshape(8, tok))
    doubled = jnp.stack(pieces + pieces)
    stats = lax.dynamic_slice_in_dim(doubled, n_head - shard, n_head, 0)
    top = jnp.max(stats[:, 0], axis=0)
    total = jnp.sum(stats[:, 1] * jnp.exp(stats[:, 0] - top), axis=0)
    lse = top + jnp.log(total)
    weight = mask_own.astype(f32) / count
    terms = weight * (lse - jnp.sum(stats[:, 2], axis=0) + z_weight * lse * lse)
    loss_part = jnp.sum(turn_back(terms.reshape(SEQS, seq_tok), 1))
    values = jnp.stack([lse, weight] + [weight] * 6).T
    dlog_b, d_final = head_dlogits(logits, values, label_slots, head_pieces, head_at, part)
    final_all = lax.all_gather(final_late, "ctx", axis=0, tiled=True)
    dlog_all = lax.all_to_all(dlog_b, "ctx", 0, 0, tiled=True).reshape(n_ctx * tok, part)

    dx2, d_gain2 = norm_back(sum_own(d_final), unit2, scale2, gain_rows[2])
    dyf_b, dlog_all, final_all = lax.optimization_barrier((spread_all(dx2), dlog_all, final_all))
    d_hidden = dot_nn(dyf_b, w_down)
    d_gate_up_b = glu_back(d_hidden)[0].astype(bf16)
    d_second = sum_own(dot_nt(d_gate_up_b, w_gu))
    d_head = dot_tn(final_all, dlog_all)
    head_sq = jnp.sum(d_head * d_head)
    d_second, d_head = lax.optimization_barrier((d_second, d_head.astype(bf16)))
    g_head = lax.all_to_all(d_head.reshape(n_ctx, rows, part), "ctx", 0, 0, tiled=True)
    dx1_norm, d_gain1 = norm_back(d_second, unit1, scale1, gain_rows[1])
    dx1 = dx2 + dx1_norm
    d_ff = outer_pair(a2, d_gate_up_b, dyf_b, hidden_b, FFG, 512, "ff_weight_grad")
    dya_b, d_ff, g_head = lax.optimization_barrier((spread_all(dx1), d_ff, g_head))
    g_ff = lax.psum_scatter(d_ff, "ctx", scatter_dimension=0, tiled=True)
    d_attn_b = dot_nn(dya_b, w_out).astype(bf16)
    d_q, d_kv = attn_back(q, d_attn_b, kv_every, qpos, kpos, cosine, sine)
    d_kv = lax.all_to_all(d_kv.reshape(n_ctx, tok, 2 * HD), "ctx", 0, 0, tiled=True)
    d_raw_b = jnp.concatenate([d_q, kv_back(d_kv, cosine, sine)], axis=1)
    dx0_norm, d_gain0 = norm_back(sum_own(dot_nt(d_raw_b, w_attn[:, :ATTN_IN])), unit0, scale0, gain_rows[0])
    dx0 = dx1 + dx0_norm

    d_at = outer_pair(a1, d_raw_b, dya_b, attn_b, 128, 2048, "attn_weight_grad")
    g_at = lax.all_to_all(d_at.reshape(n_ctx, rows, d_at.shape[1]), "ctx", 0, 0, tiled=True)
    g_at = jnp.sum(g_at.astype(f32), axis=0)
    extra = jnp.pad(jnp.stack([d_gain0, d_gain1, d_gain2]), ((0, 13), (0, 0)))
    moved = lax.all_to_all(jnp.concatenate([dx0, extra]).astype(bf16), "ctx", 1, 0, tiled=True)
    moved = moved.reshape(n_ctx, own + 16, rows)
    gain_part = jnp.sum(moved[:, own:].astype(f32), axis=0).astype(bf16)
    moved = jnp.concatenate([moved[:, :own].reshape(n_ctx * own, rows), gain_part])
    pieces = [moved]
    for s in range(1, n_head):
        pieces.append(lax.ppermute(moved, "head", [(i, (i - s) % n_head) for i in range(n_head)]))
    gain_all = jnp.stack([piece[n_ctx * own :] for piece in pieces + pieces])
    gain_all = lax.dynamic_slice_in_dim(gain_all, n_head - shard, n_head, 0)
    grad_gain = jnp.sum(gain_all.astype(f32), axis=0)[:3].T
    dx0_all = jnp.stack([piece[: n_ctx * own].reshape(n_ctx * SEQS, chunk, rows) for piece in pieces], axis=1)
    g_embed, embed_sq = embed_grad(slots, dx0_all.reshape(n_ctx * tok, rows).T)

    squares = (
        jnp.sum(jnp.square(g_ff.astype(f32)))
        + jnp.sum(jnp.square(g_at))
        + head_sq
        + jnp.sum(embed_sq)
        + jnp.sum(grad_gain * grad_gain) / n_head
    )
    squares = jnp.sum(lax.all_gather(jnp.full((8, 128), squares), "head"), axis=0)
    lane = lax.broadcasted_iota(jnp.int32, (8, 128), 1)
    totals = jnp.sum(lax.all_gather(jnp.where(lane == 0, squares, loss_part), "ctx"), axis=0)
    loss = totals[0, 1]
    grad_norm = jnp.sqrt(totals[0, 0])
    factor = jnp.minimum(1.0, clip_level / grad_norm)

    wide = 32
    spreads = (
        (1, 0, 0, ATTN_IN, D**-0.5),
        (1, ATTN_IN, ATTN_IN, QG, (length / (4.0 * HEADS * HD)) ** 0.5),
        (0, 0, ATTN_IN + QG, 2 * FFG, D**-0.5),
        (0, 2 * FFG, ATTN_IN + QG + 2 * FFG, FFG, FF**-0.5),
    )
    layer = call_update(
        functools.partial(layer_update_kernel, spreads),
        factor,
        (g_ff, g_at),
        [
            pl.BlockSpec((wide, g_ff.shape[1]), lambda i: (i, 0)),
            pl.BlockSpec((wide, g_at.shape[1]), lambda i: (i, 0)),
        ],
        w_layer,
        mom_layer,
        avg_layer,
        wide,
        "layer_update",
    )
    vocab = call_update(
        functools.partial(vocab_update_kernel, part),
        factor,
        (g_head, g_embed),
        [
            pl.BlockSpec((n_ctx, wide // 2, part), lambda i: (0, i, 0)),
            pl.BlockSpec((wide // 2, EMB_W), lambda i: (i, 0)),
        ],
        w_vocab,
        mom_vocab,
        avg_vocab,
        wide // 2,
        "vocab_update",
    )
    grad = factor * grad_gain
    gains_moment = momentum_rate * mom_gains + grad
    gains_new = gains - BASE * 0.1 * (grad + momentum_rate * gains_moment)
    gains_average = average_rate * avg_gains + (1.0 - average_rate) * gains_new
    return (
        *layer,
        *vocab,
        gains_new,
        gains_moment,
        gains_average,
        gains_new.astype(bf16),
        loss,
        grad_norm,
    )


def solution(mesh):
    token, split, gain = P("ctx"), P("ctx", "head"), P("ctx", None)
    in_specs = (token, token, token, P()) + (split, split, gain) * 3
    out_specs = (split,) * 8 + (gain,) * 4 + (P(), P())
    return jax.shard_map(local, mesh=mesh, in_specs=in_specs, out_specs=out_specs, check_vma=False)
```

```python
import functools
import math

import jax
import jax.numpy as jnp
import numpy as np
from jax import lax
from jax.experimental import pallas as pl
from jax.experimental.pallas import tpu as pltpu
from jax.sharding import PartitionSpec as P

D = 2048
HEADS = 32
KV = 4
HD = 64
FF = 5632
V = 32000
SEQS = 2

eps = 1e-05
z_weight = 0.0001
momentum_rate = 0.5
average_rate = 0.5
clip_level = 0.01

GROUP = HEADS // KV
QG = GROUP * HD
FFG = FF // KV
VG = V // KV
ATTN_IN = QG + 2 * HD
NPARAM = D * (2 * HEADS * HD + 2 * KV * HD + 3 * FF + 2 * V + 3)
BASE = 1.5 * math.sqrt(NPARAM) / clip_level
EMB_AT = VG // 128 * 128
EMB_W = 2 * VG - EMB_AT
EMB_STEPS = 7
EMB_BLOCK = EMB_W // EMB_STEPS

f32 = jnp.float32
bf16 = jnp.bfloat16
NEG = -1e30


def dot_nn(a, b):
    return lax.dot_general(a, b, (((1,), (0,)), ((), ())), preferred_element_type=f32)


def dot_nt(a, b):
    return lax.dot_general(a, b, (((1,), (1,)), ((), ())), preferred_element_type=f32)


def dot_tn(a, b):
    return lax.dot_general(a, b, (((0,), (0,)), ((), ())), preferred_element_type=f32)


def cost(flops, nbytes, trans=0):
    return pl.CostEstimate(flops=int(flops), bytes_accessed=int(nbytes), transcendentals=int(trans))


def params(**kw):
    return pltpu.CompilerParams(vmem_limit_bytes=56 * 1024 * 1024, **kw)


def one_hot(ids, base, width):
    column = lax.broadcasted_iota(jnp.int32, (ids.shape[0], width), 1) + base
    return jnp.where(ids == column, jnp.float32(1.0), jnp.float32(0.0)).astype(bf16)


def lookup_kernel(rows, ids_ref, w_ref, out_ref, acc_ref):
    step = pl.program_id(0)
    w = w_ref[...].astype(bf16)
    total = ids_ref.shape[0]

    @pl.when(step == 0)
    def _():
        acc_ref[...] = jnp.zeros_like(acc_ref)

    for r in range(0, total, rows):
        part = pl.ds(r, rows)
        acc_ref[part, :] += dot_nt(one_hot(ids_ref[part, :], step * EMB_BLOCK, EMB_BLOCK), w)

    @pl.when(step == EMB_STEPS - 1)
    def _():
        out_ref[...] = acc_ref[...].astype(bf16)


def lookup(ids, w_vocab):
    total, rows = ids.shape[0], w_vocab.shape[0]
    return pl.pallas_call(
        functools.partial(lookup_kernel, min(512, total)),
        grid=(EMB_STEPS,),
        in_specs=[
            pl.BlockSpec((total, 1), lambda i: (0, 0)),
            pl.BlockSpec((pl.Element(rows), pl.Element(EMB_BLOCK)), lambda i: (0, (EMB_AT // 128 + EMB_BLOCK // 128 * i) * 128)),
        ],
        out_specs=pl.BlockSpec((total, rows), lambda i: (0, 0)),
        out_shape=jax.ShapeDtypeStruct((total, rows), bf16),
        scratch_shapes=[pltpu.VMEM((total, rows), f32)],
        compiler_params=params(),
        cost_estimate=cost(2 * total * rows * EMB_W, rows * EMB_W * 4),
        name="embed_lookup",
    )(ids, w_vocab)


def embed_grad_kernel(rows, ids_ref, dxt_ref, out_ref, sq_ref):
    step = pl.program_id(0)
    total = ids_ref.shape[0]
    acc = jnp.zeros(out_ref.shape, f32)
    for r in range(0, total, rows):
        hot = one_hot(ids_ref[pl.ds(r, rows), :], step * EMB_BLOCK, EMB_BLOCK)
        acc = acc + dot_nn(dxt_ref[:, pl.ds(r, rows)], hot)
    out_ref[...] = acc.astype(bf16)
    square = acc * acc
    lanes = sum(square[:, k : k + 128] for k in range(0, EMB_BLOCK, 128))
    part = sum(lanes[k : k + 8] for k in range(0, lanes.shape[0], 8))

    @pl.when(step == 0)
    def _():
        sq_ref[...] = jnp.zeros_like(sq_ref)

    sq_ref[...] += part


def embed_grad(ids, dxt):
    rows, total = dxt.shape
    return pl.pallas_call(
        functools.partial(embed_grad_kernel, min(512, total)),
        grid=(EMB_STEPS,),
        in_specs=[
            pl.BlockSpec((total, 1), lambda i: (0, 0)),
            pl.BlockSpec((rows, total), lambda i: (0, 0)),
        ],
        out_specs=[
            pl.BlockSpec((rows, EMB_BLOCK), lambda i: (0, i)),
            pl.BlockSpec((8, 128), lambda i: (0, 0)),
        ],
        out_shape=[
            jax.ShapeDtypeStruct((rows, EMB_W), bf16),
            jax.ShapeDtypeStruct((8, 128), f32),
        ],
        compiler_params=params(),
        cost_estimate=cost(2 * total * rows * EMB_W, rows * EMB_W * 2),
        name="embed_grad",
    )(ids, dxt)


def partner(x):
    width = x.shape[1]
    lane = lax.broadcasted_iota(jnp.int32, x.shape, 1)
    return jnp.where(lane % HD < HD // 2, pltpu.roll(x, width - HD // 2, 1), pltpu.roll(x, HD // 2, 1))


def qkv_kernel(a_ref, w_ref, cos_ref, sin_ref, q_ref, kv_ref):
    raw = dot_nn(a_ref[...], w_ref[...])
    cosine, sine = cos_ref[...], sin_ref[...]
    for j in range(0, QG, 128):
        x = raw[:, j : j + 128]
        rot = (x * cosine + partner(x) * sine).astype(bf16)
        q_ref[:, j : j + 128] = rot * jnp.asarray(HD**-0.5, bf16)
    x = raw[:, QG:]
    lane = lax.broadcasted_iota(jnp.int32, x.shape, 1)
    kv_ref[...] = jnp.where(lane < HD, x * cosine + partner(x) * sine, x).astype(bf16)


def qkv(a1, w_in, cosine, sine):
    tok = a1.shape[0]
    return pl.pallas_call(
        qkv_kernel,
        grid=(1,),
        in_specs=[
            pl.BlockSpec((tok, D), lambda i: (0, 0)),
            pl.BlockSpec((D, ATTN_IN), lambda i: (0, 0)),
            pl.BlockSpec((tok, 128), lambda i: (0, 0)),
            pl.BlockSpec((tok, 128), lambda i: (0, 0)),
        ],
        out_specs=[
            pl.BlockSpec((tok, QG), lambda i: (0, 0)),
            pl.BlockSpec((tok, 2 * HD), lambda i: (0, 0)),
        ],
        out_shape=[
            jax.ShapeDtypeStruct((tok, QG), bf16),
            jax.ShapeDtypeStruct((tok, 2 * HD), bf16),
        ],
        compiler_params=params(),
        cost_estimate=cost(2 * tok * D * ATTN_IN, 2 * D * ATTN_IN + 2 * tok * D),
        name="qkv",
    )(a1, w_in, cosine, sine)


def split_kv(kv_ref, parts_ref):
    kv = kv_ref[...].reshape(-1, 2 * HD).astype(f32)
    lane = lax.broadcasted_iota(jnp.int32, kv.shape, 1)
    swapped = pltpu.roll(kv, HD, 1)
    zero = jnp.zeros_like(kv)
    low = lane < HD
    parts_ref[0] = jnp.where(low, kv, zero).astype(bf16)
    parts_ref[1] = jnp.where(low, zero, swapped).astype(bf16)
    parts_ref[2] = jnp.where(low, swapped, zero).astype(bf16)
    parts_ref[3] = jnp.where(low, zero, kv).astype(bf16)


def attn_kernel(q_ref, kv_ref, qpos_ref, kpos_ref, o_ref, parts_ref):
    @pl.when(pl.program_id(1) == 0)
    def _():
        split_kv(kv_ref, parts_ref)

    q = q_ref[...]
    allowed = kpos_ref[...] <= qpos_ref[...]
    out = None
    for g in range(2):
        s = jnp.where(allowed, dot_nt(q, parts_ref[g]), NEG)
        p = jnp.exp(s - jnp.max(s, axis=1, keepdims=True))
        p = p * (1.0 / jnp.sum(p, axis=1, keepdims=True))
        part = dot_nn(p.astype(bf16), parts_ref[2 + g])
        out = part if out is None else out + part
    o_ref[...] = out.astype(bf16)


def attn(q, kv_every, qpos, kpos):
    n_ctx, _, seq_tok, _ = kv_every.shape
    keys = n_ctx * seq_tok
    pairs = QG // 128
    return pl.pallas_call(
        attn_kernel,
        grid=(SEQS, pairs),
        in_specs=[
            pl.BlockSpec((seq_tok, 128), lambda s, p: (s, p)),
            pl.BlockSpec((n_ctx, 1, seq_tok, 2 * HD), lambda s, p: (0, s, 0, 0)),
            pl.BlockSpec((seq_tok, 1), lambda s, p: (0, 0)),
            pl.BlockSpec((1, keys), lambda s, p: (0, 0)),
        ],
        out_specs=pl.BlockSpec((seq_tok, 128), lambda s, p: (s, p)),
        out_shape=jax.ShapeDtypeStruct((SEQS * seq_tok, QG), bf16),
        scratch_shapes=[pltpu.VMEM((4, keys, 2 * HD), bf16)],
        compiler_params=params(),
        cost_estimate=cost(
            8 * SEQS * seq_tok * keys * QG, 4 * SEQS * seq_tok * QG, SEQS * GROUP * seq_tok * keys
        ),
        name="attn_fwd",
    )(q, kv_every, qpos.reshape(seq_tok, 1), kpos.reshape(1, keys))


def attn_back_kernel(
    pairs, q_ref, do_ref, kv_ref, qpos_ref, kpos_ref, cos_ref, sin_ref, dq_ref, dkv_ref, parts_ref, acc_ref
):
    pair = pl.program_id(1)

    @pl.when(pair == 0)
    def _():
        split_kv(kv_ref, parts_ref)
        acc_ref[...] = jnp.zeros_like(acc_ref)

    q = q_ref[...]
    do = do_ref[...]
    allowed = kpos_ref[...] <= qpos_ref[...]
    dq = None
    for g in range(2):
        s = jnp.where(allowed, dot_nt(parts_ref[g], q), NEG)
        p = jnp.exp(s - jnp.max(s, axis=0, keepdims=True))
        p = p * (1.0 / jnp.sum(p, axis=0, keepdims=True))
        dp = dot_nt(parts_ref[2 + g], do)
        delta = jnp.sum(p * dp, axis=0, keepdims=True)
        ds = (p * (dp - delta)).astype(bf16)
        part = dot_tn(ds, parts_ref[g])
        dq = part if dq is None else dq + part
        acc_ref[g] += dot_nn(ds, q)
        acc_ref[2 + g] += dot_nn(p.astype(bf16), do)
    dq = dq * (HD**-0.5)
    dq_ref[...] = (dq * cos_ref[...] - partner(dq) * sin_ref[...]).astype(bf16)

    @pl.when(pair == pairs - 1)
    def _():
        lane = lax.broadcasted_iota(jnp.int32, acc_ref.shape[1:], 1)
        grad_k = acc_ref[0] + pltpu.roll(acc_ref[1], HD, 1)
        grad_v = pltpu.roll(acc_ref[2], HD, 1) + acc_ref[3]
        dkv_ref[...] = jnp.where(lane < HD, grad_k, grad_v).astype(bf16).reshape(dkv_ref.shape)


def attn_back(q, do, kv_every, qpos, kpos, cosine, sine):
    n_ctx, _, seq_tok, _ = kv_every.shape
    keys = n_ctx * seq_tok
    pairs = QG // 128
    return pl.pallas_call(
        functools.partial(attn_back_kernel, pairs),
        grid=(SEQS, pairs),
        in_specs=[
            pl.BlockSpec((seq_tok, 128), lambda s, p: (s, p)),
            pl.BlockSpec((seq_tok, 128), lambda s, p: (s, p)),
            pl.BlockSpec((n_ctx, 1, seq_tok, 2 * HD), lambda s, p: (0, s, 0, 0)),
            pl.BlockSpec((1, seq_tok), lambda s, p: (0, 0)),
            pl.BlockSpec((keys, 1), lambda s, p: (0, 0)),
            pl.BlockSpec((seq_tok, 128), lambda s, p: (s, 0)),
            pl.BlockSpec((seq_tok, 128), lambda s, p: (s, 0)),
        ],
        out_specs=[
            pl.BlockSpec((seq_tok, 128), lambda s, p: (s, p)),
            pl.BlockSpec((n_ctx, 1, seq_tok, 2 * HD), lambda s, p: (0, s, 0, 0)),
        ],
        out_shape=[
            jax.ShapeDtypeStruct((SEQS * seq_tok, QG), bf16),
            jax.ShapeDtypeStruct(kv_every.shape, bf16),
        ],
        scratch_shapes=[
            pltpu.VMEM((4, keys, 2 * HD), bf16),
            pltpu.VMEM((4, keys, 2 * HD), f32),
        ],
        compiler_params=params(),
        cost_estimate=cost(
            20 * SEQS * seq_tok * keys * QG, 8 * SEQS * seq_tok * QG, SEQS * GROUP * seq_tok * keys
        ),
        name="attn_bwd",
    )(q, do, kv_every, qpos.reshape(1, seq_tok), kpos.reshape(keys, 1), cosine, sine)


def kv_back_kernel(parts_ref, cos_ref, sin_ref, out_ref):
    x = parts_ref[0].astype(f32)
    for k in range(1, parts_ref.shape[0]):
        x = x + parts_ref[k].astype(f32)
    lane = lax.broadcasted_iota(jnp.int32, x.shape, 1)
    out_ref[...] = jnp.where(lane < HD, x * cos_ref[...] - partner(x) * sin_ref[...], x).astype(bf16)


def kv_back(parts, cosine, sine):
    return pl.pallas_call(
        kv_back_kernel,
        out_shape=jax.ShapeDtypeStruct(parts.shape[1:], bf16),
        compiler_params=params(),
        name="kv_bwd",
    )(parts, cosine, sine)


def head_cast_kernel(block, w_ref, *outs):
    column = lax.broadcasted_iota(jnp.int32, w_ref.shape, 1) + pl.program_id(0) * block
    w = jnp.where(column < VG, w_ref[...], 0.0).astype(bf16)
    count = w.shape[0] // len(outs)
    for k, out_ref in enumerate(outs):
        out_ref[...] = w[k * count : (k + 1) * count]


def head_cast(w_vocab, width, parts):
    rows = w_vocab.shape[0]
    block = 1024
    return pl.pallas_call(
        functools.partial(head_cast_kernel, block),
        grid=(width // block,),
        in_specs=[pl.BlockSpec((rows, block), lambda i: (0, i))],
        out_specs=[pl.BlockSpec((rows // parts, block), lambda i: (0, i))] * parts,
        out_shape=[jax.ShapeDtypeStruct((rows // parts, width), bf16)] * parts,
        compiler_params=params(),
        cost_estimate=cost(rows * width, rows * width * 6),
        name="head_cast",
    )(w_vocab)


def joined(pieces, parts):
    for k in range(0, len(pieces), parts):
        run = [piece[...] for piece in pieces[k : k + parts]]
        yield k // parts, run[0] if parts == 1 else jnp.concatenate(run, axis=0)


def logits_kernel(steps, parts, at_ref, x_ref, slot_ref, *refs):
    pieces, (out_ref, stats_ref, top_ref, total_ref, label_ref) = refs[:-5], refs[-5:]
    step = pl.program_id(0)
    block = out_ref.shape[1]

    @pl.when(step == 0)
    def _():
        top_ref[...] = jnp.full_like(top_ref, NEG)
        total_ref[...] = jnp.zeros_like(total_ref)
        label_ref[...] = jnp.zeros_like(label_ref)

    logits = None
    for k, w in joined(pieces, parts):
        at = pl.multiple_of(at_ref[k], 128)
        term = dot_nn(x_ref[:, pl.ds(at, w.shape[0])], w)
        logits = term if logits is None else logits + term
    column = lax.broadcasted_iota(jnp.int32, logits.shape, 1) + step * block
    logits = jnp.where(column < VG, logits, NEG)
    out_ref[...] = logits
    top = top_ref[...]
    new_top = jnp.maximum(top, jnp.max(logits, axis=1, keepdims=True))
    total_ref[...] = total_ref[...] * jnp.exp(top - new_top) + jnp.sum(
        jnp.exp(logits - new_top), axis=1, keepdims=True
    )
    top_ref[...] = new_top
    label_ref[...] += jnp.sum(jnp.where(column == slot_ref[...], logits, 0.0), axis=1, keepdims=True)

    @pl.when(step == steps - 1)
    def _():
        lane = lax.broadcasted_iota(jnp.int32, (x_ref.shape[0], 128), 1)
        packed = jnp.where(lane == 0, top_ref[...], jnp.where(lane == 1, total_ref[...], label_ref[...]))
        stats_ref[...] = packed.T[:8]


def head_logits(x, slots, pieces, at):
    tok = x.shape[0]
    width = pieces[0].shape[1]
    block = 1024
    steps = width // block
    return pl.pallas_call(
        functools.partial(logits_kernel, steps, len(pieces) // at.shape[0]),
        grid=(steps,),
        in_specs=[
            pl.BlockSpec(memory_space=pltpu.SMEM),
            pl.BlockSpec((tok, D), lambda i: (0, 0)),
            pl.BlockSpec((tok, 1), lambda i: (0, 0)),
        ]
        + [pl.BlockSpec((piece.shape[0], block), lambda i: (0, i)) for piece in pieces],
        out_specs=[
            pl.BlockSpec((tok, block), lambda i: (0, i)),
            pl.BlockSpec((8, tok), lambda i: (0, 0)),
        ],
        out_shape=[
            jax.ShapeDtypeStruct((tok, width), f32),
            jax.ShapeDtypeStruct((8, tok), f32),
        ],
        scratch_shapes=[pltpu.VMEM((tok, 1), f32)] * 3,
        compiler_params=params(),
        cost_estimate=cost(2 * tok * D * width, 2 * D * width + 4 * tok * width, tok * width),
        name="head_logits",
    )(at, x, slots, *pieces)


def dlogits_kernel(steps, parts, at_ref, logits_ref, values_ref, slot_ref, *refs):
    pieces, (dlog_ref, dx_ref, acc_ref) = refs[:-3], refs[-3:]
    step = pl.program_id(0)
    tok, block = logits_ref.shape
    logits = logits_ref[...]
    lse = values_ref[:, 0:1]
    weight = values_ref[:, 1:2]
    column = lax.broadcasted_iota(jnp.int32, logits.shape, 1) + step * block
    hit = jnp.where(column == slot_ref[...], 1.0, 0.0)
    soft = jnp.exp(logits - lse)
    dlog = (weight * ((1.0 + 2.0 * z_weight * lse) * soft - hit)).astype(bf16)
    part = dlog_ref.shape[2]
    for k in range(dlog_ref.shape[0]):
        dlog_ref[k] = dlog[:, k * part : (k + 1) * part]

    @pl.when(step == 0)
    def _():
        acc_ref[...] = jnp.zeros_like(acc_ref)

    for k, w in joined(pieces, parts):
        at = pl.multiple_of(at_ref[k], 128)
        acc_ref[:, pl.ds(at, w.shape[0])] += dot_nt(dlog, w)

    @pl.when(step == steps - 1)
    def _():
        dx_ref[...] = acc_ref[...].astype(bf16)


def head_dlogits(logits, values, slots, pieces, at, part):
    tok, width = logits.shape
    block = 1024
    steps = width // block
    return pl.pallas_call(
        functools.partial(dlogits_kernel, steps, len(pieces) // at.shape[0]),
        grid=(steps,),
        in_specs=[
            pl.BlockSpec(memory_space=pltpu.SMEM),
            pl.BlockSpec((tok, block), lambda i: (0, i)),
            pl.BlockSpec((tok, values.shape[1]), lambda i: (0, 0)),
            pl.BlockSpec((tok, 1), lambda i: (0, 0)),
        ]
        + [pl.BlockSpec((piece.shape[0], block), lambda i: (0, i)) for piece in pieces],
        out_specs=[
            pl.BlockSpec((block // part, tok, part), lambda i: (i, 0, 0)),
            pl.BlockSpec((tok, D), lambda i: (0, 0)),
        ],
        out_shape=[
            jax.ShapeDtypeStruct((width // part, tok, part), bf16),
            jax.ShapeDtypeStruct((tok, D), bf16),
        ],
        scratch_shapes=[pltpu.VMEM((tok, D), f32)],
        compiler_params=params(),
        cost_estimate=cost(2 * tok * D * width, 2 * D * width + 6 * tok * width, tok * width),
        name="head_dlogits",
    )(at, logits, values, slots, *pieces)


def outer_kernel(a_ref, da_ref, b_ref, db_ref, out_ref, *, a_steps):
    step = pl.program_id(0)

    @pl.when(step < a_steps)
    def _():
        out_ref[...] = dot_tn(a_ref[...], da_ref[...]).astype(bf16)

    @pl.when(step >= a_steps)
    def _():
        out_ref[...] = dot_tn(b_ref[...], db_ref[...]).astype(bf16)


def outer_pair(a, da, b, db, block, rows, name):
    tok = a.shape[0]
    a_steps, b_steps = da.shape[1] // block, db.shape[1] // block
    width = da.shape[1] + db.shape[1]
    return pl.pallas_call(
        functools.partial(outer_kernel, a_steps=a_steps),
        grid=(a_steps + b_steps, D // rows),
        in_specs=[
            pl.BlockSpec((tok, rows), lambda i, j: (0, j)),
            pl.BlockSpec((tok, block), lambda i, j: (0, jnp.minimum(i, a_steps - 1))),
            pl.BlockSpec((tok, rows), lambda i, j: (0, j)),
            pl.BlockSpec((tok, block), lambda i, j: (0, jnp.maximum(i - a_steps, 0))),
        ],
        out_specs=pl.BlockSpec((rows, block), lambda i, j: (j, i)),
        out_shape=jax.ShapeDtypeStruct((D, width), bf16),
        compiler_params=params(),
        cost_estimate=cost(2 * tok * D * width, 2 * D * width + 4 * tok * D),
        name=name,
    )(a, da, b, db)


def update_piece(factor, rate, grad, w_ref, m_ref, a_ref, outs, columns):
    new_ref, moment_ref, average_ref, copy_ref = outs
    grad = factor * grad
    moment = momentum_rate * m_ref[:, columns] + grad
    new = w_ref[:, columns] - rate * (grad + momentum_rate * moment)
    new_ref[:, columns] = new
    moment_ref[:, columns] = moment
    average_ref[:, columns] = average_rate * a_ref[:, columns] + (1.0 - average_rate) * new
    copy_ref[:, columns] = new.astype(bf16)


def layer_update_kernel(spreads, factor_ref, *refs):
    grads, (w_ref, m_ref, a_ref), outs = refs[:-7], refs[-7:-4], refs[-4:]
    factor = factor_ref[0, 0]
    for source, inner, outer, width, spread in spreads:
        grad = grads[source][:, inner : inner + width].astype(f32)
        update_piece(factor, BASE * spread, grad, w_ref, m_ref, a_ref, outs, slice(outer, outer + width))


def vocab_update_kernel(part, factor_ref, head_ref, embed_ref, w_ref, m_ref, a_ref, *outs):
    factor = factor_ref[0, 0]
    head_rate = BASE * 2.0 * D**-0.5
    for k in range(head_ref.shape[0]):
        low, high = k * part, min((k + 1) * part, EMB_AT)
        if low >= high:
            continue
        grad = head_ref[k, :, : high - low].astype(f32)
        update_piece(factor, head_rate, grad, w_ref, m_ref, a_ref, outs, slice(low, high))
    edge = EMB_AT - EMB_AT // part * part
    grad_head = head_ref[EMB_AT // part, :, edge : edge + 128].astype(f32)
    grad_embed = embed_ref[:, :128].astype(f32)
    own = lax.broadcasted_iota(jnp.int32, grad_head.shape, 1) < VG - EMB_AT
    update_piece(
        factor,
        jnp.where(own, head_rate, BASE),
        jnp.where(own, grad_head, grad_embed),
        w_ref,
        m_ref,
        a_ref,
        outs,
        slice(EMB_AT, EMB_AT + 128),
    )
    for low in range(128, EMB_W, 1024):
        high = min(low + 1024, EMB_W)
        grad = embed_ref[:, low:high].astype(f32)
        update_piece(factor, BASE, grad, w_ref, m_ref, a_ref, outs, slice(EMB_AT + low, EMB_AT + high))


def call_update(kernel, factor, grads, grad_specs, w, m, a, rows, name):
    total, width = w.shape
    block = pl.BlockSpec((rows, width), lambda i: (i, 0))
    return pl.pallas_call(
        kernel,
        grid=(total // rows,),
        in_specs=[pl.BlockSpec(memory_space=pltpu.SMEM)] + grad_specs + [block] * 3,
        out_specs=[block] * 4,
        out_shape=[jax.ShapeDtypeStruct(w.shape, f32)] * 3 + [jax.ShapeDtypeStruct(w.shape, bf16)],
        compiler_params=params(),
        cost_estimate=cost(10 * total * width, 28 * total * width),
        name=name,
    )(factor.reshape(1, 1), *grads, w, m, a)


def norm_parts(x):
    scale = lax.rsqrt(jnp.mean(x * x, axis=-1, keepdims=True) + eps)
    return x * scale, scale


def norm_back(dy, unit, scale, gain):
    scaled = dy * gain
    dx = scale * (scaled - unit * jnp.mean(scaled * unit, axis=-1, keepdims=True))
    return dx, jnp.sum(dy * unit, axis=0)


def local(
    token_ids,
    labels,
    answer_mask,
    pair_map,
    w_layer,
    w_vocab,
    gains,
    mom_layer,
    mom_vocab,
    mom_gains,
    avg_layer,
    avg_vocab,
    avg_gains,
):
    n_ctx = lax.axis_size("ctx")
    n_head = lax.axis_size("head")
    place = lax.axis_index("ctx")
    shard = lax.axis_index("head")
    tok = token_ids.shape[0]
    rows = w_layer.shape[0]
    seq_tok = tok // SEQS
    span = seq_tok // 2
    chunk = seq_tok // n_head
    own = SEQS * chunk
    length = n_ctx * seq_tok
    part = -(-VG // (n_ctx * 128)) * 128

    def turn(x, axis):
        return lax.dynamic_slice_in_dim(
            jnp.concatenate([x, x], axis), shard * chunk, seq_tok, axis
        )

    def turn_back(x, axis):
        return lax.dynamic_slice_in_dim(
            jnp.concatenate([x, x], axis), seq_tok - shard * chunk, seq_tok, axis
        )

    def head_scatter(x):
        sums = x[:, 0].astype(f32)
        for s in range(1, n_head):
            sent = lax.ppermute(x[:, s], "head", [(i, (i + s) % n_head) for i in range(n_head)])
            sums = sums + sent.astype(f32)
        return sums

    def head_gather(x):
        pieces = [x]
        for s in range(1, n_head):
            pieces.append(lax.ppermute(x, "head", [(i, (i - s) % n_head) for i in range(n_head)]))
        return jnp.stack(pieces, axis=1)

    def sum_own(partial):
        split = partial.astype(bf16).reshape(SEQS, n_head, chunk, D)
        return head_scatter(split).reshape(own, D)

    def spread_all(x):
        return head_gather(x.astype(bf16).reshape(SEQS, chunk, D)).reshape(tok, D)

    layer_b = w_layer.astype(bf16)
    edge = ATTN_IN + QG
    w_attn = lax.all_gather(layer_b[:, :edge], "ctx", axis=0, tiled=True)
    w_ff = lax.all_gather(layer_b[:, edge:], "ctx", axis=0, tiled=True)
    w_out, w_gu, w_down = w_attn[:, ATTN_IN:], w_ff[:, : 2 * FFG], w_ff[:, 2 * FFG :]
    corners = n_ctx == 8
    head_own = head_cast(w_vocab, n_ctx * part, 2 if corners else 1)

    def swap(x, bit):
        return lax.ppermute(x, "ctx", [(i, i ^ bit) for i in range(n_ctx)])

    gain_own = lax.reduce_precision(gains, exponent_bits=8, mantissa_bits=7).T.reshape(3 * rows)
    every = jnp.concatenate([token_ids.astype(f32), answer_mask.astype(f32), gain_own])
    every = lax.all_gather(every, "ctx")
    ids_all = every[:, :tok].astype(jnp.int32).reshape(n_ctx, SEQS, seq_tok)
    ids_all = turn(ids_all, 2).reshape(n_ctx * tok)
    count = jnp.sum(every[:, tok : 2 * tok])
    gain_rows = jnp.moveaxis(every[:, 2 * tok :].reshape(n_ctx, 3, rows), 1, 0).reshape(3, D)
    labels_own = turn(labels.reshape(SEQS, seq_tok), 1).reshape(tok)
    mask_own = turn(answer_mask.reshape(SEQS, seq_tok), 1).reshape(tok)

    offset_id = shard * VG
    local_ids = ids_all - offset_id
    inside = (local_ids >= 0) & (local_ids < VG)
    slots = jnp.where(inside, local_ids + (VG - EMB_AT), -1).reshape(-1, 1)
    picked = lookup(slots, w_vocab).reshape(n_ctx * SEQS, n_head, chunk, rows)
    picked, *head_own = lax.optimization_barrier((picked, *head_own))
    picked = head_scatter(picked).astype(bf16).reshape(n_ctx * own, rows)
    x0 = lax.all_to_all(picked, "ctx", 0, 1, tiled=True).astype(f32)

    unit0, scale0 = norm_parts(x0)
    a1 = spread_all(unit0 * gain_rows[0])
    row = (jnp.arange(seq_tok, dtype=jnp.int32) + shard * chunk) % seq_tok

    def positions(index):
        index = index[:, None]
        at = jnp.where(row // span == 0, index, 2 * n_ctx - 1 - index)
        return at * span + row % span

    qpos = positions(pair_map[place][None])[0]
    kpos = positions(pair_map).reshape(length)
    half = HD // 2
    inverse = 10000.0 ** (-2.0 * np.arange(half) / HD)
    ramp = np.clip((2048.0 * inverse / (2.0 * math.pi) - 1.0) / 31.0, 0.0, 1.0)
    freq = np.tile(((1.0 - ramp) * inverse / 4.0 + ramp * inverse).astype(np.float32), 128 // half)
    sign = np.where(np.arange(128) % HD < half, -1.0, 1.0).astype(np.float32)
    mscale = 0.1 * math.log(4.0) + 1.0
    angle = jnp.tile(qpos, SEQS).astype(f32)[:, None] * freq[None, :]
    cosine = jnp.cos(angle) * mscale
    sine = jnp.sin(angle) * (mscale * sign)[None, :]
    q, kv_own = qkv(a1, w_attn, cosine, sine)
    kv_every = lax.all_gather(kv_own, "ctx").reshape(n_ctx, SEQS, seq_tok, 2 * HD)
    kv_every, *head_own = lax.optimization_barrier((kv_every, *head_own))
    if corners:
        low, high = head_own
        y_low, x_high, x_low, y_high = swap(low, 4), swap(high, 2), swap(low, 2), swap(high, 4)
        over_low, over_high = swap(low, 1), swap(high, 1)
    attn_b = attn(q, kv_every, qpos, kpos)
    x1 = x0 + sum_own(dot_nt(attn_b, w_out))

    unit1, scale1 = norm_parts(x1)
    a2 = spread_all(unit1 * gain_rows[1])
    if corners:
        a2, y_low, x_high = lax.optimization_barrier((a2, y_low, x_high))
        far_low, far_high = swap(y_low, 2), swap(x_high, 4)
        over_y_low, over_x_high = swap(y_low, 1), swap(x_high, 1)
    gate_up = dot_nn(a2, w_gu)

    def glu(values):
        return jax.nn.silu(values[:, :FFG]) * values[:, FFG:]

    hidden_f, glu_back = jax.vjp(glu, gate_up)
    hidden_b = hidden_f.astype(bf16)
    second = sum_own(dot_nt(hidden_b, w_down))
    if corners:
        second, *placed = lax.optimization_barrier(
            (second, x_low, y_high)
        )
        x_low, y_high = placed
    x2 = x1 + second

    unit2, scale2 = norm_parts(x2)
    final_b = spread_all(unit2 * gain_rows[2])
    label_ids = labels_own - offset_id
    label_slots = jnp.where((label_ids >= 0) & (label_ids < VG), label_ids, -1).reshape(tok, 1)
    if corners:
        over_x_low, over_y_high = swap(x_low, 1), swap(y_high, 1)
        final_b, far_low, far_high = lax.optimization_barrier((final_b, far_low, far_high))
        head_pieces = [low, high, over_low, over_high, x_low, x_high, over_x_low, over_x_high, y_low, y_high, over_y_low, over_y_high]
        head_pieces += [far_low, far_high, swap(far_low, 1), swap(far_high, 1)]
        head_at = jnp.stack([(place ^ bits) * rows for bits in (0, 1, 2, 3, 4, 5, 6, 7)])
    else:
        head_pieces = [lax.all_gather(head_own[0], "ctx", axis=0, tiled=True)]
        head_at = jnp.zeros((1,), jnp.int32)
    logits, stats = head_logits(final_b, label_slots, head_pieces, head_at)
    stats, final_late = lax.optimization_barrier((stats, final_b))
    pieces = [stats]
    for s in range(1, n_head):
        sent = lax.ppermute(stats, "head", [(i, (i - s) % n_head) for i in range(n_head)])
        sent = sent.reshape(8, SEQS, n_head, chunk)
        pieces.append(jnp.roll(sent, s, axis=2).reshape(8, tok))
    doubled = jnp.stack(pieces + pieces)
    stats = lax.dynamic_slice_in_dim(doubled, n_head - shard, n_head, 0)
    top = jnp.max(stats[:, 0], axis=0)
    total = jnp.sum(stats[:, 1] * jnp.exp(stats[:, 0] - top), axis=0)
    lse = top + jnp.log(total)
    weight = mask_own.astype(f32) / count
    terms = weight * (lse - jnp.sum(stats[:, 2], axis=0) + z_weight * lse * lse)
    loss_part = jnp.sum(turn_back(terms.reshape(SEQS, seq_tok), 1))
    values = jnp.stack([lse, weight] + [weight] * 6).T
    dlog_b, d_final = head_dlogits(logits, values, label_slots, head_pieces, head_at, part)
    final_all = lax.all_gather(final_late, "ctx", axis=0, tiled=True)
    dlog_all = lax.all_to_all(dlog_b, "ctx", 0, 0, tiled=True).reshape(n_ctx * tok, part)

    dx2, d_gain2 = norm_back(sum_own(d_final), unit2, scale2, gain_rows[2])
    dyf_b = spread_all(dx2)
    d_hidden = dot_nn(dyf_b, w_down)
    d_gate_up_b = glu_back(d_hidden)[0].astype(bf16)
    d_second = sum_own(dot_nt(d_gate_up_b, w_gu))
    d_ff = outer_pair(a2, d_gate_up_b, dyf_b, hidden_b, FFG, 512, "ff_weight_grad")
    d_second, d_ff, dlog_all, final_all = lax.optimization_barrier((d_second, d_ff, dlog_all, final_all))
    g_ff = lax.psum_scatter(d_ff, "ctx", scatter_dimension=0, tiled=True)
    dx1_norm, d_gain1 = norm_back(d_second, unit1, scale1, gain_rows[1])
    dx1 = dx2 + dx1_norm
    d_head = dot_tn(final_all, dlog_all)
    head_sq = jnp.sum(d_head * d_head)
    dya_b, d_head = lax.optimization_barrier((spread_all(dx1), d_head.astype(bf16)))
    d_attn_b = dot_nn(dya_b, w_out).astype(bf16)
    d_q, d_kv = attn_back(q, d_attn_b, kv_every, qpos, kpos, cosine, sine)
    d_kv = lax.all_to_all(d_kv.reshape(n_ctx, tok, 2 * HD), "ctx", 0, 0, tiled=True)
    d_raw_b = jnp.concatenate([d_q, kv_back(d_kv, cosine, sine)], axis=1)
    d_first = sum_own(dot_nt(d_raw_b, w_attn[:, :ATTN_IN]))
    d_at = outer_pair(a1, d_raw_b, dya_b, attn_b, 128, 2048, "attn_weight_grad")
    if corners:
        core, along_x, along_y = place & 1, (place >> 1) & 1, place >> 2

        def total(kept, sent):
            return kept.astype(f32) + sent.astype(f32)

        def split(x, mine, axis, bit):
            kept = lax.dynamic_index_in_dim(x, mine, axis, keepdims=False)
            return kept, swap(lax.dynamic_index_in_dim(x, 1 - mine, axis, keepdims=False), bit)

        kept, sent = split(d_at.reshape(2, 2, 2, rows, ATTN_IN + QG), core, 2, 1)
        d_first, sent = lax.optimization_barrier((d_first, sent))
        d_pair = total(kept, sent).astype(bf16)
        d_in, d_out = d_pair[..., :ATTN_IN], d_pair[..., ATTN_IN:]
    dx0_norm, d_gain0 = norm_back(d_first, unit0, scale0, gain_rows[0])
    dx0 = dx1 + dx0_norm

    extra = jnp.pad(jnp.stack([d_gain0, d_gain1, d_gain2]), ((0, 13), (0, 0)))
    moved = lax.all_to_all(jnp.concatenate([dx0, extra]).astype(bf16), "ctx", 1, 0, tiled=True)
    if corners:
        moved, d_in, d_out = lax.optimization_barrier((moved, d_in, d_out))
        in_kept, in_sent = split(d_in, along_x, 1, 2)
        out_kept, out_sent = split(d_out, along_y, 0, 4)
        d_in, d_out = total(in_kept, in_sent).astype(bf16), total(out_kept, out_sent).astype(bf16)
        in_kept, in_sent = split(d_in, along_y, 0, 4)
        out_kept, out_sent = split(d_out, along_x, 0, 2)
        d_head, in_sent, out_sent = lax.optimization_barrier((d_head, in_sent, out_sent))
        g_in, g_out = total(in_kept, in_sent), total(out_kept, out_sent)
    else:
        moved, d_head, d_at, g_ff = lax.optimization_barrier((moved, d_head, d_at, g_ff))
        g_at = lax.psum_scatter(d_at, "ctx", scatter_dimension=0, tiled=True).astype(f32)
        g_in, g_out = g_at[:, :ATTN_IN], g_at[:, ATTN_IN:]
    g_head = lax.all_to_all(d_head.reshape(n_ctx, rows, part), "ctx", 0, 0, tiled=True)
    moved = moved.reshape(n_ctx, own + 16, rows)
    gain_part = jnp.sum(moved[:, own:].astype(f32), axis=0).astype(bf16)
    moved = jnp.concatenate([moved[:, :own].reshape(n_ctx * own, rows), gain_part])
    pieces = [moved]
    for s in range(1, n_head):
        pieces.append(lax.ppermute(moved, "head", [(i, (i - s) % n_head) for i in range(n_head)]))
    gain_all = jnp.stack([piece[n_ctx * own :] for piece in pieces + pieces])
    gain_all = lax.dynamic_slice_in_dim(gain_all, n_head - shard, n_head, 0)
    grad_gain = jnp.sum(gain_all.astype(f32), axis=0)[:3].T
    dx0_all = jnp.stack([piece[: n_ctx * own].reshape(n_ctx * SEQS, chunk, rows) for piece in pieces], axis=1)
    g_embed, embed_sq = embed_grad(slots, dx0_all.reshape(n_ctx * tok, rows).T)

    squares = (
        jnp.sum(jnp.square(g_ff.astype(f32)))
        + jnp.sum(jnp.square(g_in))
        + jnp.sum(jnp.square(g_out))
        + head_sq
        + jnp.sum(embed_sq)
        + jnp.sum(grad_gain * grad_gain) / n_head
    )
    squares = jnp.full((8, 128), squares)
    if n_head & (n_head - 1):
        squares = jnp.sum(lax.all_gather(squares, "head"), axis=0)
    else:
        for step in range(n_head.bit_length() - 1):
            squares = squares + lax.ppermute(squares, "head", [(i, i ^ (1 << step)) for i in range(n_head)])
    lane = lax.broadcasted_iota(jnp.int32, (8, 128), 1)
    totals = jnp.sum(lax.all_gather(jnp.where(lane == 0, squares, loss_part), "ctx"), axis=0)
    loss = totals[0, 1]
    grad_norm = jnp.sqrt(totals[0, 0])
    factor = jnp.minimum(1.0, clip_level / grad_norm)

    wide = 32
    spreads = (
        (1, 0, 0, ATTN_IN, D**-0.5),
        (2, 0, ATTN_IN, QG, (length / (4.0 * HEADS * HD)) ** 0.5),
        (0, 0, ATTN_IN + QG, 2 * FFG, D**-0.5),
        (0, 2 * FFG, ATTN_IN + QG + 2 * FFG, FFG, FF**-0.5),
    )
    layer = call_update(
        functools.partial(layer_update_kernel, spreads),
        factor,
        (g_ff, g_in, g_out),
        [
            pl.BlockSpec((wide, g_ff.shape[1]), lambda i: (i, 0)),
            pl.BlockSpec((wide, ATTN_IN), lambda i: (i, 0)),
            pl.BlockSpec((wide, QG), lambda i: (i, 0)),
        ],
        w_layer,
        mom_layer,
        avg_layer,
        wide,
        "layer_update",
    )
    g_head, *layer = lax.optimization_barrier((g_head, *layer))
    vocab = call_update(
        functools.partial(vocab_update_kernel, part),
        factor,
        (g_head, g_embed),
        [
            pl.BlockSpec((n_ctx, wide // 2, part), lambda i: (0, i, 0)),
            pl.BlockSpec((wide // 2, EMB_W), lambda i: (i, 0)),
        ],
        w_vocab,
        mom_vocab,
        avg_vocab,
        wide // 2,
        "vocab_update",
    )
    grad = factor * grad_gain
    gains_moment = momentum_rate * mom_gains + grad
    gains_new = gains - BASE * 0.1 * (grad + momentum_rate * gains_moment)
    gains_average = average_rate * avg_gains + (1.0 - average_rate) * gains_new
    return (
        *layer,
        *vocab,
        gains_new,
        gains_moment,
        gains_average,
        gains_new.astype(bf16),
        loss,
        grad_norm,
    )


def solution(mesh):
    token, split, gain = P("ctx"), P("ctx", "head"), P("ctx", None)
    in_specs = (token, token, token, P()) + (split, split, gain) * 3
    out_specs = (split,) * 8 + (gain,) * 4 + (P(), P())
    return jax.shard_map(local, mesh=mesh, in_specs=in_specs, out_specs=out_specs, check_vma=False)
```

```python
import functools
import math

import jax
import jax.numpy as jnp
import numpy as np
from jax import lax
from jax.experimental import pallas as pl
from jax.experimental.pallas import tpu as pltpu
from jax.sharding import PartitionSpec as P

D = 2048
HEADS = 32
KV = 4
HD = 64
FF = 5632
V = 32000
SEQS = 2

eps = 1e-05
z_weight = 0.0001
momentum_rate = 0.5
average_rate = 0.5
clip_level = 0.01

GROUP = HEADS // KV
QG = GROUP * HD
FFG = FF // KV
VG = V // KV
ATTN_IN = QG + 2 * HD
NPARAM = D * (2 * HEADS * HD + 2 * KV * HD + 3 * FF + 2 * V + 3)
BASE = 1.5 * math.sqrt(NPARAM) / clip_level
EMB_AT = VG // 128 * 128
EMB_W = 2 * VG - EMB_AT
EMB_STEPS = 7
EMB_BLOCK = EMB_W // EMB_STEPS

f32 = jnp.float32
bf16 = jnp.bfloat16
NEG = -1e30


def dot_nn(a, b):
    return lax.dot_general(a, b, (((1,), (0,)), ((), ())), preferred_element_type=f32)


def dot_nt(a, b):
    return lax.dot_general(a, b, (((1,), (1,)), ((), ())), preferred_element_type=f32)


def dot_tn(a, b):
    return lax.dot_general(a, b, (((0,), (0,)), ((), ())), preferred_element_type=f32)


def cost(flops, nbytes, trans=0):
    return pl.CostEstimate(flops=int(flops), bytes_accessed=int(nbytes), transcendentals=int(trans))


def params(**kw):
    return pltpu.CompilerParams(vmem_limit_bytes=56 * 1024 * 1024, **kw)


def one_hot(ids, base, width):
    column = lax.broadcasted_iota(jnp.int32, (ids.shape[0], width), 1) + base
    return jnp.where(ids == column, jnp.float32(1.0), jnp.float32(0.0)).astype(bf16)


def lookup_kernel(rows, ids_ref, w_ref, out_ref, acc_ref):
    step = pl.program_id(0)
    w = w_ref[...].astype(bf16)
    total = ids_ref.shape[0]

    @pl.when(step == 0)
    def _():
        acc_ref[...] = jnp.zeros_like(acc_ref)

    for r in range(0, total, rows):
        part = pl.ds(r, rows)
        acc_ref[part, :] += dot_nt(one_hot(ids_ref[part, :], step * EMB_BLOCK, EMB_BLOCK), w)

    @pl.when(step == EMB_STEPS - 1)
    def _():
        out_ref[...] = acc_ref[...].astype(bf16)


def lookup(ids, w_vocab):
    total, rows = ids.shape[0], w_vocab.shape[0]
    return pl.pallas_call(
        functools.partial(lookup_kernel, min(512, total)),
        grid=(EMB_STEPS,),
        in_specs=[
            pl.BlockSpec((total, 1), lambda i: (0, 0)),
            pl.BlockSpec((pl.Element(rows), pl.Element(EMB_BLOCK)), lambda i: (0, (EMB_AT // 128 + EMB_BLOCK // 128 * i) * 128)),
        ],
        out_specs=pl.BlockSpec((total, rows), lambda i: (0, 0)),
        out_shape=jax.ShapeDtypeStruct((total, rows), bf16),
        scratch_shapes=[pltpu.VMEM((total, rows), f32)],
        compiler_params=params(),
        cost_estimate=cost(2 * total * rows * EMB_W, rows * EMB_W * 4),
        name="embed_lookup",
    )(ids, w_vocab)


def embed_grad_kernel(rows, ids_ref, dxt_ref, out_ref, sq_ref):
    step = pl.program_id(0)
    total = ids_ref.shape[0]
    acc = jnp.zeros(out_ref.shape, f32)
    for r in range(0, total, rows):
        hot = one_hot(ids_ref[pl.ds(r, rows), :], step * EMB_BLOCK, EMB_BLOCK)
        acc = acc + dot_nn(dxt_ref[:, pl.ds(r, rows)], hot)
    out_ref[...] = acc.astype(bf16)
    square = acc * acc
    lanes = sum(square[:, k : k + 128] for k in range(0, EMB_BLOCK, 128))
    part = sum(lanes[k : k + 8] for k in range(0, lanes.shape[0], 8))

    @pl.when(step == 0)
    def _():
        sq_ref[...] = jnp.zeros_like(sq_ref)

    sq_ref[...] += part


def embed_grad(ids, dxt):
    rows, total = dxt.shape
    return pl.pallas_call(
        functools.partial(embed_grad_kernel, min(512, total)),
        grid=(EMB_STEPS,),
        in_specs=[
            pl.BlockSpec((total, 1), lambda i: (0, 0)),
            pl.BlockSpec((rows, total), lambda i: (0, 0)),
        ],
        out_specs=[
            pl.BlockSpec((rows, EMB_BLOCK), lambda i: (0, i)),
            pl.BlockSpec((8, 128), lambda i: (0, 0)),
        ],
        out_shape=[
            jax.ShapeDtypeStruct((rows, EMB_W), bf16),
            jax.ShapeDtypeStruct((8, 128), f32),
        ],
        compiler_params=params(),
        cost_estimate=cost(2 * total * rows * EMB_W, rows * EMB_W * 2),
        name="embed_grad",
    )(ids, dxt)


def partner(x):
    width = x.shape[1]
    lane = lax.broadcasted_iota(jnp.int32, x.shape, 1)
    return jnp.where(lane % HD < HD // 2, pltpu.roll(x, width - HD // 2, 1), pltpu.roll(x, HD // 2, 1))


def qkv_kernel(a_ref, w_ref, cos_ref, sin_ref, q_ref, kv_ref):
    raw = dot_nn(a_ref[...], w_ref[...])
    cosine, sine = cos_ref[...], sin_ref[...]
    for j in range(0, QG, 128):
        x = raw[:, j : j + 128]
        rot = (x * cosine + partner(x) * sine).astype(bf16)
        q_ref[:, j : j + 128] = rot * jnp.asarray(HD**-0.5, bf16)
    x = raw[:, QG:]
    lane = lax.broadcasted_iota(jnp.int32, x.shape, 1)
    kv_ref[...] = jnp.where(lane < HD, x * cosine + partner(x) * sine, x).astype(bf16)


def qkv(a1, w_in, cosine, sine):
    tok = a1.shape[0]
    return pl.pallas_call(
        qkv_kernel,
        grid=(1,),
        in_specs=[
            pl.BlockSpec((tok, D), lambda i: (0, 0)),
            pl.BlockSpec((D, ATTN_IN), lambda i: (0, 0)),
            pl.BlockSpec((tok, 128), lambda i: (0, 0)),
            pl.BlockSpec((tok, 128), lambda i: (0, 0)),
        ],
        out_specs=[
            pl.BlockSpec((tok, QG), lambda i: (0, 0)),
            pl.BlockSpec((tok, 2 * HD), lambda i: (0, 0)),
        ],
        out_shape=[
            jax.ShapeDtypeStruct((tok, QG), bf16),
            jax.ShapeDtypeStruct((tok, 2 * HD), bf16),
        ],
        compiler_params=params(),
        cost_estimate=cost(2 * tok * D * ATTN_IN, 2 * D * ATTN_IN + 2 * tok * D),
        name="qkv",
    )(a1, w_in, cosine, sine)


def split_kv(kv_ref, parts_ref):
    kv = kv_ref[...].reshape(-1, 2 * HD).astype(f32)
    lane = lax.broadcasted_iota(jnp.int32, kv.shape, 1)
    swapped = pltpu.roll(kv, HD, 1)
    zero = jnp.zeros_like(kv)
    low = lane < HD
    parts_ref[0] = jnp.where(low, kv, zero).astype(bf16)
    parts_ref[1] = jnp.where(low, zero, swapped).astype(bf16)
    parts_ref[2] = jnp.where(low, swapped, zero).astype(bf16)
    parts_ref[3] = jnp.where(low, zero, kv).astype(bf16)


def attn_kernel(q_ref, kv_ref, qpos_ref, kpos_ref, o_ref, parts_ref):
    @pl.when(pl.program_id(1) == 0)
    def _():
        split_kv(kv_ref, parts_ref)

    q = q_ref[...]
    allowed = kpos_ref[...] <= qpos_ref[...]
    out = None
    for g in range(2):
        s = jnp.where(allowed, dot_nt(q, parts_ref[g]), NEG)
        p = jnp.exp(s - jnp.max(s, axis=1, keepdims=True))
        p = p * (1.0 / jnp.sum(p, axis=1, keepdims=True))
        part = dot_nn(p.astype(bf16), parts_ref[2 + g])
        out = part if out is None else out + part
    o_ref[...] = out.astype(bf16)


def attn(q, kv_every, qpos, kpos):
    n_ctx, _, seq_tok, _ = kv_every.shape
    keys = n_ctx * seq_tok
    pairs = QG // 128
    return pl.pallas_call(
        attn_kernel,
        grid=(SEQS, pairs),
        in_specs=[
            pl.BlockSpec((seq_tok, 128), lambda s, p: (s, p)),
            pl.BlockSpec((n_ctx, 1, seq_tok, 2 * HD), lambda s, p: (0, s, 0, 0)),
            pl.BlockSpec((seq_tok, 1), lambda s, p: (0, 0)),
            pl.BlockSpec((1, keys), lambda s, p: (0, 0)),
        ],
        out_specs=pl.BlockSpec((seq_tok, 128), lambda s, p: (s, p)),
        out_shape=jax.ShapeDtypeStruct((SEQS * seq_tok, QG), bf16),
        scratch_shapes=[pltpu.VMEM((4, keys, 2 * HD), bf16)],
        compiler_params=params(),
        cost_estimate=cost(
            8 * SEQS * seq_tok * keys * QG, 4 * SEQS * seq_tok * QG, SEQS * GROUP * seq_tok * keys
        ),
        name="attn_fwd",
    )(q, kv_every, qpos.reshape(seq_tok, 1), kpos.reshape(1, keys))


def attn_back_kernel(
    pairs, q_ref, do_ref, kv_ref, qpos_ref, kpos_ref, cos_ref, sin_ref, dq_ref, dkv_ref, parts_ref, acc_ref
):
    pair = pl.program_id(1)

    @pl.when(pair == 0)
    def _():
        split_kv(kv_ref, parts_ref)
        acc_ref[...] = jnp.zeros_like(acc_ref)

    q = q_ref[...]
    do = do_ref[...]
    allowed = kpos_ref[...] <= qpos_ref[...]
    dq = None
    for g in range(2):
        s = jnp.where(allowed, dot_nt(parts_ref[g], q), NEG)
        p = jnp.exp(s - jnp.max(s, axis=0, keepdims=True))
        p = p * (1.0 / jnp.sum(p, axis=0, keepdims=True))
        dp = dot_nt(parts_ref[2 + g], do)
        delta = jnp.sum(p * dp, axis=0, keepdims=True)
        ds = (p * (dp - delta)).astype(bf16)
        part = dot_tn(ds, parts_ref[g])
        dq = part if dq is None else dq + part
        acc_ref[g] += dot_nn(ds, q)
        acc_ref[2 + g] += dot_nn(p.astype(bf16), do)
    dq = dq * (HD**-0.5)
    dq_ref[...] = (dq * cos_ref[...] - partner(dq) * sin_ref[...]).astype(bf16)

    @pl.when(pair == pairs - 1)
    def _():
        lane = lax.broadcasted_iota(jnp.int32, acc_ref.shape[1:], 1)
        grad_k = acc_ref[0] + pltpu.roll(acc_ref[1], HD, 1)
        grad_v = pltpu.roll(acc_ref[2], HD, 1) + acc_ref[3]
        dkv_ref[...] = jnp.where(lane < HD, grad_k, grad_v).astype(bf16).reshape(dkv_ref.shape)


def attn_back(q, do, kv_every, qpos, kpos, cosine, sine):
    n_ctx, _, seq_tok, _ = kv_every.shape
    keys = n_ctx * seq_tok
    pairs = QG // 128
    return pl.pallas_call(
        functools.partial(attn_back_kernel, pairs),
        grid=(SEQS, pairs),
        in_specs=[
            pl.BlockSpec((seq_tok, 128), lambda s, p: (s, p)),
            pl.BlockSpec((seq_tok, 128), lambda s, p: (s, p)),
            pl.BlockSpec((n_ctx, 1, seq_tok, 2 * HD), lambda s, p: (0, s, 0, 0)),
            pl.BlockSpec((1, seq_tok), lambda s, p: (0, 0)),
            pl.BlockSpec((keys, 1), lambda s, p: (0, 0)),
            pl.BlockSpec((seq_tok, 128), lambda s, p: (s, 0)),
            pl.BlockSpec((seq_tok, 128), lambda s, p: (s, 0)),
        ],
        out_specs=[
            pl.BlockSpec((seq_tok, 128), lambda s, p: (s, p)),
            pl.BlockSpec((n_ctx, 1, seq_tok, 2 * HD), lambda s, p: (0, s, 0, 0)),
        ],
        out_shape=[
            jax.ShapeDtypeStruct((SEQS * seq_tok, QG), bf16),
            jax.ShapeDtypeStruct(kv_every.shape, bf16),
        ],
        scratch_shapes=[
            pltpu.VMEM((4, keys, 2 * HD), bf16),
            pltpu.VMEM((4, keys, 2 * HD), f32),
        ],
        compiler_params=params(),
        cost_estimate=cost(
            20 * SEQS * seq_tok * keys * QG, 8 * SEQS * seq_tok * QG, SEQS * GROUP * seq_tok * keys
        ),
        name="attn_bwd",
    )(q, do, kv_every, qpos.reshape(1, seq_tok), kpos.reshape(keys, 1), cosine, sine)


def kv_back_kernel(parts_ref, cos_ref, sin_ref, out_ref):
    x = parts_ref[0].astype(f32)
    for k in range(1, parts_ref.shape[0]):
        x = x + parts_ref[k].astype(f32)
    lane = lax.broadcasted_iota(jnp.int32, x.shape, 1)
    out_ref[...] = jnp.where(lane < HD, x * cos_ref[...] - partner(x) * sin_ref[...], x).astype(bf16)


def kv_back(parts, cosine, sine):
    return pl.pallas_call(
        kv_back_kernel,
        out_shape=jax.ShapeDtypeStruct(parts.shape[1:], bf16),
        compiler_params=params(),
        name="kv_bwd",
    )(parts, cosine, sine)


def head_cast_kernel(block, w_ref, *outs):
    column = lax.broadcasted_iota(jnp.int32, w_ref.shape, 1) + pl.program_id(0) * block
    w = jnp.where(column < VG, w_ref[...], 0.0).astype(bf16)
    count = w.shape[0] // len(outs)
    for k, out_ref in enumerate(outs):
        out_ref[...] = w[k * count : (k + 1) * count]


def head_cast(w_vocab, width, parts):
    rows = w_vocab.shape[0]
    block = 1024
    return pl.pallas_call(
        functools.partial(head_cast_kernel, block),
        grid=(width // block,),
        in_specs=[pl.BlockSpec((rows, block), lambda i: (0, i))],
        out_specs=[pl.BlockSpec((rows // parts, block), lambda i: (0, i))] * parts,
        out_shape=[jax.ShapeDtypeStruct((rows // parts, width), bf16)] * parts,
        compiler_params=params(),
        cost_estimate=cost(rows * width, rows * width * 6),
        name="head_cast",
    )(w_vocab)


def joined(pieces, parts):
    for k in range(0, len(pieces), parts):
        run = [piece[...] for piece in pieces[k : k + parts]]
        yield k // parts, run[0] if parts == 1 else jnp.concatenate(run, axis=0)


def partial_kernel(parts, at_ref, x_ref, *refs):
    pieces, out_ref = refs[:-1], refs[-1]
    logits = None
    for k, w in joined(pieces, parts):
        at = pl.multiple_of(at_ref[k], 128)
        term = dot_nn(x_ref[:, pl.ds(at, w.shape[0])], w)
        logits = term if logits is None else logits + term
    out_ref[...] = logits


def head_partial(x, pieces, at):
    tok = x.shape[0]
    width = pieces[0].shape[1]
    rows = sum(piece.shape[0] for piece in pieces)
    block = 1024
    return pl.pallas_call(
        functools.partial(partial_kernel, len(pieces) // at.shape[0]),
        grid=(width // block,),
        in_specs=[
            pl.BlockSpec(memory_space=pltpu.SMEM),
            pl.BlockSpec((tok, D), lambda i: (0, 0)),
        ]
        + [pl.BlockSpec((piece.shape[0], block), lambda i: (0, i)) for piece in pieces],
        out_specs=pl.BlockSpec((tok, block), lambda i: (0, i)),
        out_shape=jax.ShapeDtypeStruct((tok, width), f32),
        compiler_params=params(),
        cost_estimate=cost(2 * tok * rows * width, 2 * rows * width + 4 * tok * width),
        name="head_partial",
    )(at, x, *pieces)


def logits_kernel(steps, parts, based, at_ref, x_ref, slot_ref, *refs):
    base = refs[:based]
    pieces, (out_ref, stats_ref, top_ref, total_ref, label_ref) = refs[based:-5], refs[-5:]
    step = pl.program_id(0)
    block = out_ref.shape[1]

    @pl.when(step == 0)
    def _():
        top_ref[...] = jnp.full_like(top_ref, NEG)
        total_ref[...] = jnp.zeros_like(total_ref)
        label_ref[...] = jnp.zeros_like(label_ref)

    logits = base[0][...] if based else None
    for k, w in joined(pieces, parts):
        at = pl.multiple_of(at_ref[k], 128)
        term = dot_nn(x_ref[:, pl.ds(at, w.shape[0])], w)
        logits = term if logits is None else logits + term
    column = lax.broadcasted_iota(jnp.int32, logits.shape, 1) + step * block
    logits = jnp.where(column < VG, logits, NEG)
    out_ref[...] = logits
    top = top_ref[...]
    new_top = jnp.maximum(top, jnp.max(logits, axis=1, keepdims=True))
    total_ref[...] = total_ref[...] * jnp.exp(top - new_top) + jnp.sum(
        jnp.exp(logits - new_top), axis=1, keepdims=True
    )
    top_ref[...] = new_top
    label_ref[...] += jnp.sum(jnp.where(column == slot_ref[...], logits, 0.0), axis=1, keepdims=True)

    @pl.when(step == steps - 1)
    def _():
        lane = lax.broadcasted_iota(jnp.int32, (x_ref.shape[0], 128), 1)
        packed = jnp.where(lane == 0, top_ref[...], jnp.where(lane == 1, total_ref[...], label_ref[...]))
        stats_ref[...] = packed.T[:8]


def head_logits(x, slots, base, pieces, at):
    tok = x.shape[0]
    rows = sum(piece.shape[0] for piece in pieces)
    width = pieces[0].shape[1]
    block = 1024
    steps = width // block
    return pl.pallas_call(
        functools.partial(logits_kernel, steps, len(pieces) // at.shape[0], len(base)),
        grid=(steps,),
        in_specs=[
            pl.BlockSpec(memory_space=pltpu.SMEM),
            pl.BlockSpec((tok, D), lambda i: (0, 0)),
            pl.BlockSpec((tok, 1), lambda i: (0, 0)),
        ]
        + [pl.BlockSpec((tok, block), lambda i: (0, i)) for _ in base]
        + [pl.BlockSpec((piece.shape[0], block), lambda i: (0, i)) for piece in pieces],
        out_specs=[
            pl.BlockSpec((tok, block), lambda i: (0, i)),
            pl.BlockSpec((8, tok), lambda i: (0, 0)),
        ],
        out_shape=[
            jax.ShapeDtypeStruct((tok, width), f32),
            jax.ShapeDtypeStruct((8, tok), f32),
        ],
        scratch_shapes=[pltpu.VMEM((tok, 1), f32)] * 3,
        compiler_params=params(),
        cost_estimate=cost(2 * tok * rows * width, 2 * rows * width + 8 * tok * width, tok * width),
        name="head_logits",
    )(at, x, slots, *base, *pieces)


def dlogits_kernel(steps, parts, at_ref, logits_ref, values_ref, slot_ref, *refs):
    pieces, (dlog_ref, dx_ref, acc_ref) = refs[:-3], refs[-3:]
    step = pl.program_id(0)
    tok, block = logits_ref.shape
    logits = logits_ref[...]
    lse = values_ref[:, 0:1]
    weight = values_ref[:, 1:2]
    column = lax.broadcasted_iota(jnp.int32, logits.shape, 1) + step * block
    hit = jnp.where(column == slot_ref[...], 1.0, 0.0)
    soft = jnp.exp(logits - lse)
    dlog = (weight * ((1.0 + 2.0 * z_weight * lse) * soft - hit)).astype(bf16)
    part = dlog_ref.shape[2]
    for k in range(dlog_ref.shape[0]):
        dlog_ref[k] = dlog[:, k * part : (k + 1) * part]

    @pl.when(step == 0)
    def _():
        acc_ref[...] = jnp.zeros_like(acc_ref)

    for k, w in joined(pieces, parts):
        at = pl.multiple_of(at_ref[k], 128)
        acc_ref[:, pl.ds(at, w.shape[0])] += dot_nt(dlog, w)

    @pl.when(step == steps - 1)
    def _():
        dx_ref[...] = acc_ref[...].astype(bf16)


def head_dlogits(logits, values, slots, pieces, at, part):
    tok, width = logits.shape
    block = 1024
    steps = width // block
    return pl.pallas_call(
        functools.partial(dlogits_kernel, steps, len(pieces) // at.shape[0]),
        grid=(steps,),
        in_specs=[
            pl.BlockSpec(memory_space=pltpu.SMEM),
            pl.BlockSpec((tok, block), lambda i: (0, i)),
            pl.BlockSpec((tok, values.shape[1]), lambda i: (0, 0)),
            pl.BlockSpec((tok, 1), lambda i: (0, 0)),
        ]
        + [pl.BlockSpec((piece.shape[0], block), lambda i: (0, i)) for piece in pieces],
        out_specs=[
            pl.BlockSpec((block // part, tok, part), lambda i: (i, 0, 0)),
            pl.BlockSpec((tok, D), lambda i: (0, 0)),
        ],
        out_shape=[
            jax.ShapeDtypeStruct((width // part, tok, part), bf16),
            jax.ShapeDtypeStruct((tok, D), bf16),
        ],
        scratch_shapes=[pltpu.VMEM((tok, D), f32)],
        compiler_params=params(),
        cost_estimate=cost(2 * tok * D * width, 2 * D * width + 6 * tok * width, tok * width),
        name="head_dlogits",
    )(at, logits, values, slots, *pieces)


def outer_kernel(a_ref, da_ref, b_ref, db_ref, out_ref, *, a_steps):
    step = pl.program_id(0)

    @pl.when(step < a_steps)
    def _():
        out_ref[...] = dot_tn(a_ref[...], da_ref[...]).astype(bf16)

    @pl.when(step >= a_steps)
    def _():
        out_ref[...] = dot_tn(b_ref[...], db_ref[...]).astype(bf16)


def outer_pair(a, da, b, db, block, rows, name):
    tok = a.shape[0]
    a_steps, b_steps = da.shape[1] // block, db.shape[1] // block
    width = da.shape[1] + db.shape[1]
    return pl.pallas_call(
        functools.partial(outer_kernel, a_steps=a_steps),
        grid=(a_steps + b_steps, D // rows),
        in_specs=[
            pl.BlockSpec((tok, rows), lambda i, j: (0, j)),
            pl.BlockSpec((tok, block), lambda i, j: (0, jnp.minimum(i, a_steps - 1))),
            pl.BlockSpec((tok, rows), lambda i, j: (0, j)),
            pl.BlockSpec((tok, block), lambda i, j: (0, jnp.maximum(i - a_steps, 0))),
        ],
        out_specs=pl.BlockSpec((rows, block), lambda i, j: (j, i)),
        out_shape=jax.ShapeDtypeStruct((D, width), bf16),
        compiler_params=params(),
        cost_estimate=cost(2 * tok * D * width, 2 * D * width + 4 * tok * D),
        name=name,
    )(a, da, b, db)


def update_piece(factor, rate, grad, w_ref, m_ref, a_ref, outs, columns):
    new_ref, moment_ref, average_ref, copy_ref = outs
    grad = factor * grad
    moment = momentum_rate * m_ref[:, columns] + grad
    new = w_ref[:, columns] - rate * (grad + momentum_rate * moment)
    new_ref[:, columns] = new
    moment_ref[:, columns] = moment
    average_ref[:, columns] = average_rate * a_ref[:, columns] + (1.0 - average_rate) * new
    copy_ref[:, columns] = new.astype(bf16)


def layer_update_kernel(spreads, factor_ref, *refs):
    grads, (w_ref, m_ref, a_ref), outs = refs[:-7], refs[-7:-4], refs[-4:]
    factor = factor_ref[0, 0]
    for source, inner, outer, width, spread in spreads:
        grad = grads[source][:, inner : inner + width].astype(f32)
        update_piece(factor, BASE * spread, grad, w_ref, m_ref, a_ref, outs, slice(outer, outer + width))


def vocab_update_kernel(part, factor_ref, head_ref, embed_ref, w_ref, m_ref, a_ref, *outs):
    factor = factor_ref[0, 0]
    head_rate = BASE * 2.0 * D**-0.5
    for k in range(head_ref.shape[0]):
        low, high = k * part, min((k + 1) * part, EMB_AT)
        if low >= high:
            continue
        grad = head_ref[k, :, : high - low].astype(f32)
        update_piece(factor, head_rate, grad, w_ref, m_ref, a_ref, outs, slice(low, high))
    edge = EMB_AT - EMB_AT // part * part
    grad_head = head_ref[EMB_AT // part, :, edge : edge + 128].astype(f32)
    grad_embed = embed_ref[:, :128].astype(f32)
    own = lax.broadcasted_iota(jnp.int32, grad_head.shape, 1) < VG - EMB_AT
    update_piece(
        factor,
        jnp.where(own, head_rate, BASE),
        jnp.where(own, grad_head, grad_embed),
        w_ref,
        m_ref,
        a_ref,
        outs,
        slice(EMB_AT, EMB_AT + 128),
    )
    for low in range(128, EMB_W, 1024):
        high = min(low + 1024, EMB_W)
        grad = embed_ref[:, low:high].astype(f32)
        update_piece(factor, BASE, grad, w_ref, m_ref, a_ref, outs, slice(EMB_AT + low, EMB_AT + high))


def call_update(kernel, factor, grads, grad_specs, w, m, a, rows, name):
    total, width = w.shape
    block = pl.BlockSpec((rows, width), lambda i: (i, 0))
    return pl.pallas_call(
        kernel,
        grid=(total // rows,),
        in_specs=[pl.BlockSpec(memory_space=pltpu.SMEM)] + grad_specs + [block] * 3,
        out_specs=[block] * 4,
        out_shape=[jax.ShapeDtypeStruct(w.shape, f32)] * 3 + [jax.ShapeDtypeStruct(w.shape, bf16)],
        compiler_params=params(),
        cost_estimate=cost(10 * total * width, 28 * total * width),
        name=name,
    )(factor.reshape(1, 1), *grads, w, m, a)


def norm_parts(x):
    scale = lax.rsqrt(jnp.mean(x * x, axis=-1, keepdims=True) + eps)
    return x * scale, scale


def norm_back(dy, unit, scale, gain):
    scaled = dy * gain
    dx = scale * (scaled - unit * jnp.mean(scaled * unit, axis=-1, keepdims=True))
    return dx, jnp.sum(dy * unit, axis=0)


def local(
    token_ids,
    labels,
    answer_mask,
    pair_map,
    w_layer,
    w_vocab,
    gains,
    mom_layer,
    mom_vocab,
    mom_gains,
    avg_layer,
    avg_vocab,
    avg_gains,
):
    n_ctx = lax.axis_size("ctx")
    n_head = lax.axis_size("head")
    place = lax.axis_index("ctx")
    shard = lax.axis_index("head")
    tok = token_ids.shape[0]
    rows = w_layer.shape[0]
    seq_tok = tok // SEQS
    span = seq_tok // 2
    chunk = seq_tok // n_head
    own = SEQS * chunk
    length = n_ctx * seq_tok
    part = -(-VG // (n_ctx * 128)) * 128

    def turn(x, axis):
        return lax.dynamic_slice_in_dim(
            jnp.concatenate([x, x], axis), shard * chunk, seq_tok, axis
        )

    def turn_back(x, axis):
        return lax.dynamic_slice_in_dim(
            jnp.concatenate([x, x], axis), seq_tok - shard * chunk, seq_tok, axis
        )

    def head_scatter(x):
        sums = x[:, 0].astype(f32)
        for s in range(1, n_head):
            sent = lax.ppermute(x[:, s], "head", [(i, (i + s) % n_head) for i in range(n_head)])
            sums = sums + sent.astype(f32)
        return sums

    def head_gather(x):
        pieces = [x]
        for s in range(1, n_head):
            pieces.append(lax.ppermute(x, "head", [(i, (i - s) % n_head) for i in range(n_head)]))
        return jnp.stack(pieces, axis=1)

    def sum_own(partial):
        split = partial.astype(bf16).reshape(SEQS, n_head, chunk, D)
        return head_scatter(split).reshape(own, D)

    def spread_all(x):
        return head_gather(x.astype(bf16).reshape(SEQS, chunk, D)).reshape(tok, D)

    layer_b = w_layer.astype(bf16)
    edge = ATTN_IN + QG
    w_attn = lax.all_gather(layer_b[:, :edge], "ctx", axis=0, tiled=True)
    w_ff = lax.all_gather(layer_b[:, edge:], "ctx", axis=0, tiled=True)
    w_out, w_gu, w_down = w_attn[:, ATTN_IN:], w_ff[:, : 2 * FFG], w_ff[:, 2 * FFG :]
    corners = n_ctx == 8
    head_own = head_cast(w_vocab, n_ctx * part, 2 if corners else 1)

    def swap(x, bit):
        return lax.ppermute(x, "ctx", [(i, i ^ bit) for i in range(n_ctx)])

    gain_own = lax.reduce_precision(gains, exponent_bits=8, mantissa_bits=7).T.reshape(3 * rows)
    every = jnp.concatenate([token_ids.astype(f32), answer_mask.astype(f32), gain_own])
    every = lax.all_gather(every, "ctx")
    ids_all = every[:, :tok].astype(jnp.int32).reshape(n_ctx, SEQS, seq_tok)
    ids_all = turn(ids_all, 2).reshape(n_ctx * tok)
    count = jnp.sum(every[:, tok : 2 * tok])
    gain_rows = jnp.moveaxis(every[:, 2 * tok :].reshape(n_ctx, 3, rows), 1, 0).reshape(3, D)
    labels_own = turn(labels.reshape(SEQS, seq_tok), 1).reshape(tok)
    mask_own = turn(answer_mask.reshape(SEQS, seq_tok), 1).reshape(tok)

    offset_id = shard * VG
    local_ids = ids_all - offset_id
    inside = (local_ids >= 0) & (local_ids < VG)
    slots = jnp.where(inside, local_ids + (VG - EMB_AT), -1).reshape(-1, 1)
    picked = lookup(slots, w_vocab).reshape(n_ctx * SEQS, n_head, chunk, rows)
    picked = head_scatter(picked).astype(bf16).reshape(n_ctx * own, rows)
    x0 = lax.all_to_all(picked, "ctx", 0, 1, tiled=True).astype(f32)

    unit0, scale0 = norm_parts(x0)
    a1 = spread_all(unit0 * gain_rows[0])
    if corners:
        over = [swap(x, 1) for x in head_own]
        a1, low, high, over_low, over_high = lax.optimization_barrier((a1, *head_own, *over))
    row = (jnp.arange(seq_tok, dtype=jnp.int32) + shard * chunk) % seq_tok

    def positions(index):
        index = index[:, None]
        at = jnp.where(row // span == 0, index, 2 * n_ctx - 1 - index)
        return at * span + row % span

    qpos = positions(pair_map[place][None])[0]
    kpos = positions(pair_map).reshape(length)
    half = HD // 2
    inverse = 10000.0 ** (-2.0 * np.arange(half) / HD)
    ramp = np.clip((2048.0 * inverse / (2.0 * math.pi) - 1.0) / 31.0, 0.0, 1.0)
    freq = np.tile(((1.0 - ramp) * inverse / 4.0 + ramp * inverse).astype(np.float32), 128 // half)
    sign = np.where(np.arange(128) % HD < half, -1.0, 1.0).astype(np.float32)
    mscale = 0.1 * math.log(4.0) + 1.0
    angle = jnp.tile(qpos, SEQS).astype(f32)[:, None] * freq[None, :]
    cosine = jnp.cos(angle) * mscale
    sine = jnp.sin(angle) * (mscale * sign)[None, :]
    q, kv_own = qkv(a1, w_attn, cosine, sine)
    kv_every = lax.all_gather(kv_own, "ctx").reshape(n_ctx, SEQS, seq_tok, 2 * HD)
    if corners:
        kv_every, low, high = lax.optimization_barrier((kv_every, low, high))
        y_low, x_high, x_low, y_high = swap(low, 4), swap(high, 2), swap(low, 2), swap(high, 4)
    attn_b = attn(q, kv_every, qpos, kpos)
    x1 = x0 + sum_own(dot_nt(attn_b, w_out))

    unit1, scale1 = norm_parts(x1)
    a2 = spread_all(unit1 * gain_rows[1])
    if corners:
        a2, y_low, x_high = lax.optimization_barrier((a2, y_low, x_high))
        far_low, far_high = swap(y_low, 2), swap(x_high, 4)
    gate_up = dot_nn(a2, w_gu)

    def glu(values):
        return jax.nn.silu(values[:, :FFG]) * values[:, FFG:]

    hidden_f, glu_back = jax.vjp(glu, gate_up)
    hidden_b = hidden_f.astype(bf16)
    second = sum_own(dot_nt(hidden_b, w_down))
    if corners:
        second, x_low, y_high = lax.optimization_barrier((second, x_low, y_high))
    x2 = x1 + second

    unit2, scale2 = norm_parts(x2)
    final_b = spread_all(unit2 * gain_rows[2])
    label_ids = labels_own - offset_id
    label_slots = jnp.where((label_ids >= 0) & (label_ids < VG), label_ids, -1).reshape(tok, 1)
    if corners:
        near = [low, high, over_low, over_high, x_low, x_high, y_low, y_high]
        head_at = jnp.stack([(place ^ bits) * rows for bits in (0, 1, 2, 4, 3, 5, 6, 7)])
        base = head_partial(final_b, near, head_at[:4])
        base, far_low, far_high = lax.optimization_barrier((base, far_low, far_high))
        far = [swap(x, 1) for x in (x_low, x_high, y_low, y_high)]
        far += [far_low, far_high, swap(far_low, 1), swap(far_high, 1)]
        head_pieces = near + far
        logits, stats = head_logits(final_b, label_slots, [base], far, head_at[4:])
    else:
        head_pieces = [lax.all_gather(head_own[0], "ctx", axis=0, tiled=True)]
        head_at = jnp.zeros((1,), jnp.int32)
        logits, stats = head_logits(final_b, label_slots, [], head_pieces, head_at)
    stats, final_late = lax.optimization_barrier((stats, final_b))
    pieces = [stats]
    for s in range(1, n_head):
        sent = lax.ppermute(stats, "head", [(i, (i - s) % n_head) for i in range(n_head)])
        sent = sent.reshape(8, SEQS, n_head, chunk)
        pieces.append(jnp.roll(sent, s, axis=2).reshape(8, tok))
    doubled = jnp.stack(pieces + pieces)
    stats = lax.dynamic_slice_in_dim(doubled, n_head - shard, n_head, 0)
    top = jnp.max(stats[:, 0], axis=0)
    total = jnp.sum(stats[:, 1] * jnp.exp(stats[:, 0] - top), axis=0)
    lse = top + jnp.log(total)
    weight = mask_own.astype(f32) / count
    terms = weight * (lse - jnp.sum(stats[:, 2], axis=0) + z_weight * lse * lse)
    loss_part = jnp.sum(turn_back(terms.reshape(SEQS, seq_tok), 1))
    values = jnp.stack([lse, weight] + [weight] * 6).T
    dlog_b, d_final = head_dlogits(logits, values, label_slots, head_pieces, head_at, part)
    final_all = lax.all_gather(final_late, "ctx", axis=0, tiled=True)
    dlog_all = lax.all_to_all(dlog_b, "ctx", 0, 0, tiled=True).reshape(n_ctx * tok, part)

    dx2, d_gain2 = norm_back(sum_own(d_final), unit2, scale2, gain_rows[2])
    dyf_b = spread_all(dx2)
    d_hidden = dot_nn(dyf_b, w_down)
    d_gate_up_b = glu_back(d_hidden)[0].astype(bf16)
    d_second = sum_own(dot_nt(d_gate_up_b, w_gu))
    d_ff = outer_pair(a2, d_gate_up_b, dyf_b, hidden_b, FFG, 512, "ff_weight_grad")
    d_second, d_ff, dlog_all, final_all = lax.optimization_barrier((d_second, d_ff, dlog_all, final_all))
    g_ff = lax.psum_scatter(d_ff, "ctx", scatter_dimension=0, tiled=True)
    dx1_norm, d_gain1 = norm_back(d_second, unit1, scale1, gain_rows[1])
    dx1 = dx2 + dx1_norm
    d_head = dot_tn(final_all, dlog_all)
    head_sq = jnp.sum(d_head * d_head)
    dya_b, d_head = lax.optimization_barrier((spread_all(dx1), d_head.astype(bf16)))
    d_attn_b = dot_nn(dya_b, w_out).astype(bf16)
    d_q, d_kv = attn_back(q, d_attn_b, kv_every, qpos, kpos, cosine, sine)
    d_out = dot_tn(dya_b, attn_b).astype(bf16)
    d_kv = lax.all_to_all(d_kv.reshape(n_ctx, tok, 2 * HD), "ctx", 0, 0, tiled=True)
    if corners:
        core, along_x, along_y = place & 1, (place >> 1) & 1, place >> 2

        def total(kept, sent):
            return kept.astype(f32) + sent.astype(f32)

        def split(x, mine, axis, bit):
            kept = lax.dynamic_index_in_dim(x, mine, axis, keepdims=False)
            return kept, swap(lax.dynamic_index_in_dim(x, 1 - mine, axis, keepdims=False), bit)

        out_kept, out_sent = split(d_out.reshape(2, 2, 2, rows, QG), core, 2, 1)
    d_raw_b = jnp.concatenate([d_q, kv_back(d_kv, cosine, sine)], axis=1)
    d_first = sum_own(dot_nt(d_raw_b, w_attn[:, :ATTN_IN]))
    d_in = dot_tn(a1, d_raw_b).astype(bf16)
    if corners:
        d_first, d_in, out_sent = lax.optimization_barrier((d_first, d_in, out_sent))
        d_out = total(out_kept, out_sent).astype(bf16)
        in_kept, in_sent = split(d_in.reshape(2, 2, 2, rows, ATTN_IN), core, 2, 1)
    dx0_norm, d_gain0 = norm_back(d_first, unit0, scale0, gain_rows[0])
    dx0 = dx1 + dx0_norm

    extra = jnp.pad(jnp.stack([d_gain0, d_gain1, d_gain2]), ((0, 13), (0, 0)))
    moved = lax.all_to_all(jnp.concatenate([dx0, extra]).astype(bf16), "ctx", 1, 0, tiled=True)
    if corners:
        moved, in_sent, d_out = lax.optimization_barrier((moved, in_sent, d_out))
        d_in = total(in_kept, in_sent).astype(bf16)
        in_kept, in_sent = split(d_in, along_x, 1, 2)
        out_kept, out_sent = split(d_out, along_y, 0, 4)
        d_in, d_out = total(in_kept, in_sent).astype(bf16), total(out_kept, out_sent).astype(bf16)
        in_kept, in_sent = split(d_in, along_y, 0, 4)
        out_kept, out_sent = split(d_out, along_x, 0, 2)
        ff_sq = jnp.sum(jnp.square(g_ff.astype(f32)))
        d_head, in_sent, out_sent, ff_sq = lax.optimization_barrier((d_head, in_sent, out_sent, ff_sq))
        g_in, g_out = total(in_kept, in_sent), total(out_kept, out_sent)
    else:
        moved, d_head, d_in, d_out, g_ff = lax.optimization_barrier((moved, d_head, d_in, d_out, g_ff))
        g_in, g_out = (
            lax.psum_scatter(x, "ctx", scatter_dimension=0, tiled=True).astype(f32) for x in (d_in, d_out)
        )
        ff_sq = jnp.sum(jnp.square(g_ff.astype(f32)))
    g_head = lax.all_to_all(d_head.reshape(n_ctx, rows, part), "ctx", 0, 0, tiled=True)
    moved = moved.reshape(n_ctx, own + 16, rows)
    gain_part = jnp.sum(moved[:, own:].astype(f32), axis=0).astype(bf16)
    moved = jnp.concatenate([moved[:, :own].reshape(n_ctx * own, rows), gain_part])
    pieces = [moved]
    for s in range(1, n_head):
        pieces.append(lax.ppermute(moved, "head", [(i, (i - s) % n_head) for i in range(n_head)]))
    gain_all = jnp.stack([piece[n_ctx * own :] for piece in pieces + pieces])
    gain_all = lax.dynamic_slice_in_dim(gain_all, n_head - shard, n_head, 0)
    grad_gain = jnp.sum(gain_all.astype(f32), axis=0)[:3].T
    dx0_all = jnp.stack([piece[: n_ctx * own].reshape(n_ctx * SEQS, chunk, rows) for piece in pieces], axis=1)
    g_embed, embed_sq = embed_grad(slots, dx0_all.reshape(n_ctx * tok, rows).T)

    squares = (
        ff_sq
        + jnp.sum(jnp.square(g_in))
        + jnp.sum(jnp.square(g_out))
        + head_sq
        + jnp.sum(embed_sq)
        + jnp.sum(grad_gain * grad_gain) / n_head
    )
    squares = jnp.full((8, 128), squares)
    if n_head & (n_head - 1):
        squares = jnp.sum(lax.all_gather(squares, "head"), axis=0)
    else:
        for step in range(n_head.bit_length() - 1):
            squares = squares + lax.ppermute(squares, "head", [(i, i ^ (1 << step)) for i in range(n_head)])
    lane = lax.broadcasted_iota(jnp.int32, (8, 128), 1)
    totals = jnp.sum(lax.all_gather(jnp.where(lane == 0, squares, loss_part), "ctx"), axis=0)
    loss = totals[0, 1]
    grad_norm = jnp.sqrt(totals[0, 0])
    factor = jnp.minimum(1.0, clip_level / grad_norm)

    wide = 32
    spreads = (
        (1, 0, 0, ATTN_IN, D**-0.5),
        (2, 0, ATTN_IN, QG, (length / (4.0 * HEADS * HD)) ** 0.5),
        (0, 0, ATTN_IN + QG, 2 * FFG, D**-0.5),
        (0, 2 * FFG, ATTN_IN + QG + 2 * FFG, FFG, FF**-0.5),
    )
    layer = call_update(
        functools.partial(layer_update_kernel, spreads),
        factor,
        (g_ff, g_in, g_out),
        [
            pl.BlockSpec((wide, g_ff.shape[1]), lambda i: (i, 0)),
            pl.BlockSpec((wide, ATTN_IN), lambda i: (i, 0)),
            pl.BlockSpec((wide, QG), lambda i: (i, 0)),
        ],
        w_layer,
        mom_layer,
        avg_layer,
        wide,
        "layer_update",
    )
    g_head, *layer = lax.optimization_barrier((g_head, *layer))
    vocab = call_update(
        functools.partial(vocab_update_kernel, part),
        factor,
        (g_head, g_embed),
        [
            pl.BlockSpec((n_ctx, wide // 2, part), lambda i: (0, i, 0)),
            pl.BlockSpec((wide // 2, EMB_W), lambda i: (i, 0)),
        ],
        w_vocab,
        mom_vocab,
        avg_vocab,
        wide // 2,
        "vocab_update",
    )
    grad = factor * grad_gain
    gains_moment = momentum_rate * mom_gains + grad
    gains_new = gains - BASE * 0.1 * (grad + momentum_rate * gains_moment)
    gains_average = average_rate * avg_gains + (1.0 - average_rate) * gains_new
    return (
        *layer,
        *vocab,
        gains_new,
        gains_moment,
        gains_average,
        gains_new.astype(bf16),
        loss,
        grad_norm,
    )


def solution(mesh):
    token, split, gain = P("ctx"), P("ctx", "head"), P("ctx", None)
    in_specs = (token, token, token, P()) + (split, split, gain) * 3
    out_specs = (split,) * 8 + (gain,) * 4 + (P(), P())
    return jax.shard_map(local, mesh=mesh, in_specs=in_specs, out_specs=out_specs, check_vma=False)
```

```python
import functools
import math

import jax
import jax.numpy as jnp
import numpy as np
from jax import lax
from jax.experimental import pallas as pl
from jax.experimental.pallas import tpu as pltpu
from jax.sharding import PartitionSpec as P

D = 2048
HEADS = 32
KV = 4
HD = 64
FF = 5632
V = 32000
SEQS = 2

eps = 1e-05
z_weight = 0.0001
momentum_rate = 0.5
average_rate = 0.5
clip_level = 0.01

GROUP = HEADS // KV
QG = GROUP * HD
FFG = FF // KV
VG = V // KV
ATTN_IN = QG + 2 * HD
NPARAM = D * (2 * HEADS * HD + 2 * KV * HD + 3 * FF + 2 * V + 3)
BASE = 1.5 * math.sqrt(NPARAM) / clip_level
EMB_AT = VG // 128 * 128
EMB_W = 2 * VG - EMB_AT
EMB_STEPS = 3
EMB_BLOCK = EMB_W // EMB_STEPS

f32 = jnp.float32
bf16 = jnp.bfloat16
NEG = -1e30


def dot_nn(a, b):
    return lax.dot_general(a, b, (((1,), (0,)), ((), ())), preferred_element_type=f32)


def dot_nt(a, b):
    return lax.dot_general(a, b, (((1,), (1,)), ((), ())), preferred_element_type=f32)


def dot_tn(a, b):
    return lax.dot_general(a, b, (((0,), (0,)), ((), ())), preferred_element_type=f32)


def cost(flops, nbytes, trans=0):
    return pl.CostEstimate(flops=int(flops), bytes_accessed=int(nbytes), transcendentals=int(trans))


def params(**kw):
    return pltpu.CompilerParams(vmem_limit_bytes=56 * 1024 * 1024, **kw)


def one_hot(ids, base, width):
    column = lax.broadcasted_iota(jnp.int32, (ids.shape[0], width), 1) + base
    return jnp.where(ids == column, jnp.float32(1.0), jnp.float32(0.0)).astype(bf16)


def lookup_kernel(rows, ids_ref, w_ref, out_ref, acc_ref):
    step = pl.program_id(0)
    w = w_ref[...].astype(bf16)
    total = ids_ref.shape[0]

    @pl.when(step == 0)
    def _():
        acc_ref[...] = jnp.zeros_like(acc_ref)

    for r in range(0, total, rows):
        part = pl.ds(r, rows)
        acc_ref[part, :] += dot_nt(one_hot(ids_ref[part, :], step * EMB_BLOCK, EMB_BLOCK), w)

    @pl.when(step == EMB_STEPS - 1)
    def _():
        out_ref[...] = acc_ref[...].astype(bf16)


def lookup(ids, w_vocab):
    total, rows = ids.shape[0], w_vocab.shape[0]
    return pl.pallas_call(
        functools.partial(lookup_kernel, min(512, total)),
        grid=(EMB_STEPS,),
        in_specs=[
            pl.BlockSpec((total, 1), lambda i: (0, 0)),
            pl.BlockSpec((pl.Element(rows), pl.Element(EMB_BLOCK)), lambda i: (0, (EMB_AT // 128 + EMB_BLOCK // 128 * i) * 128)),
        ],
        out_specs=pl.BlockSpec((total, rows), lambda i: (0, 0)),
        out_shape=jax.ShapeDtypeStruct((total, rows), bf16),
        scratch_shapes=[pltpu.VMEM((total, rows), f32)],
        compiler_params=params(),
        cost_estimate=cost(2 * total * rows * EMB_W, rows * EMB_W * 4),
        name="embed_lookup",
    )(ids, w_vocab)


def embed_grad_kernel(rows, ids_ref, dxt_ref, out_ref, sq_ref):
    step = pl.program_id(0)
    total = ids_ref.shape[0]
    acc = jnp.zeros(out_ref.shape, f32)
    for r in range(0, total, rows):
        hot = one_hot(ids_ref[pl.ds(r, rows), :], step * EMB_BLOCK, EMB_BLOCK)
        acc = acc + dot_nn(dxt_ref[:, pl.ds(r, rows)], hot)
    out_ref[...] = acc.astype(bf16)
    square = acc * acc
    lanes = sum(square[:, k : k + 128] for k in range(0, EMB_BLOCK, 128))
    part = sum(lanes[k : k + 8] for k in range(0, lanes.shape[0], 8))

    @pl.when(step == 0)
    def _():
        sq_ref[...] = jnp.zeros_like(sq_ref)

    sq_ref[...] += part


def embed_grad(ids, dxt):
    rows, total = dxt.shape
    return pl.pallas_call(
        functools.partial(embed_grad_kernel, min(512, total)),
        grid=(EMB_STEPS,),
        in_specs=[
            pl.BlockSpec((total, 1), lambda i: (0, 0)),
            pl.BlockSpec((rows, total), lambda i: (0, 0)),
        ],
        out_specs=[
            pl.BlockSpec((rows, EMB_BLOCK), lambda i: (0, i)),
            pl.BlockSpec((8, 128), lambda i: (0, 0)),
        ],
        out_shape=[
            jax.ShapeDtypeStruct((rows, EMB_W), bf16),
            jax.ShapeDtypeStruct((8, 128), f32),
        ],
        compiler_params=params(),
        cost_estimate=cost(2 * total * rows * EMB_W, rows * EMB_W * 2),
        name="embed_grad",
    )(ids, dxt)


def partner(x):
    width = x.shape[1]
    lane = lax.broadcasted_iota(jnp.int32, x.shape, 1)
    return jnp.where(lane % HD < HD // 2, pltpu.roll(x, width - HD // 2, 1), pltpu.roll(x, HD // 2, 1))


def qkv_kernel(a_ref, w_ref, cos_ref, sin_ref, q_ref, kv_ref):
    raw = dot_nn(a_ref[...], w_ref[...])
    cosine, sine = cos_ref[...], sin_ref[...]
    for j in range(0, QG, 128):
        x = raw[:, j : j + 128]
        rot = (x * cosine + partner(x) * sine).astype(bf16)
        q_ref[:, j : j + 128] = rot * jnp.asarray(HD**-0.5, bf16)
    x = raw[:, QG:]
    lane = lax.broadcasted_iota(jnp.int32, x.shape, 1)
    kv_ref[...] = jnp.where(lane < HD, x * cosine + partner(x) * sine, x).astype(bf16)


def qkv(a1, w_in, cosine, sine):
    tok = a1.shape[0]
    return pl.pallas_call(
        qkv_kernel,
        grid=(1,),
        in_specs=[
            pl.BlockSpec((tok, D), lambda i: (0, 0)),
            pl.BlockSpec((D, ATTN_IN), lambda i: (0, 0)),
            pl.BlockSpec((tok, 128), lambda i: (0, 0)),
            pl.BlockSpec((tok, 128), lambda i: (0, 0)),
        ],
        out_specs=[
            pl.BlockSpec((tok, QG), lambda i: (0, 0)),
            pl.BlockSpec((tok, 2 * HD), lambda i: (0, 0)),
        ],
        out_shape=[
            jax.ShapeDtypeStruct((tok, QG), bf16),
            jax.ShapeDtypeStruct((tok, 2 * HD), bf16),
        ],
        compiler_params=params(),
        cost_estimate=cost(2 * tok * D * ATTN_IN, 2 * D * ATTN_IN + 2 * tok * D),
        name="qkv",
    )(a1, w_in, cosine, sine)


def split_kv(kv_ref, parts_ref):
    kv = kv_ref[...].reshape(-1, 2 * HD).astype(f32)
    lane = lax.broadcasted_iota(jnp.int32, kv.shape, 1)
    swapped = pltpu.roll(kv, HD, 1)
    zero = jnp.zeros_like(kv)
    low = lane < HD
    parts_ref[0] = jnp.where(low, kv, zero).astype(bf16)
    parts_ref[1] = jnp.where(low, zero, swapped).astype(bf16)
    parts_ref[2] = jnp.where(low, swapped, zero).astype(bf16)
    parts_ref[3] = jnp.where(low, zero, kv).astype(bf16)


def attn_kernel(q_ref, kv_ref, qpos_ref, kpos_ref, o_ref, parts_ref):
    @pl.when(pl.program_id(1) == 0)
    def _():
        split_kv(kv_ref, parts_ref)

    q = q_ref[...]
    allowed = kpos_ref[...] <= qpos_ref[...]
    out = None
    for g in range(2):
        s = jnp.where(allowed, dot_nt(q, parts_ref[g]), NEG)
        p = jnp.exp(s - jnp.max(s, axis=1, keepdims=True))
        p = p * (1.0 / jnp.sum(p, axis=1, keepdims=True))
        part = dot_nn(p.astype(bf16), parts_ref[2 + g])
        out = part if out is None else out + part
    o_ref[...] = out.astype(bf16)


def attn(q, kv_every, qpos, kpos):
    n_ctx, _, seq_tok, _ = kv_every.shape
    keys = n_ctx * seq_tok
    pairs = QG // 128
    return pl.pallas_call(
        attn_kernel,
        grid=(SEQS, pairs),
        in_specs=[
            pl.BlockSpec((seq_tok, 128), lambda s, p: (s, p)),
            pl.BlockSpec((n_ctx, 1, seq_tok, 2 * HD), lambda s, p: (0, s, 0, 0)),
            pl.BlockSpec((seq_tok, 1), lambda s, p: (0, 0)),
            pl.BlockSpec((1, keys), lambda s, p: (0, 0)),
        ],
        out_specs=pl.BlockSpec((seq_tok, 128), lambda s, p: (s, p)),
        out_shape=jax.ShapeDtypeStruct((SEQS * seq_tok, QG), bf16),
        scratch_shapes=[pltpu.VMEM((4, keys, 2 * HD), bf16)],
        compiler_params=params(),
        cost_estimate=cost(
            8 * SEQS * seq_tok * keys * QG, 4 * SEQS * seq_tok * QG, SEQS * GROUP * seq_tok * keys
        ),
        name="attn_fwd",
    )(q, kv_every, qpos.reshape(seq_tok, 1), kpos.reshape(1, keys))


def attn_back_kernel(
    pairs, q_ref, do_ref, kv_ref, qpos_ref, kpos_ref, cos_ref, sin_ref, dq_ref, dkv_ref, parts_ref, acc_ref
):
    pair = pl.program_id(1)

    @pl.when(pair == 0)
    def _():
        split_kv(kv_ref, parts_ref)
        acc_ref[...] = jnp.zeros_like(acc_ref)

    q = q_ref[...]
    do = do_ref[...]
    allowed = kpos_ref[...] <= qpos_ref[...]
    dq = None
    for g in range(2):
        s = jnp.where(allowed, dot_nt(parts_ref[g], q), NEG)
        p = jnp.exp(s - jnp.max(s, axis=0, keepdims=True))
        p = p * (1.0 / jnp.sum(p, axis=0, keepdims=True))
        dp = dot_nt(parts_ref[2 + g], do)
        delta = jnp.sum(p * dp, axis=0, keepdims=True)
        ds = (p * (dp - delta)).astype(bf16)
        part = dot_tn(ds, parts_ref[g])
        dq = part if dq is None else dq + part
        acc_ref[g] += dot_nn(ds, q)
        acc_ref[2 + g] += dot_nn(p.astype(bf16), do)
    dq = dq * (HD**-0.5)
    dq_ref[...] = (dq * cos_ref[...] - partner(dq) * sin_ref[...]).astype(bf16)

    @pl.when(pair == pairs - 1)
    def _():
        lane = lax.broadcasted_iota(jnp.int32, acc_ref.shape[1:], 1)
        grad_k = acc_ref[0] + pltpu.roll(acc_ref[1], HD, 1)
        grad_v = pltpu.roll(acc_ref[2], HD, 1) + acc_ref[3]
        dkv_ref[...] = jnp.where(lane < HD, grad_k, grad_v).astype(bf16).reshape(dkv_ref.shape)


def attn_back(q, do, kv_every, qpos, kpos, cosine, sine):
    n_ctx, _, seq_tok, _ = kv_every.shape
    keys = n_ctx * seq_tok
    pairs = QG // 128
    return pl.pallas_call(
        functools.partial(attn_back_kernel, pairs),
        grid=(SEQS, pairs),
        in_specs=[
            pl.BlockSpec((seq_tok, 128), lambda s, p: (s, p)),
            pl.BlockSpec((seq_tok, 128), lambda s, p: (s, p)),
            pl.BlockSpec((n_ctx, 1, seq_tok, 2 * HD), lambda s, p: (0, s, 0, 0)),
            pl.BlockSpec((1, seq_tok), lambda s, p: (0, 0)),
            pl.BlockSpec((keys, 1), lambda s, p: (0, 0)),
            pl.BlockSpec((seq_tok, 128), lambda s, p: (s, 0)),
            pl.BlockSpec((seq_tok, 128), lambda s, p: (s, 0)),
        ],
        out_specs=[
            pl.BlockSpec((seq_tok, 128), lambda s, p: (s, p)),
            pl.BlockSpec((n_ctx, 1, seq_tok, 2 * HD), lambda s, p: (0, s, 0, 0)),
        ],
        out_shape=[
            jax.ShapeDtypeStruct((SEQS * seq_tok, QG), bf16),
            jax.ShapeDtypeStruct(kv_every.shape, bf16),
        ],
        scratch_shapes=[
            pltpu.VMEM((4, keys, 2 * HD), bf16),
            pltpu.VMEM((4, keys, 2 * HD), f32),
        ],
        compiler_params=params(),
        cost_estimate=cost(
            20 * SEQS * seq_tok * keys * QG, 8 * SEQS * seq_tok * QG, SEQS * GROUP * seq_tok * keys
        ),
        name="attn_bwd",
    )(q, do, kv_every, qpos.reshape(1, seq_tok), kpos.reshape(keys, 1), cosine, sine)


def kv_back_kernel(parts_ref, cos_ref, sin_ref, out_ref):
    x = parts_ref[0].astype(f32)
    for k in range(1, parts_ref.shape[0]):
        x = x + parts_ref[k].astype(f32)
    lane = lax.broadcasted_iota(jnp.int32, x.shape, 1)
    out_ref[...] = jnp.where(lane < HD, x * cos_ref[...] - partner(x) * sin_ref[...], x).astype(bf16)


def kv_back(parts, cosine, sine):
    return pl.pallas_call(
        kv_back_kernel,
        out_shape=jax.ShapeDtypeStruct(parts.shape[1:], bf16),
        compiler_params=params(),
        name="kv_bwd",
    )(parts, cosine, sine)


def head_cast_kernel(block, w_ref, *outs):
    column = lax.broadcasted_iota(jnp.int32, w_ref.shape, 1) + pl.program_id(0) * block
    w = jnp.where(column < VG, w_ref[...], 0.0).astype(bf16)
    count = w.shape[0] // len(outs)
    for k, out_ref in enumerate(outs):
        out_ref[...] = w[k * count : (k + 1) * count]


def head_cast(w_vocab, width, parts):
    rows = w_vocab.shape[0]
    block = 1024
    return pl.pallas_call(
        functools.partial(head_cast_kernel, block),
        grid=(width // block,),
        in_specs=[pl.BlockSpec((rows, block), lambda i: (0, i))],
        out_specs=[pl.BlockSpec((rows // parts, block), lambda i: (0, i))] * parts,
        out_shape=[jax.ShapeDtypeStruct((rows // parts, width), bf16)] * parts,
        compiler_params=params(),
        cost_estimate=cost(rows * width, rows * width * 6),
        name="head_cast",
    )(w_vocab)


def joined(pieces, parts):
    for k in range(0, len(pieces), parts):
        run = [piece[...] for piece in pieces[k : k + parts]]
        yield k // parts, run[0] if parts == 1 else jnp.concatenate(run, axis=0)


def partial_kernel(parts, at_ref, x_ref, *refs):
    pieces, out_ref = refs[:-1], refs[-1]
    logits = None
    for k, w in joined(pieces, parts):
        at = pl.multiple_of(at_ref[k], 128)
        term = dot_nn(x_ref[:, pl.ds(at, w.shape[0])], w)
        logits = term if logits is None else logits + term
    out_ref[...] = logits


def head_partial(x, pieces, at):
    tok = x.shape[0]
    width = pieces[0].shape[1]
    rows = sum(piece.shape[0] for piece in pieces)
    block = 1024
    return pl.pallas_call(
        functools.partial(partial_kernel, len(pieces) // at.shape[0]),
        grid=(width // block,),
        in_specs=[
            pl.BlockSpec(memory_space=pltpu.SMEM),
            pl.BlockSpec((tok, D), lambda i: (0, 0)),
        ]
        + [pl.BlockSpec((piece.shape[0], block), lambda i: (0, i)) for piece in pieces],
        out_specs=pl.BlockSpec((tok, block), lambda i: (0, i)),
        out_shape=jax.ShapeDtypeStruct((tok, width), f32),
        compiler_params=params(),
        cost_estimate=cost(2 * tok * rows * width, 2 * rows * width + 4 * tok * width),
        name="head_partial",
    )(at, x, *pieces)


def logits_kernel(steps, parts, based, at_ref, x_ref, slot_ref, *refs):
    base = refs[:based]
    pieces, (out_ref, stats_ref, top_ref, total_ref, label_ref) = refs[based:-5], refs[-5:]
    step = pl.program_id(0)
    block = out_ref.shape[1]

    @pl.when(step == 0)
    def _():
        top_ref[...] = jnp.full_like(top_ref, NEG)
        total_ref[...] = jnp.zeros_like(total_ref)
        label_ref[...] = jnp.zeros_like(label_ref)

    logits = base[0][...] if based else None
    for k, w in joined(pieces, parts):
        at = pl.multiple_of(at_ref[k], 128)
        term = dot_nn(x_ref[:, pl.ds(at, w.shape[0])], w)
        logits = term if logits is None else logits + term
    column = lax.broadcasted_iota(jnp.int32, logits.shape, 1) + step * block
    logits = jnp.where(column < VG, logits, NEG)
    out_ref[...] = logits
    top = top_ref[...]
    new_top = jnp.maximum(top, jnp.max(logits, axis=1, keepdims=True))
    total_ref[...] = total_ref[...] * jnp.exp(top - new_top) + jnp.sum(
        jnp.exp(logits - new_top), axis=1, keepdims=True
    )
    top_ref[...] = new_top
    label_ref[...] += jnp.sum(jnp.where(column == slot_ref[...], logits, 0.0), axis=1, keepdims=True)

    @pl.when(step == steps - 1)
    def _():
        lane = lax.broadcasted_iota(jnp.int32, (x_ref.shape[0], 128), 1)
        packed = jnp.where(lane == 0, top_ref[...], jnp.where(lane == 1, total_ref[...], label_ref[...]))
        stats_ref[...] = packed.T[:8]


def head_logits(x, slots, base, pieces, at):
    tok = x.shape[0]
    rows = sum(piece.shape[0] for piece in pieces)
    width = pieces[0].shape[1]
    block = 1024
    steps = width // block
    return pl.pallas_call(
        functools.partial(logits_kernel, steps, len(pieces) // at.shape[0], len(base)),
        grid=(steps,),
        in_specs=[
            pl.BlockSpec(memory_space=pltpu.SMEM),
            pl.BlockSpec((tok, D), lambda i: (0, 0)),
            pl.BlockSpec((tok, 1), lambda i: (0, 0)),
        ]
        + [pl.BlockSpec((tok, block), lambda i: (0, i)) for _ in base]
        + [pl.BlockSpec((piece.shape[0], block), lambda i: (0, i)) for piece in pieces],
        out_specs=[
            pl.BlockSpec((tok, block), lambda i: (0, i)),
            pl.BlockSpec((8, tok), lambda i: (0, 0)),
        ],
        out_shape=[
            jax.ShapeDtypeStruct((tok, width), f32),
            jax.ShapeDtypeStruct((8, tok), f32),
        ],
        scratch_shapes=[pltpu.VMEM((tok, 1), f32)] * 3,
        compiler_params=params(),
        cost_estimate=cost(2 * tok * rows * width, 2 * rows * width + 8 * tok * width, tok * width),
        name="head_logits",
    )(at, x, slots, *base, *pieces)


def dlogits_kernel(steps, parts, at_ref, logits_ref, values_ref, slot_ref, *refs):
    pieces, (dlog_ref, dx_ref, acc_ref) = refs[:-3], refs[-3:]
    step = pl.program_id(0)
    tok, block = logits_ref.shape
    logits = logits_ref[...]
    lse = values_ref[:, 0:1]
    weight = values_ref[:, 1:2]
    column = lax.broadcasted_iota(jnp.int32, logits.shape, 1) + step * block
    hit = jnp.where(column == slot_ref[...], 1.0, 0.0)
    soft = jnp.exp(logits - lse)
    dlog = (weight * ((1.0 + 2.0 * z_weight * lse) * soft - hit)).astype(bf16)
    part = dlog_ref.shape[2]
    for k in range(dlog_ref.shape[0]):
        dlog_ref[k] = dlog[:, k * part : (k + 1) * part]

    @pl.when(step == 0)
    def _():
        acc_ref[...] = jnp.zeros_like(acc_ref)

    for k, w in joined(pieces, parts):
        at = pl.multiple_of(at_ref[k], 128)
        acc_ref[pl.ds(at, w.shape[0]), :] += dot_nt(w, dlog)

    @pl.when(step == steps - 1)
    def _():
        for k in range(0, acc_ref.shape[0], 256):
            dx_ref[:, k : k + 256] = acc_ref[k : k + 256, :].T.astype(bf16)


def head_dlogits(logits, values, slots, pieces, at, part):
    tok, width = logits.shape
    block = 1024
    steps = width // block
    return pl.pallas_call(
        functools.partial(dlogits_kernel, steps, len(pieces) // at.shape[0]),
        grid=(steps,),
        in_specs=[
            pl.BlockSpec(memory_space=pltpu.SMEM),
            pl.BlockSpec((tok, block), lambda i: (0, i)),
            pl.BlockSpec((tok, values.shape[1]), lambda i: (0, 0)),
            pl.BlockSpec((tok, 1), lambda i: (0, 0)),
        ]
        + [pl.BlockSpec((piece.shape[0], block), lambda i: (0, i)) for piece in pieces],
        out_specs=[
            pl.BlockSpec((block // part, tok, part), lambda i: (i, 0, 0)),
            pl.BlockSpec((tok, D), lambda i: (0, 0)),
        ],
        out_shape=[
            jax.ShapeDtypeStruct((width // part, tok, part), bf16),
            jax.ShapeDtypeStruct((tok, D), bf16),
        ],
        scratch_shapes=[pltpu.VMEM((D, tok), f32)],
        compiler_params=params(),
        cost_estimate=cost(2 * tok * D * width, 2 * D * width + 6 * tok * width, tok * width),
        name="head_dlogits",
    )(at, logits, values, slots, *pieces)


def outer_kernel(a_ref, da_ref, b_ref, db_ref, out_ref, *, a_steps):
    step = pl.program_id(0)

    @pl.when(step < a_steps)
    def _():
        out_ref[...] = dot_tn(a_ref[...], da_ref[...]).astype(bf16)

    @pl.when(step >= a_steps)
    def _():
        out_ref[...] = dot_tn(b_ref[...], db_ref[...]).astype(bf16)


def outer_pair(a, da, b, db, block, rows, name):
    tok = a.shape[0]
    a_steps, b_steps = da.shape[1] // block, db.shape[1] // block
    width = da.shape[1] + db.shape[1]
    return pl.pallas_call(
        functools.partial(outer_kernel, a_steps=a_steps),
        grid=(a_steps + b_steps, D // rows),
        in_specs=[
            pl.BlockSpec((tok, rows), lambda i, j: (0, j)),
            pl.BlockSpec((tok, block), lambda i, j: (0, jnp.minimum(i, a_steps - 1))),
            pl.BlockSpec((tok, rows), lambda i, j: (0, j)),
            pl.BlockSpec((tok, block), lambda i, j: (0, jnp.maximum(i - a_steps, 0))),
        ],
        out_specs=pl.BlockSpec((rows, block), lambda i, j: (j, i)),
        out_shape=jax.ShapeDtypeStruct((D, width), bf16),
        compiler_params=params(),
        cost_estimate=cost(2 * tok * D * width, 2 * D * width + 4 * tok * D),
        name=name,
    )(a, da, b, db)


def update_piece(factor, rate, grad, w_ref, m_ref, a_ref, outs, columns):
    new_ref, moment_ref, average_ref, copy_ref = outs
    grad = factor * grad
    moment = momentum_rate * m_ref[:, columns] + grad
    new = w_ref[:, columns] - rate * (grad + momentum_rate * moment)
    new_ref[:, columns] = new
    moment_ref[:, columns] = moment
    average_ref[:, columns] = average_rate * a_ref[:, columns] + (1.0 - average_rate) * new
    copy_ref[:, columns] = new.astype(bf16)


def layer_update_kernel(spreads, factor_ref, *refs):
    grads, (w_ref, m_ref, a_ref), outs = refs[:-7], refs[-7:-4], refs[-4:]
    factor = factor_ref[0, 0]
    for source, inner, outer, width, spread in spreads:
        grad = grads[source][:, inner : inner + width].astype(f32)
        update_piece(factor, BASE * spread, grad, w_ref, m_ref, a_ref, outs, slice(outer, outer + width))


def vocab_update_kernel(part, factor_ref, head_ref, embed_ref, w_ref, m_ref, a_ref, *outs):
    factor = factor_ref[0, 0]
    head_rate = BASE * 2.0 * D**-0.5
    for k in range(head_ref.shape[0]):
        low, high = k * part, min((k + 1) * part, EMB_AT)
        if low >= high:
            continue
        grad = head_ref[k, :, : high - low].astype(f32)
        update_piece(factor, head_rate, grad, w_ref, m_ref, a_ref, outs, slice(low, high))
    edge = EMB_AT - EMB_AT // part * part
    grad_head = head_ref[EMB_AT // part, :, edge : edge + 128].astype(f32)
    grad_embed = embed_ref[:, :128].astype(f32)
    own = lax.broadcasted_iota(jnp.int32, grad_head.shape, 1) < VG - EMB_AT
    update_piece(
        factor,
        jnp.where(own, head_rate, BASE),
        jnp.where(own, grad_head, grad_embed),
        w_ref,
        m_ref,
        a_ref,
        outs,
        slice(EMB_AT, EMB_AT + 128),
    )
    for low in range(128, EMB_W, 1024):
        high = min(low + 1024, EMB_W)
        grad = embed_ref[:, low:high].astype(f32)
        update_piece(factor, BASE, grad, w_ref, m_ref, a_ref, outs, slice(EMB_AT + low, EMB_AT + high))


def call_update(kernel, factor, grads, grad_specs, w, m, a, rows, name):
    total, width = w.shape
    block = pl.BlockSpec((rows, width), lambda i: (i, 0))
    return pl.pallas_call(
        kernel,
        grid=(total // rows,),
        in_specs=[pl.BlockSpec(memory_space=pltpu.SMEM)] + grad_specs + [block] * 3,
        out_specs=[block] * 4,
        out_shape=[jax.ShapeDtypeStruct(w.shape, f32)] * 3 + [jax.ShapeDtypeStruct(w.shape, bf16)],
        compiler_params=params(),
        cost_estimate=cost(10 * total * width, 28 * total * width),
        name=name,
    )(factor.reshape(1, 1), *grads, w, m, a)


def norm_parts(x):
    scale = lax.rsqrt(jnp.mean(x * x, axis=-1, keepdims=True) + eps)
    return x * scale, scale


def norm_back(dy, unit, scale, gain):
    scaled = dy * gain
    dx = scale * (scaled - unit * jnp.mean(scaled * unit, axis=-1, keepdims=True))
    return dx, jnp.sum(dy * unit, axis=0)


def local(
    token_ids,
    labels,
    answer_mask,
    pair_map,
    w_layer,
    w_vocab,
    gains,
    mom_layer,
    mom_vocab,
    mom_gains,
    avg_layer,
    avg_vocab,
    avg_gains,
):
    n_ctx = lax.axis_size("ctx")
    n_head = lax.axis_size("head")
    place = lax.axis_index("ctx")
    shard = lax.axis_index("head")
    tok = token_ids.shape[0]
    rows = w_layer.shape[0]
    seq_tok = tok // SEQS
    span = seq_tok // 2
    chunk = seq_tok // n_head
    own = SEQS * chunk
    length = n_ctx * seq_tok
    part = -(-VG // (n_ctx * 128)) * 128

    def turn(x, axis):
        return lax.dynamic_slice_in_dim(
            jnp.concatenate([x, x], axis), shard * chunk, seq_tok, axis
        )

    def turn_back(x, axis):
        return lax.dynamic_slice_in_dim(
            jnp.concatenate([x, x], axis), seq_tok - shard * chunk, seq_tok, axis
        )

    def head_scatter(x):
        sums = x[:, 0].astype(f32)
        for s in range(1, n_head):
            sent = lax.ppermute(x[:, s], "head", [(i, (i + s) % n_head) for i in range(n_head)])
            sums = sums + sent.astype(f32)
        return sums

    def head_gather(x):
        pieces = [x]
        for s in range(1, n_head):
            pieces.append(lax.ppermute(x, "head", [(i, (i - s) % n_head) for i in range(n_head)]))
        return jnp.stack(pieces, axis=1)

    def sum_own(partial):
        split = partial.astype(bf16).reshape(SEQS, n_head, chunk, D)
        return head_scatter(split).reshape(own, D)

    def spread_all(x):
        return head_gather(x.astype(bf16).reshape(SEQS, chunk, D)).reshape(tok, D)

    layer_b = w_layer.astype(bf16)
    edge = ATTN_IN + QG
    w_attn = lax.all_gather(layer_b[:, :edge], "ctx", axis=0, tiled=True)
    w_ff = lax.all_gather(layer_b[:, edge:], "ctx", axis=0, tiled=True)
    w_out, w_gu, w_down = w_attn[:, ATTN_IN:], w_ff[:, : 2 * FFG], w_ff[:, 2 * FFG :]
    corners = n_ctx == 8
    head_own = head_cast(w_vocab, n_ctx * part, 2 if corners else 1)

    def swap(x, bit):
        return lax.ppermute(x, "ctx", [(i, i ^ bit) for i in range(n_ctx)])

    gain_own = lax.reduce_precision(gains, exponent_bits=8, mantissa_bits=7).T.reshape(3 * rows)
    every = jnp.concatenate([token_ids.astype(f32), answer_mask.astype(f32), gain_own])
    every = lax.all_gather(every, "ctx")
    ids_all = every[:, :tok].astype(jnp.int32).reshape(n_ctx, SEQS, seq_tok)
    ids_all = turn(ids_all, 2).reshape(n_ctx * tok)
    count = jnp.sum(every[:, tok : 2 * tok])
    gain_rows = jnp.moveaxis(every[:, 2 * tok :].reshape(n_ctx, 3, rows), 1, 0).reshape(3, D)
    labels_own = turn(labels.reshape(SEQS, seq_tok), 1).reshape(tok)
    mask_own = turn(answer_mask.reshape(SEQS, seq_tok), 1).reshape(tok)

    offset_id = shard * VG
    local_ids = ids_all - offset_id
    inside = (local_ids >= 0) & (local_ids < VG)
    slots = jnp.where(inside, local_ids + (VG - EMB_AT), -1).reshape(-1, 1)
    picked = lookup(slots, w_vocab).reshape(n_ctx * SEQS, n_head, chunk, rows)
    picked = head_scatter(picked).astype(bf16).reshape(n_ctx * own, rows)
    x0 = lax.all_to_all(picked, "ctx", 0, 1, tiled=True).astype(f32)

    unit0, scale0 = norm_parts(x0)
    a1 = spread_all(unit0 * gain_rows[0])
    if corners:
        over = [swap(x, 1) for x in head_own]
        a1, low, high, over_low, over_high = lax.optimization_barrier((a1, *head_own, *over))
    row = (jnp.arange(seq_tok, dtype=jnp.int32) + shard * chunk) % seq_tok

    def positions(index):
        index = index[:, None]
        at = jnp.where(row // span == 0, index, 2 * n_ctx - 1 - index)
        return at * span + row % span

    qpos = positions(pair_map[place][None])[0]
    kpos = positions(pair_map).reshape(length)
    half = HD // 2
    inverse = 10000.0 ** (-2.0 * np.arange(half) / HD)
    ramp = np.clip((2048.0 * inverse / (2.0 * math.pi) - 1.0) / 31.0, 0.0, 1.0)
    freq = np.tile(((1.0 - ramp) * inverse / 4.0 + ramp * inverse).astype(np.float32), 128 // half)
    sign = np.where(np.arange(128) % HD < half, -1.0, 1.0).astype(np.float32)
    mscale = 0.1 * math.log(4.0) + 1.0
    angle = jnp.tile(qpos, SEQS).astype(f32)[:, None] * freq[None, :]
    cosine = jnp.cos(angle) * mscale
    sine = jnp.sin(angle) * (mscale * sign)[None, :]
    q, kv_own = qkv(a1, w_attn, cosine, sine)
    kv_every = lax.all_gather(kv_own, "ctx").reshape(n_ctx, SEQS, seq_tok, 2 * HD)
    if corners:
        kv_every, low, high = lax.optimization_barrier((kv_every, low, high))
        y_low, x_high, x_low, y_high = swap(low, 4), swap(high, 2), swap(low, 2), swap(high, 4)
    attn_b = attn(q, kv_every, qpos, kpos)
    x1 = x0 + sum_own(dot_nt(attn_b, w_out))

    unit1, scale1 = norm_parts(x1)
    a2 = spread_all(unit1 * gain_rows[1])
    if corners:
        a2, y_low, x_high = lax.optimization_barrier((a2, y_low, x_high))
        far_low, far_high = swap(y_low, 2), swap(x_high, 4)
    gate_up = dot_nn(a2, w_gu)

    def glu(values):
        return jax.nn.silu(values[:, :FFG]) * values[:, FFG:]

    hidden_f, glu_back = jax.vjp(glu, gate_up)
    hidden_b = hidden_f.astype(bf16)
    second = sum_own(dot_nt(hidden_b, w_down))
    if corners:
        second, x_low, y_high = lax.optimization_barrier((second, x_low, y_high))
    x2 = x1 + second

    unit2, scale2 = norm_parts(x2)
    final_b = spread_all(unit2 * gain_rows[2])
    label_ids = labels_own - offset_id
    label_slots = jnp.where((label_ids >= 0) & (label_ids < VG), label_ids, -1).reshape(tok, 1)
    if corners:
        near = [low, high, over_low, over_high, x_low, x_high, y_low, y_high]
        head_at = jnp.stack([(place ^ bits) * rows for bits in (0, 1, 2, 4, 3, 5, 6, 7)])
        base = head_partial(final_b, near, head_at[:4])
        base, far_low, far_high = lax.optimization_barrier((base, far_low, far_high))
        far = [swap(x, 1) for x in (x_low, x_high, y_low, y_high)]
        far += [far_low, far_high, swap(far_low, 1), swap(far_high, 1)]
        head_pieces = near + far
        logits, stats = head_logits(final_b, label_slots, [base], far, head_at[4:])
    else:
        head_pieces = [lax.all_gather(head_own[0], "ctx", axis=0, tiled=True)]
        head_at = jnp.zeros((1,), jnp.int32)
        logits, stats = head_logits(final_b, label_slots, [], head_pieces, head_at)
    stats, final_late = lax.optimization_barrier((stats, final_b))
    pieces = [stats]
    for s in range(1, n_head):
        sent = lax.ppermute(stats, "head", [(i, (i - s) % n_head) for i in range(n_head)])
        sent = sent.reshape(8, SEQS, n_head, chunk)
        pieces.append(jnp.roll(sent, s, axis=2).reshape(8, tok))
    doubled = jnp.stack(pieces + pieces)
    stats = lax.dynamic_slice_in_dim(doubled, n_head - shard, n_head, 0)
    top = jnp.max(stats[:, 0], axis=0)
    total = jnp.sum(stats[:, 1] * jnp.exp(stats[:, 0] - top), axis=0)
    lse = top + jnp.log(total)
    weight = mask_own.astype(f32) / count
    terms = weight * (lse - jnp.sum(stats[:, 2], axis=0) + z_weight * lse * lse)
    loss_part = jnp.sum(turn_back(terms.reshape(SEQS, seq_tok), 1))
    values = jnp.stack([lse, weight] + [weight] * 6).T
    dlog_b, d_final = head_dlogits(logits, values, label_slots, head_pieces, head_at, part)
    final_all = lax.all_gather(final_late, "ctx", axis=0, tiled=True)
    dlog_all = lax.all_to_all(dlog_b, "ctx", 0, 0, tiled=True).reshape(n_ctx * tok, part)

    dx2, d_gain2 = norm_back(sum_own(d_final), unit2, scale2, gain_rows[2])
    dyf_b = spread_all(dx2)
    d_hidden = dot_nn(dyf_b, w_down)
    d_gate_up_b = glu_back(d_hidden)[0].astype(bf16)
    d_second = sum_own(dot_nt(d_gate_up_b, w_gu))
    d_ff = outer_pair(a2, d_gate_up_b, dyf_b, hidden_b, FFG, 512, "ff_weight_grad")
    d_second, d_ff, dlog_all, final_all = lax.optimization_barrier((d_second, d_ff, dlog_all, final_all))
    g_ff = lax.psum_scatter(d_ff, "ctx", scatter_dimension=0, tiled=True)
    dx1_norm, d_gain1 = norm_back(d_second, unit1, scale1, gain_rows[1])
    dx1 = dx2 + dx1_norm
    d_head = dot_tn(final_all, dlog_all)
    head_sq = jnp.sum(d_head * d_head)
    dya_b, d_head = lax.optimization_barrier((spread_all(dx1), d_head.astype(bf16)))
    d_attn_b = dot_nn(dya_b, w_out).astype(bf16)
    d_q, d_kv = attn_back(q, d_attn_b, kv_every, qpos, kpos, cosine, sine)
    d_out = dot_tn(dya_b, attn_b).astype(bf16)
    d_kv = lax.all_to_all(d_kv.reshape(n_ctx, tok, 2 * HD), "ctx", 0, 0, tiled=True)
    if corners:
        core, along_x, along_y = place & 1, (place >> 1) & 1, place >> 2

        def total(kept, sent):
            return kept.astype(f32) + sent.astype(f32)

        def split(x, mine, axis, bit):
            kept = lax.dynamic_index_in_dim(x, mine, axis, keepdims=False)
            return kept, swap(lax.dynamic_index_in_dim(x, 1 - mine, axis, keepdims=False), bit)

        out_kept, out_sent = split(d_out.reshape(2, 2, 2, rows, QG), core, 2, 1)
    d_raw_b = jnp.concatenate([d_q, kv_back(d_kv, cosine, sine)], axis=1)
    d_first = sum_own(dot_nt(d_raw_b, w_attn[:, :ATTN_IN]))
    d_in = dot_tn(a1, d_raw_b).astype(bf16)
    if corners:
        d_first, d_in, out_sent = lax.optimization_barrier((d_first, d_in, out_sent))
        d_out = total(out_kept, out_sent).astype(bf16)
        in_kept, in_sent = split(d_in.reshape(2, 2, 2, rows, ATTN_IN), core, 2, 1)
    dx0_norm, d_gain0 = norm_back(d_first, unit0, scale0, gain_rows[0])
    dx0 = dx1 + dx0_norm

    extra = jnp.pad(jnp.stack([d_gain0, d_gain1, d_gain2]), ((0, 13), (0, 0)))
    moved = lax.all_to_all(jnp.concatenate([dx0, extra]).astype(bf16), "ctx", 1, 0, tiled=True)
    if corners:
        moved, in_sent, d_out = lax.optimization_barrier((moved, in_sent, d_out))
        d_in = total(in_kept, in_sent).astype(bf16)
        in_kept, in_sent = split(d_in, along_x, 1, 2)
        out_kept, out_sent = split(d_out, along_y, 0, 4)
        d_in, d_out = total(in_kept, in_sent).astype(bf16), total(out_kept, out_sent).astype(bf16)
        in_kept, in_sent = split(d_in, along_y, 0, 4)
        out_kept, out_sent = split(d_out, along_x, 0, 2)
        d_head, in_sent, out_sent = lax.optimization_barrier((d_head, in_sent, out_sent))
        g_in, g_out = total(in_kept, in_sent), total(out_kept, out_sent)
    else:
        moved, d_head, d_in, d_out, g_ff = lax.optimization_barrier((moved, d_head, d_in, d_out, g_ff))
        g_in, g_out = (
            lax.psum_scatter(x, "ctx", scatter_dimension=0, tiled=True).astype(f32) for x in (d_in, d_out)
        )
    g_head = lax.all_to_all(d_head.reshape(n_ctx, rows, part), "ctx", 0, 0, tiled=True)
    moved = moved.reshape(n_ctx, own + 16, rows)
    gain_part = jnp.sum(moved[:, own:].astype(f32), axis=0).astype(bf16)
    moved = jnp.concatenate([moved[:, :own].reshape(n_ctx * own, rows), gain_part])
    pieces = [moved]
    for s in range(1, n_head):
        pieces.append(lax.ppermute(moved, "head", [(i, (i - s) % n_head) for i in range(n_head)]))
    gain_all = jnp.stack([piece[n_ctx * own :] for piece in pieces + pieces])
    gain_all = lax.dynamic_slice_in_dim(gain_all, n_head - shard, n_head, 0)
    grad_gain = jnp.sum(gain_all.astype(f32), axis=0)[:3].T
    dx0_all = jnp.stack([piece[: n_ctx * own].reshape(n_ctx * SEQS, chunk, rows) for piece in pieces], axis=1)
    g_embed, embed_sq = embed_grad(slots, dx0_all.reshape(n_ctx * tok, rows).T)

    squares = (
        jnp.sum(jnp.square(g_ff.astype(f32)))
        + jnp.sum(jnp.square(g_in))
        + jnp.sum(jnp.square(g_out))
        + head_sq
        + jnp.sum(embed_sq)
        + jnp.sum(grad_gain * grad_gain) / n_head
    )
    squares = jnp.full((8, 128), squares)
    if n_head & (n_head - 1):
        squares = jnp.sum(lax.all_gather(squares, "head"), axis=0)
    else:
        level = [squares]
        for s in range(1, n_head):
            level.append(lax.ppermute(squares, "head", [(i, i ^ s) for i in range(n_head)]))
        while len(level) > 1:
            level = [a + b for a, b in zip(level[::2], level[1::2])]
        squares = level[0]
    lane = lax.broadcasted_iota(jnp.int32, (8, 128), 1)
    totals = jnp.sum(lax.all_gather(jnp.where(lane == 0, squares, loss_part), "ctx"), axis=0)
    loss = totals[0, 1]
    grad_norm = jnp.sqrt(totals[0, 0])
    factor = jnp.minimum(1.0, clip_level / grad_norm)

    wide = 32
    spreads = (
        (1, 0, 0, ATTN_IN, D**-0.5),
        (2, 0, ATTN_IN, QG, (length / (4.0 * HEADS * HD)) ** 0.5),
        (0, 0, ATTN_IN + QG, 2 * FFG, D**-0.5),
        (0, 2 * FFG, ATTN_IN + QG + 2 * FFG, FFG, FF**-0.5),
    )
    layer = call_update(
        functools.partial(layer_update_kernel, spreads),
        factor,
        (g_ff, g_in, g_out),
        [
            pl.BlockSpec((wide, g_ff.shape[1]), lambda i: (i, 0)),
            pl.BlockSpec((wide, ATTN_IN), lambda i: (i, 0)),
            pl.BlockSpec((wide, QG), lambda i: (i, 0)),
        ],
        w_layer,
        mom_layer,
        avg_layer,
        wide,
        "layer_update",
    )
    g_head, *layer = lax.optimization_barrier((g_head, *layer))
    vocab = call_update(
        functools.partial(vocab_update_kernel, part),
        factor,
        (g_head, g_embed),
        [
            pl.BlockSpec((n_ctx, wide // 2, part), lambda i: (0, i, 0)),
            pl.BlockSpec((wide // 2, EMB_W), lambda i: (i, 0)),
        ],
        w_vocab,
        mom_vocab,
        avg_vocab,
        wide // 2,
        "vocab_update",
    )
    grad = factor * grad_gain
    gains_moment = momentum_rate * mom_gains + grad
    gains_new = gains - BASE * 0.1 * (grad + momentum_rate * gains_moment)
    gains_average = average_rate * avg_gains + (1.0 - average_rate) * gains_new
    return (
        *layer,
        *vocab,
        gains_new,
        gains_moment,
        gains_average,
        gains_new.astype(bf16),
        loss,
        grad_norm,
    )


def solution(mesh):
    token, split, gain = P("ctx"), P("ctx", "head"), P("ctx", None)
    in_specs = (token, token, token, P()) + (split, split, gain) * 3
    out_specs = (split,) * 8 + (gain,) * 4 + (P(), P())
    return jax.shard_map(local, mesh=mesh, in_specs=in_specs, out_specs=out_specs, check_vma=False)
```

```python
import functools
import math

import jax
import jax.numpy as jnp
import numpy as np
from jax import lax
from jax.experimental import pallas as pl
from jax.experimental.pallas import tpu as pltpu
from jax.sharding import PartitionSpec as P

D = 2048
HEADS = 32
KV = 4
HD = 64
FF = 5632
V = 32000
SEQS = 2

eps = 1e-05
z_weight = 0.0001
momentum_rate = 0.5
average_rate = 0.5
clip_level = 0.01

GROUP = HEADS // KV
QG = GROUP * HD
FFG = FF // KV
VG = V // KV
ATTN_IN = QG + 2 * HD
NPARAM = D * (2 * HEADS * HD + 2 * KV * HD + 3 * FF + 2 * V + 3)
BASE = 1.5 * math.sqrt(NPARAM) / clip_level
EMB_AT = VG // 128 * 128
EMB_W = 2 * VG - EMB_AT
EMB_STEPS = 3
EMB_BLOCK = EMB_W // EMB_STEPS

f32 = jnp.float32
bf16 = jnp.bfloat16
NEG = -1e30


def dot_nn(a, b):
    return lax.dot_general(a, b, (((1,), (0,)), ((), ())), preferred_element_type=f32)


def dot_nt(a, b):
    return lax.dot_general(a, b, (((1,), (1,)), ((), ())), preferred_element_type=f32)


def dot_tn(a, b):
    return lax.dot_general(a, b, (((0,), (0,)), ((), ())), preferred_element_type=f32)


def cost(flops, nbytes, trans=0):
    return pl.CostEstimate(flops=int(flops), bytes_accessed=int(nbytes), transcendentals=int(trans))


def params(**kw):
    return pltpu.CompilerParams(vmem_limit_bytes=56 * 1024 * 1024, **kw)


def one_hot(ids, base, width):
    column = lax.broadcasted_iota(jnp.int32, (ids.shape[0], width), 1) + base
    return jnp.where(ids == column, jnp.float32(1.0), jnp.float32(0.0)).astype(bf16)


def lookup_kernel(rows, ids_ref, w_ref, out_ref, acc_ref):
    step = pl.program_id(0)
    w = w_ref[...].astype(bf16)
    total = ids_ref.shape[0]

    @pl.when(step == 0)
    def _():
        acc_ref[...] = jnp.zeros_like(acc_ref)

    for r in range(0, total, rows):
        part = pl.ds(r, rows)
        acc_ref[part, :] += dot_nt(one_hot(ids_ref[part, :], step * EMB_BLOCK, EMB_BLOCK), w)

    @pl.when(step == EMB_STEPS - 1)
    def _():
        out_ref[...] = acc_ref[...].astype(bf16)


def lookup(ids, w_vocab):
    total, rows = ids.shape[0], w_vocab.shape[0]
    return pl.pallas_call(
        functools.partial(lookup_kernel, min(512, total)),
        grid=(EMB_STEPS,),
        in_specs=[
            pl.BlockSpec((total, 1), lambda i: (0, 0)),
            pl.BlockSpec((pl.Element(rows), pl.Element(EMB_BLOCK)), lambda i: (0, (EMB_AT // 128 + EMB_BLOCK // 128 * i) * 128)),
        ],
        out_specs=pl.BlockSpec((total, rows), lambda i: (0, 0)),
        out_shape=jax.ShapeDtypeStruct((total, rows), bf16),
        scratch_shapes=[pltpu.VMEM((total, rows), f32)],
        compiler_params=params(),
        cost_estimate=cost(2 * total * rows * EMB_W, rows * EMB_W * 4),
        name="embed_lookup",
    )(ids, w_vocab)


def embed_grad_kernel(rows, ids_ref, dxt_ref, out_ref, sq_ref):
    step = pl.program_id(0)
    total = ids_ref.shape[0]
    acc = jnp.zeros(out_ref.shape, f32)
    for r in range(0, total, rows):
        hot = one_hot(ids_ref[pl.ds(r, rows), :], step * EMB_BLOCK, EMB_BLOCK)
        acc = acc + dot_nn(dxt_ref[:, pl.ds(r, rows)], hot)
    out_ref[...] = acc.astype(bf16)
    square = acc * acc
    lanes = sum(square[:, k : k + 128] for k in range(0, EMB_BLOCK, 128))
    part = sum(lanes[k : k + 8] for k in range(0, lanes.shape[0], 8))

    @pl.when(step == 0)
    def _():
        sq_ref[...] = jnp.zeros_like(sq_ref)

    sq_ref[...] += part


def embed_grad(ids, dxt):
    rows, total = dxt.shape
    return pl.pallas_call(
        functools.partial(embed_grad_kernel, min(512, total)),
        grid=(EMB_STEPS,),
        in_specs=[
            pl.BlockSpec((total, 1), lambda i: (0, 0)),
            pl.BlockSpec((rows, total), lambda i: (0, 0)),
        ],
        out_specs=[
            pl.BlockSpec((rows, EMB_BLOCK), lambda i: (0, i)),
            pl.BlockSpec((8, 128), lambda i: (0, 0)),
        ],
        out_shape=[
            jax.ShapeDtypeStruct((rows, EMB_W), bf16),
            jax.ShapeDtypeStruct((8, 128), f32),
        ],
        compiler_params=params(),
        cost_estimate=cost(2 * total * rows * EMB_W, rows * EMB_W * 2),
        name="embed_grad",
    )(ids, dxt)


def partner(x):
    width = x.shape[1]
    lane = lax.broadcasted_iota(jnp.int32, x.shape, 1)
    return jnp.where(lane % HD < HD // 2, pltpu.roll(x, width - HD // 2, 1), pltpu.roll(x, HD // 2, 1))


def qkv_kernel(a_ref, w_ref, cos_ref, sin_ref, q_ref, kv_ref):
    raw = dot_nn(a_ref[...], w_ref[...])
    cosine, sine = cos_ref[...], sin_ref[...]
    for j in range(0, QG, 128):
        x = raw[:, j : j + 128]
        rot = (x * cosine + partner(x) * sine).astype(bf16)
        q_ref[:, j : j + 128] = rot * jnp.asarray(HD**-0.5, bf16)
    x = raw[:, QG:]
    lane = lax.broadcasted_iota(jnp.int32, x.shape, 1)
    kv_ref[...] = jnp.where(lane < HD, x * cosine + partner(x) * sine, x).astype(bf16)


def qkv(a1, w_in, cosine, sine):
    tok = a1.shape[0]
    return pl.pallas_call(
        qkv_kernel,
        grid=(1,),
        in_specs=[
            pl.BlockSpec((tok, D), lambda i: (0, 0)),
            pl.BlockSpec((D, ATTN_IN), lambda i: (0, 0)),
            pl.BlockSpec((tok, 128), lambda i: (0, 0)),
            pl.BlockSpec((tok, 128), lambda i: (0, 0)),
        ],
        out_specs=[
            pl.BlockSpec((tok, QG), lambda i: (0, 0)),
            pl.BlockSpec((tok, 2 * HD), lambda i: (0, 0)),
        ],
        out_shape=[
            jax.ShapeDtypeStruct((tok, QG), bf16),
            jax.ShapeDtypeStruct((tok, 2 * HD), bf16),
        ],
        compiler_params=params(),
        cost_estimate=cost(2 * tok * D * ATTN_IN, 2 * D * ATTN_IN + 2 * tok * D),
        name="qkv",
    )(a1, w_in, cosine, sine)


def split_kv(kv_ref, parts_ref):
    kv = kv_ref[...].reshape(-1, 2 * HD).astype(f32)
    lane = lax.broadcasted_iota(jnp.int32, kv.shape, 1)
    swapped = pltpu.roll(kv, HD, 1)
    zero = jnp.zeros_like(kv)
    low = lane < HD
    parts_ref[0] = jnp.where(low, kv, zero).astype(bf16)
    parts_ref[1] = jnp.where(low, zero, swapped).astype(bf16)
    parts_ref[2] = jnp.where(low, swapped, zero).astype(bf16)
    parts_ref[3] = jnp.where(low, zero, kv).astype(bf16)


def attn_kernel(q_ref, kv_ref, qpos_ref, kpos_ref, o_ref, lse_ref, parts_ref):
    @pl.when(pl.program_id(1) == 0)
    def _():
        split_kv(kv_ref, parts_ref)

    q = q_ref[...]
    allowed = kpos_ref[...] <= qpos_ref[...]
    out = None
    norms = []
    for g in range(2):
        s = jnp.where(allowed, dot_nt(q, parts_ref[g]), NEG)
        top = jnp.max(s, axis=1, keepdims=True)
        p = jnp.exp(s - top)
        total = jnp.sum(p, axis=1, keepdims=True)
        p = p * (1.0 / total)
        norms.append(top + jnp.log(total))
        part = dot_nn(p.astype(bf16), parts_ref[2 + g])
        out = part if out is None else out + part
    o_ref[...] = out.astype(bf16)
    lane = lax.broadcasted_iota(jnp.int32, q.shape, 1)
    lse_ref[0, 0] = jnp.where(lane == 0, norms[0], norms[1]).T[:8]


def attn(q, kv_every, qpos, kpos):
    n_ctx, _, seq_tok, _ = kv_every.shape
    keys = n_ctx * seq_tok
    pairs = QG // 128
    return pl.pallas_call(
        attn_kernel,
        grid=(SEQS, pairs),
        in_specs=[
            pl.BlockSpec((seq_tok, 128), lambda s, p: (s, p)),
            pl.BlockSpec((n_ctx, 1, seq_tok, 2 * HD), lambda s, p: (0, s, 0, 0)),
            pl.BlockSpec((seq_tok, 1), lambda s, p: (0, 0)),
            pl.BlockSpec((1, keys), lambda s, p: (0, 0)),
        ],
        out_specs=[
            pl.BlockSpec((seq_tok, 128), lambda s, p: (s, p)),
            pl.BlockSpec((1, 1, 8, seq_tok), lambda s, p: (s, p, 0, 0)),
        ],
        out_shape=[
            jax.ShapeDtypeStruct((SEQS * seq_tok, QG), bf16),
            jax.ShapeDtypeStruct((SEQS, pairs, 8, seq_tok), f32),
        ],
        scratch_shapes=[pltpu.VMEM((4, keys, 2 * HD), bf16)],
        compiler_params=params(),
        cost_estimate=cost(
            8 * SEQS * seq_tok * keys * QG, 4 * SEQS * seq_tok * QG, SEQS * GROUP * seq_tok * keys
        ),
        name="attn_fwd",
    )(q, kv_every, qpos.reshape(seq_tok, 1), kpos.reshape(1, keys))


def attn_back_kernel(
    pairs, q_ref, do_ref, o_ref, lse_ref, kv_ref, qpos_ref, kpos_ref, cos_ref, sin_ref, dq_ref, dkv_ref, parts_ref, acc_ref
):
    pair = pl.program_id(1)

    @pl.when(pair == 0)
    def _():
        split_kv(kv_ref, parts_ref)
        acc_ref[...] = jnp.zeros_like(acc_ref)

    q = q_ref[...]
    do = do_ref[...]
    allowed = kpos_ref[...] <= qpos_ref[...]
    dq = None
    shares = (do.astype(f32) * o_ref[...].astype(f32)).T
    for g in range(2):
        s = jnp.where(allowed, dot_nt(parts_ref[g], q), NEG)
        p = jnp.exp(s - lse_ref[0, 0, g : g + 1])
        dp = dot_nt(parts_ref[2 + g], do)
        delta = jnp.sum(shares[g * HD : (g + 1) * HD], axis=0, keepdims=True)
        ds = (p * (dp - delta)).astype(bf16)
        part = dot_tn(ds, parts_ref[g])
        dq = part if dq is None else dq + part
        acc_ref[g] += dot_nn(ds, q)
        acc_ref[2 + g] += dot_nn(p.astype(bf16), do)
    dq = dq * (HD**-0.5)
    dq_ref[...] = (dq * cos_ref[...] - partner(dq) * sin_ref[...]).astype(bf16)

    @pl.when(pair == pairs - 1)
    def _():
        lane = lax.broadcasted_iota(jnp.int32, acc_ref.shape[1:], 1)
        grad_k = acc_ref[0] + pltpu.roll(acc_ref[1], HD, 1)
        grad_v = pltpu.roll(acc_ref[2], HD, 1) + acc_ref[3]
        dkv_ref[...] = jnp.where(lane < HD, grad_k, grad_v).astype(bf16).reshape(dkv_ref.shape)


def attn_back(q, do, o, lse, kv_every, qpos, kpos, cosine, sine):
    n_ctx, _, seq_tok, _ = kv_every.shape
    keys = n_ctx * seq_tok
    pairs = QG // 128
    return pl.pallas_call(
        functools.partial(attn_back_kernel, pairs),
        grid=(SEQS, pairs),
        in_specs=[
            pl.BlockSpec((seq_tok, 128), lambda s, p: (s, p)),
            pl.BlockSpec((seq_tok, 128), lambda s, p: (s, p)),
            pl.BlockSpec((seq_tok, 128), lambda s, p: (s, p)),
            pl.BlockSpec((1, 1, 8, seq_tok), lambda s, p: (s, p, 0, 0)),
            pl.BlockSpec((n_ctx, 1, seq_tok, 2 * HD), lambda s, p: (0, s, 0, 0)),
            pl.BlockSpec((1, seq_tok), lambda s, p: (0, 0)),
            pl.BlockSpec((keys, 1), lambda s, p: (0, 0)),
            pl.BlockSpec((seq_tok, 128), lambda s, p: (s, 0)),
            pl.BlockSpec((seq_tok, 128), lambda s, p: (s, 0)),
        ],
        out_specs=[
            pl.BlockSpec((seq_tok, 128), lambda s, p: (s, p)),
            pl.BlockSpec((n_ctx, 1, seq_tok, 2 * HD), lambda s, p: (0, s, 0, 0)),
        ],
        out_shape=[
            jax.ShapeDtypeStruct((SEQS * seq_tok, QG), bf16),
            jax.ShapeDtypeStruct(kv_every.shape, bf16),
        ],
        scratch_shapes=[
            pltpu.VMEM((4, keys, 2 * HD), bf16),
            pltpu.VMEM((4, keys, 2 * HD), f32),
        ],
        compiler_params=params(),
        cost_estimate=cost(
            20 * SEQS * seq_tok * keys * QG, 8 * SEQS * seq_tok * QG, SEQS * GROUP * seq_tok * keys
        ),
        name="attn_bwd",
    )(q, do, o, lse, kv_every, qpos.reshape(1, seq_tok), kpos.reshape(keys, 1), cosine, sine)


def kv_back_kernel(parts_ref, cos_ref, sin_ref, out_ref):
    x = parts_ref[0].astype(f32)
    for k in range(1, parts_ref.shape[0]):
        x = x + parts_ref[k].astype(f32)
    lane = lax.broadcasted_iota(jnp.int32, x.shape, 1)
    out_ref[...] = jnp.where(lane < HD, x * cos_ref[...] - partner(x) * sin_ref[...], x).astype(bf16)


def kv_back(parts, cosine, sine):
    return pl.pallas_call(
        kv_back_kernel,
        out_shape=jax.ShapeDtypeStruct(parts.shape[1:], bf16),
        compiler_params=params(),
        name="kv_bwd",
    )(parts, cosine, sine)


def head_cast_kernel(block, w_ref, *outs):
    column = lax.broadcasted_iota(jnp.int32, w_ref.shape, 1) + pl.program_id(0) * block
    w = jnp.where(column < VG, w_ref[...], 0.0).astype(bf16)
    count = w.shape[0] // len(outs)
    for k, out_ref in enumerate(outs):
        out_ref[...] = w[k * count : (k + 1) * count]


def head_cast(w_vocab, width, parts):
    rows = w_vocab.shape[0]
    block = 1024
    return pl.pallas_call(
        functools.partial(head_cast_kernel, block),
        grid=(width // block,),
        in_specs=[pl.BlockSpec((rows, block), lambda i: (0, i))],
        out_specs=[pl.BlockSpec((rows // parts, block), lambda i: (0, i))] * parts,
        out_shape=[jax.ShapeDtypeStruct((rows // parts, width), bf16)] * parts,
        compiler_params=params(),
        cost_estimate=cost(rows * width, rows * width * 6),
        name="head_cast",
    )(w_vocab)


def joined(pieces, parts):
    for k in range(0, len(pieces), parts):
        run = [piece[...] for piece in pieces[k : k + parts]]
        yield k // parts, run[0] if parts == 1 else jnp.concatenate(run, axis=0)


def partial_kernel(parts, at_ref, x_ref, *refs):
    pieces, out_ref = refs[:-1], refs[-1]
    logits = None
    for k, w in joined(pieces, parts):
        at = pl.multiple_of(at_ref[k], 128)
        term = dot_nn(x_ref[:, pl.ds(at, w.shape[0])], w)
        logits = term if logits is None else logits + term
    out_ref[...] = logits


def head_partial(x, pieces, at):
    tok = x.shape[0]
    width = pieces[0].shape[1]
    rows = sum(piece.shape[0] for piece in pieces)
    block = 1024
    return pl.pallas_call(
        functools.partial(partial_kernel, len(pieces) // at.shape[0]),
        grid=(width // block,),
        in_specs=[
            pl.BlockSpec(memory_space=pltpu.SMEM),
            pl.BlockSpec((tok, D), lambda i: (0, 0)),
        ]
        + [pl.BlockSpec((piece.shape[0], block), lambda i: (0, i)) for piece in pieces],
        out_specs=pl.BlockSpec((tok, block), lambda i: (0, i)),
        out_shape=jax.ShapeDtypeStruct((tok, width), f32),
        compiler_params=params(),
        cost_estimate=cost(2 * tok * rows * width, 2 * rows * width + 4 * tok * width),
        name="head_partial",
    )(at, x, *pieces)


def logits_kernel(steps, parts, based, at_ref, x_ref, slot_ref, *refs):
    base = refs[:based]
    pieces, (out_ref, stats_ref, top_ref, total_ref, label_ref) = refs[based:-5], refs[-5:]
    step = pl.program_id(0)
    block = out_ref.shape[1]

    @pl.when(step == 0)
    def _():
        top_ref[...] = jnp.full_like(top_ref, NEG)
        total_ref[...] = jnp.zeros_like(total_ref)
        label_ref[...] = jnp.zeros_like(label_ref)

    logits = base[0][...] if based else None
    for k, w in joined(pieces, parts):
        at = pl.multiple_of(at_ref[k], 128)
        term = dot_nn(x_ref[:, pl.ds(at, w.shape[0])], w)
        logits = term if logits is None else logits + term
    column = lax.broadcasted_iota(jnp.int32, logits.shape, 1) + step * block
    logits = jnp.where(column < VG, logits, NEG)
    out_ref[...] = logits
    top = top_ref[...]
    new_top = jnp.maximum(top, jnp.max(logits, axis=1, keepdims=True))
    total_ref[...] = total_ref[...] * jnp.exp(top - new_top) + jnp.sum(
        jnp.exp(logits - new_top), axis=1, keepdims=True
    )
    top_ref[...] = new_top
    label_ref[...] += jnp.sum(jnp.where(column == slot_ref[...], logits, 0.0), axis=1, keepdims=True)

    @pl.when(step == steps - 1)
    def _():
        lane = lax.broadcasted_iota(jnp.int32, (x_ref.shape[0], 128), 1)
        packed = jnp.where(lane == 0, top_ref[...], jnp.where(lane == 1, total_ref[...], label_ref[...]))
        stats_ref[...] = packed.T[:8]


def head_logits(x, slots, base, pieces, at):
    tok = x.shape[0]
    rows = sum(piece.shape[0] for piece in pieces)
    width = pieces[0].shape[1]
    block = 1024
    steps = width // block
    return pl.pallas_call(
        functools.partial(logits_kernel, steps, len(pieces) // at.shape[0], len(base)),
        grid=(steps,),
        in_specs=[
            pl.BlockSpec(memory_space=pltpu.SMEM),
            pl.BlockSpec((tok, D), lambda i: (0, 0)),
            pl.BlockSpec((tok, 1), lambda i: (0, 0)),
        ]
        + [pl.BlockSpec((tok, block), lambda i: (0, i)) for _ in base]
        + [pl.BlockSpec((piece.shape[0], block), lambda i: (0, i)) for piece in pieces],
        out_specs=[
            pl.BlockSpec((tok, block), lambda i: (0, i)),
            pl.BlockSpec((8, tok), lambda i: (0, 0)),
        ],
        out_shape=[
            jax.ShapeDtypeStruct((tok, width), f32),
            jax.ShapeDtypeStruct((8, tok), f32),
        ],
        scratch_shapes=[pltpu.VMEM((tok, 1), f32)] * 3,
        compiler_params=params(),
        cost_estimate=cost(2 * tok * rows * width, 2 * rows * width + 8 * tok * width, tok * width),
        name="head_logits",
    )(at, x, slots, *base, *pieces)


def dlogits_kernel(steps, parts, at_ref, logits_ref, values_ref, slot_ref, *refs):
    pieces, (dlog_ref, dx_ref, acc_ref) = refs[:-3], refs[-3:]
    step = pl.program_id(0)
    tok, block = logits_ref.shape
    logits = logits_ref[...]
    lse = values_ref[:, 0:1]
    weight = values_ref[:, 1:2]
    column = lax.broadcasted_iota(jnp.int32, logits.shape, 1) + step * block
    hit = jnp.where(column == slot_ref[...], 1.0, 0.0)
    soft = jnp.exp(logits - lse)
    dlog = (weight * ((1.0 + 2.0 * z_weight * lse) * soft - hit)).astype(bf16)
    part = dlog_ref.shape[2]
    for k in range(dlog_ref.shape[0]):
        dlog_ref[k] = dlog[:, k * part : (k + 1) * part]

    @pl.when(step == 0)
    def _():
        acc_ref[...] = jnp.zeros_like(acc_ref)

    for k, w in joined(pieces, parts):
        at = pl.multiple_of(at_ref[k], 128)
        acc_ref[pl.ds(at, w.shape[0]), :] += dot_nt(w, dlog)

    @pl.when(step == steps - 1)
    def _():
        for k in range(0, acc_ref.shape[0], 256):
            dx_ref[:, k : k + 256] = acc_ref[k : k + 256, :].T.astype(bf16)


def head_dlogits(logits, values, slots, pieces, at, part):
    tok, width = logits.shape
    block = 1024
    steps = width // block
    return pl.pallas_call(
        functools.partial(dlogits_kernel, steps, len(pieces) // at.shape[0]),
        grid=(steps,),
        in_specs=[
            pl.BlockSpec(memory_space=pltpu.SMEM),
            pl.BlockSpec((tok, block), lambda i: (0, i)),
            pl.BlockSpec((tok, values.shape[1]), lambda i: (0, 0)),
            pl.BlockSpec((tok, 1), lambda i: (0, 0)),
        ]
        + [pl.BlockSpec((piece.shape[0], block), lambda i: (0, i)) for piece in pieces],
        out_specs=[
            pl.BlockSpec((block // part, tok, part), lambda i: (i, 0, 0)),
            pl.BlockSpec((tok, D), lambda i: (0, 0)),
        ],
        out_shape=[
            jax.ShapeDtypeStruct((width // part, tok, part), bf16),
            jax.ShapeDtypeStruct((tok, D), bf16),
        ],
        scratch_shapes=[pltpu.VMEM((D, tok), f32)],
        compiler_params=params(),
        cost_estimate=cost(2 * tok * D * width, 2 * D * width + 6 * tok * width, tok * width),
        name="head_dlogits",
    )(at, logits, values, slots, *pieces)


def outer_kernel(a_ref, da_ref, b_ref, db_ref, out_ref, *, a_steps):
    step = pl.program_id(0)

    @pl.when(step < a_steps)
    def _():
        out_ref[...] = dot_tn(a_ref[...], da_ref[...]).astype(bf16)

    @pl.when(step >= a_steps)
    def _():
        out_ref[...] = dot_tn(b_ref[...], db_ref[...]).astype(bf16)


def outer_pair(a, da, b, db, block, rows, name):
    tok = a.shape[0]
    a_steps, b_steps = da.shape[1] // block, db.shape[1] // block
    width = da.shape[1] + db.shape[1]
    return pl.pallas_call(
        functools.partial(outer_kernel, a_steps=a_steps),
        grid=(a_steps + b_steps, D // rows),
        in_specs=[
            pl.BlockSpec((tok, rows), lambda i, j: (0, j)),
            pl.BlockSpec((tok, block), lambda i, j: (0, jnp.minimum(i, a_steps - 1))),
            pl.BlockSpec((tok, rows), lambda i, j: (0, j)),
            pl.BlockSpec((tok, block), lambda i, j: (0, jnp.maximum(i - a_steps, 0))),
        ],
        out_specs=pl.BlockSpec((rows, block), lambda i, j: (j, i)),
        out_shape=jax.ShapeDtypeStruct((D, width), bf16),
        compiler_params=params(),
        cost_estimate=cost(2 * tok * D * width, 2 * D * width + 4 * tok * D),
        name=name,
    )(a, da, b, db)


def update_piece(factor, rate, grad, w_ref, m_ref, a_ref, outs, columns):
    new_ref, moment_ref, average_ref, copy_ref = outs
    grad = factor * grad
    moment = momentum_rate * m_ref[:, columns] + grad
    new = w_ref[:, columns] - rate * (grad + momentum_rate * moment)
    new_ref[:, columns] = new
    moment_ref[:, columns] = moment
    average_ref[:, columns] = average_rate * a_ref[:, columns] + (1.0 - average_rate) * new
    copy_ref[:, columns] = new.astype(bf16)


def layer_update_kernel(spreads, factor_ref, *refs):
    grads, (w_ref, m_ref, a_ref), outs = refs[:-7], refs[-7:-4], refs[-4:]
    factor = factor_ref[0, 0]
    for source, inner, outer, width, spread in spreads:
        grad = grads[source][:, inner : inner + width].astype(f32)
        update_piece(factor, BASE * spread, grad, w_ref, m_ref, a_ref, outs, slice(outer, outer + width))


def vocab_update_kernel(part, factor_ref, head_ref, embed_ref, w_ref, m_ref, a_ref, *outs):
    factor = factor_ref[0, 0]
    head_rate = BASE * 2.0 * D**-0.5
    for k in range(head_ref.shape[0]):
        low, high = k * part, min((k + 1) * part, EMB_AT)
        if low >= high:
            continue
        grad = head_ref[k, :, : high - low].astype(f32)
        update_piece(factor, head_rate, grad, w_ref, m_ref, a_ref, outs, slice(low, high))
    edge = EMB_AT - EMB_AT // part * part
    grad_head = head_ref[EMB_AT // part, :, edge : edge + 128].astype(f32)
    grad_embed = embed_ref[:, :128].astype(f32)
    own = lax.broadcasted_iota(jnp.int32, grad_head.shape, 1) < VG - EMB_AT
    update_piece(
        factor,
        jnp.where(own, head_rate, BASE),
        jnp.where(own, grad_head, grad_embed),
        w_ref,
        m_ref,
        a_ref,
        outs,
        slice(EMB_AT, EMB_AT + 128),
    )
    for low in range(128, EMB_W, 1024):
        high = min(low + 1024, EMB_W)
        grad = embed_ref[:, low:high].astype(f32)
        update_piece(factor, BASE, grad, w_ref, m_ref, a_ref, outs, slice(EMB_AT + low, EMB_AT + high))


def call_update(kernel, factor, grads, grad_specs, w, m, a, rows, name, span=None, earlier=()):
    total, width = w.shape
    first, steps = span or (0, total // rows)
    block = pl.BlockSpec((rows, width), lambda i: (first + i, 0))
    count = 4 + len(grads)
    inner = kernel
    if earlier:

        def inner(*refs):
            kernel(*refs[:count], *refs[count + len(earlier) :])

    return pl.pallas_call(
        inner,
        grid=(steps,),
        in_specs=[pl.BlockSpec(memory_space=pltpu.SMEM)]
        + grad_specs
        + [block] * 3
        + [pl.BlockSpec(memory_space=pl.ANY)] * len(earlier),
        out_specs=[block] * 4,
        out_shape=[jax.ShapeDtypeStruct(w.shape, f32)] * 3 + [jax.ShapeDtypeStruct(w.shape, bf16)],
        input_output_aliases={count + k: k for k in range(len(earlier))},
        compiler_params=params(),
        cost_estimate=cost(10 * steps * rows * width, 28 * steps * rows * width),
        name=name,
    )(factor.reshape(1, 1), *grads, w, m, a, *earlier)


def norm_parts(x):
    scale = lax.rsqrt(jnp.mean(x * x, axis=-1, keepdims=True) + eps)
    return x * scale, scale


def norm_back(dy, unit, scale, gain):
    scaled = dy * gain
    dx = scale * (scaled - unit * jnp.mean(scaled * unit, axis=-1, keepdims=True))
    return dx, jnp.sum(dy * unit, axis=0)


def local(
    token_ids,
    labels,
    answer_mask,
    pair_map,
    w_layer,
    w_vocab,
    gains,
    mom_layer,
    mom_vocab,
    mom_gains,
    avg_layer,
    avg_vocab,
    avg_gains,
):
    n_ctx = lax.axis_size("ctx")
    n_head = lax.axis_size("head")
    place = lax.axis_index("ctx")
    shard = lax.axis_index("head")
    tok = token_ids.shape[0]
    rows = w_layer.shape[0]
    seq_tok = tok // SEQS
    span = seq_tok // 2
    chunk = seq_tok // n_head
    own = SEQS * chunk
    length = n_ctx * seq_tok
    part = -(-VG // (n_ctx * 128)) * 128

    def turn(x, axis):
        return lax.dynamic_slice_in_dim(
            jnp.concatenate([x, x], axis), shard * chunk, seq_tok, axis
        )

    def turn_back(x, axis):
        return lax.dynamic_slice_in_dim(
            jnp.concatenate([x, x], axis), seq_tok - shard * chunk, seq_tok, axis
        )

    def head_scatter(x):
        sums = x[:, 0].astype(f32)
        for s in range(1, n_head):
            sent = lax.ppermute(x[:, s], "head", [(i, (i + s) % n_head) for i in range(n_head)])
            sums = sums + sent.astype(f32)
        return sums

    def head_gather(x):
        pieces = [x]
        for s in range(1, n_head):
            pieces.append(lax.ppermute(x, "head", [(i, (i - s) % n_head) for i in range(n_head)]))
        return jnp.stack(pieces, axis=1)

    def sum_own(partial):
        split = partial.astype(bf16).reshape(SEQS, n_head, chunk, D)
        return head_scatter(split).reshape(own, D)

    def spread_all(x):
        return head_gather(x.astype(bf16).reshape(SEQS, chunk, D)).reshape(tok, D)

    layer_b = w_layer.astype(bf16)
    edge = ATTN_IN + QG
    w_attn = lax.all_gather(layer_b[:, :edge], "ctx", axis=0, tiled=True)
    w_ff = lax.all_gather(layer_b[:, edge:], "ctx", axis=0, tiled=True)
    w_out, w_gu, w_down = w_attn[:, ATTN_IN:], w_ff[:, : 2 * FFG], w_ff[:, 2 * FFG :]
    corners = n_ctx == 8
    head_own = head_cast(w_vocab, n_ctx * part, 2 if corners else 1)

    def swap(x, bit):
        return lax.ppermute(x, "ctx", [(i, i ^ bit) for i in range(n_ctx)])

    gain_own = lax.reduce_precision(gains, exponent_bits=8, mantissa_bits=7).T.reshape(3 * rows)
    every = jnp.concatenate([token_ids.astype(f32), answer_mask.astype(f32), gain_own])
    every = lax.all_gather(every, "ctx")
    ids_all = every[:, :tok].astype(jnp.int32).reshape(n_ctx, SEQS, seq_tok)
    ids_all = turn(ids_all, 2).reshape(n_ctx * tok)
    count = jnp.sum(every[:, tok : 2 * tok])
    gain_rows = jnp.moveaxis(every[:, 2 * tok :].reshape(n_ctx, 3, rows), 1, 0).reshape(3, D)
    labels_own = turn(labels.reshape(SEQS, seq_tok), 1).reshape(tok)
    mask_own = turn(answer_mask.reshape(SEQS, seq_tok), 1).reshape(tok)

    offset_id = shard * VG
    local_ids = ids_all - offset_id
    inside = (local_ids >= 0) & (local_ids < VG)
    slots = jnp.where(inside, local_ids + (VG - EMB_AT), -1).reshape(-1, 1)
    picked = lookup(slots, w_vocab).reshape(n_ctx * SEQS, n_head, chunk, rows)
    picked = head_scatter(picked).astype(bf16).reshape(n_ctx * own, rows)
    x0 = lax.all_to_all(picked, "ctx", 0, 1, tiled=True).astype(f32)

    unit0, scale0 = norm_parts(x0)
    a1 = spread_all(unit0 * gain_rows[0])
    if corners:
        over = [swap(x, 1) for x in head_own]
        a1, low, high, over_low, over_high = lax.optimization_barrier((a1, *head_own, *over))
    row = (jnp.arange(seq_tok, dtype=jnp.int32) + shard * chunk) % seq_tok

    def positions(index):
        index = index[:, None]
        at = jnp.where(row // span == 0, index, 2 * n_ctx - 1 - index)
        return at * span + row % span

    qpos = positions(pair_map[place][None])[0]
    kpos = positions(pair_map).reshape(length)
    half = HD // 2
    inverse = 10000.0 ** (-2.0 * np.arange(half) / HD)
    ramp = np.clip((2048.0 * inverse / (2.0 * math.pi) - 1.0) / 31.0, 0.0, 1.0)
    freq = np.tile(((1.0 - ramp) * inverse / 4.0 + ramp * inverse).astype(np.float32), 128 // half)
    sign = np.where(np.arange(128) % HD < half, -1.0, 1.0).astype(np.float32)
    mscale = 0.1 * math.log(4.0) + 1.0
    angle = jnp.tile(qpos, SEQS).astype(f32)[:, None] * freq[None, :]
    cosine = jnp.cos(angle) * mscale
    sine = jnp.sin(angle) * (mscale * sign)[None, :]
    q, kv_own = qkv(a1, w_attn, cosine, sine)
    kv_every = lax.all_gather(kv_own, "ctx").reshape(n_ctx, SEQS, seq_tok, 2 * HD)
    if corners:
        kv_every, low, high = lax.optimization_barrier((kv_every, low, high))
        y_low, x_high, x_low, y_high = swap(low, 4), swap(high, 2), swap(low, 2), swap(high, 4)
    attn_b, attn_lse = attn(q, kv_every, qpos, kpos)
    x1 = x0 + sum_own(dot_nt(attn_b, w_out))

    unit1, scale1 = norm_parts(x1)
    a2 = spread_all(unit1 * gain_rows[1])
    if corners:
        a2, y_low, x_high = lax.optimization_barrier((a2, y_low, x_high))
        far_low, far_high = swap(y_low, 2), swap(x_high, 4)
    gate_up = dot_nn(a2, w_gu)

    def glu(values):
        return jax.nn.silu(values[:, :FFG]) * values[:, FFG:]

    hidden_f, glu_back = jax.vjp(glu, gate_up)
    hidden_b = hidden_f.astype(bf16)
    second = sum_own(dot_nt(hidden_b, w_down))
    if corners:
        second, x_low, y_high = lax.optimization_barrier((second, x_low, y_high))
    x2 = x1 + second

    unit2, scale2 = norm_parts(x2)
    final_b = spread_all(unit2 * gain_rows[2])
    label_ids = labels_own - offset_id
    label_slots = jnp.where((label_ids >= 0) & (label_ids < VG), label_ids, -1).reshape(tok, 1)
    if corners:
        near = [low, high, over_low, over_high, x_low, x_high, y_low, y_high]
        head_at = jnp.stack([(place ^ bits) * rows for bits in (0, 1, 2, 4, 3, 5, 6, 7)])
        base = head_partial(final_b, near, head_at[:4])
        base, far_low, far_high = lax.optimization_barrier((base, far_low, far_high))
        far = [swap(x, 1) for x in (x_low, x_high, y_low, y_high)]
        far += [far_low, far_high, swap(far_low, 1), swap(far_high, 1)]
        head_pieces = near + far
        logits, stats = head_logits(final_b, label_slots, [base], far, head_at[4:])
    else:
        head_pieces = [lax.all_gather(head_own[0], "ctx", axis=0, tiled=True)]
        head_at = jnp.zeros((1,), jnp.int32)
        logits, stats = head_logits(final_b, label_slots, [], head_pieces, head_at)
    stats, final_late = lax.optimization_barrier((stats, final_b))
    pieces = [stats]
    for s in range(1, n_head):
        sent = lax.ppermute(stats, "head", [(i, (i - s) % n_head) for i in range(n_head)])
        sent = sent.reshape(8, SEQS, n_head, chunk)
        pieces.append(jnp.roll(sent, s, axis=2).reshape(8, tok))
    doubled = jnp.stack(pieces + pieces)
    stats = lax.dynamic_slice_in_dim(doubled, n_head - shard, n_head, 0)
    top = jnp.max(stats[:, 0], axis=0)
    total = jnp.sum(stats[:, 1] * jnp.exp(stats[:, 0] - top), axis=0)
    lse = top + jnp.log(total)
    weight = mask_own.astype(f32) / count
    terms = weight * (lse - jnp.sum(stats[:, 2], axis=0) + z_weight * lse * lse)
    loss_part = jnp.sum(turn_back(terms.reshape(SEQS, seq_tok), 1))
    values = jnp.stack([lse, weight] + [weight] * 6).T
    dlog_b, d_final = head_dlogits(logits, values, label_slots, head_pieces, head_at, part)
    final_all = lax.all_gather(final_late, "ctx", axis=0, tiled=True)
    dlog_all = lax.all_to_all(dlog_b, "ctx", 0, 0, tiled=True).reshape(n_ctx * tok, part)

    dx2, d_gain2 = norm_back(sum_own(d_final), unit2, scale2, gain_rows[2])
    dyf_b = spread_all(dx2)
    d_hidden = dot_nn(dyf_b, w_down)
    d_gate_up_b = glu_back(d_hidden)[0].astype(bf16)
    d_second = sum_own(dot_nt(d_gate_up_b, w_gu))
    d_ff = outer_pair(a2, d_gate_up_b, dyf_b, hidden_b, FFG, 512, "ff_weight_grad")
    d_second, d_ff, dlog_all, final_all = lax.optimization_barrier((d_second, d_ff, dlog_all, final_all))
    g_ff = lax.psum_scatter(d_ff, "ctx", scatter_dimension=0, tiled=True)
    dx1_norm, d_gain1 = norm_back(d_second, unit1, scale1, gain_rows[1])
    dx1 = dx2 + dx1_norm
    d_head = dot_tn(final_all, dlog_all)
    head_sq = jnp.sum(d_head * d_head)
    d_head = d_head.astype(bf16).reshape(n_ctx, rows, part)
    dya_b, d_head_a, d_head_b = lax.optimization_barrier(
        (spread_all(dx1), d_head[:, : rows // 2], d_head[:, rows // 2 :])
    )
    d_attn_b = dot_nn(dya_b, w_out).astype(bf16)
    d_q, d_kv = attn_back(q, d_attn_b, attn_b, attn_lse, kv_every, qpos, kpos, cosine, sine)
    d_out = dot_tn(dya_b, attn_b).astype(bf16)
    d_kv = lax.all_to_all(d_kv.reshape(n_ctx, tok, 2 * HD), "ctx", 0, 0, tiled=True)
    if corners:
        core, along_x, along_y = place & 1, (place >> 1) & 1, place >> 2

        def total(kept, sent):
            return kept.astype(f32) + sent.astype(f32)

        def split(x, mine, axis, bit):
            kept = lax.dynamic_index_in_dim(x, mine, axis, keepdims=False)
            return kept, swap(lax.dynamic_index_in_dim(x, 1 - mine, axis, keepdims=False), bit)

        out_kept, out_sent = split(d_out.reshape(2, 2, 2, rows, QG), core, 2, 1)
    d_raw_b = jnp.concatenate([d_q, kv_back(d_kv, cosine, sine)], axis=1)
    d_first = sum_own(dot_nt(d_raw_b, w_attn[:, :ATTN_IN]))
    d_in = dot_tn(a1, d_raw_b).astype(bf16)
    if corners:
        d_first, d_in, out_sent = lax.optimization_barrier((d_first, d_in, out_sent))
        d_out = total(out_kept, out_sent).astype(bf16)
        in_kept, in_sent = split(d_in.reshape(2, 2, 2, rows, ATTN_IN), core, 2, 1)
    dx0_norm, d_gain0 = norm_back(d_first, unit0, scale0, gain_rows[0])
    dx0 = dx1 + dx0_norm

    extra = jnp.pad(jnp.stack([d_gain0, d_gain1, d_gain2]), ((0, 13), (0, 0)))
    moved = lax.all_to_all(jnp.concatenate([dx0, extra]).astype(bf16), "ctx", 1, 0, tiled=True)
    if corners:
        moved, in_sent, d_out = lax.optimization_barrier((moved, in_sent, d_out))
        d_in = total(in_kept, in_sent).astype(bf16)
        in_kept, in_sent = split(d_in, along_x, 1, 2)
        out_kept, out_sent = split(d_out, along_y, 0, 4)
        d_in, d_out = total(in_kept, in_sent).astype(bf16), total(out_kept, out_sent).astype(bf16)
        in_kept, in_sent = split(d_in, along_y, 0, 4)
        out_kept, out_sent = split(d_out, along_x, 0, 2)
        d_head_a, in_sent, out_sent = lax.optimization_barrier((d_head_a, in_sent, out_sent))
        g_in, g_out = total(in_kept, in_sent), total(out_kept, out_sent)
    else:
        moved, d_head_a, d_in, d_out, g_ff = lax.optimization_barrier((moved, d_head_a, d_in, d_out, g_ff))
        g_in, g_out = (
            lax.psum_scatter(x, "ctx", scatter_dimension=0, tiled=True).astype(f32) for x in (d_in, d_out)
        )
    g_head_a = lax.all_to_all(d_head_a, "ctx", 0, 0, tiled=True)
    moved = moved.reshape(n_ctx, own + 16, rows)
    gain_part = jnp.sum(moved[:, own:].astype(f32), axis=0).astype(bf16)
    moved = jnp.concatenate([moved[:, :own].reshape(n_ctx * own, rows), gain_part])
    pieces = [moved]
    for s in range(1, n_head):
        pieces.append(lax.ppermute(moved, "head", [(i, (i - s) % n_head) for i in range(n_head)]))
    gain_all = jnp.stack([piece[n_ctx * own :] for piece in pieces + pieces])
    gain_all = lax.dynamic_slice_in_dim(gain_all, n_head - shard, n_head, 0)
    grad_gain = jnp.sum(gain_all.astype(f32), axis=0)[:3].T
    dx0_all = jnp.stack([piece[: n_ctx * own].reshape(n_ctx * SEQS, chunk, rows) for piece in pieces], axis=1)
    g_embed, embed_sq = embed_grad(slots, dx0_all.reshape(n_ctx * tok, rows).T)

    squares = (
        jnp.sum(jnp.square(g_ff.astype(f32)))
        + jnp.sum(jnp.square(g_in))
        + jnp.sum(jnp.square(g_out))
        + head_sq
        + jnp.sum(embed_sq)
        + jnp.sum(grad_gain * grad_gain) / n_head
    )
    squares = jnp.full((8, 128), squares)
    if n_head & (n_head - 1):
        squares = jnp.sum(lax.all_gather(squares, "head"), axis=0)
    else:
        level = [squares]
        for s in range(1, n_head):
            level.append(lax.ppermute(squares, "head", [(i, i ^ s) for i in range(n_head)]))
        while len(level) > 1:
            level = [a + b for a, b in zip(level[::2], level[1::2])]
        squares = level[0]
    lane = lax.broadcasted_iota(jnp.int32, (8, 128), 1)
    totals = jnp.sum(lax.all_gather(jnp.where(lane == 0, squares, loss_part), "ctx"), axis=0)
    totals, d_head_b = lax.optimization_barrier((totals, d_head_b))
    g_head_b = lax.all_to_all(d_head_b, "ctx", 0, 0, tiled=True)
    loss = totals[0, 1]
    grad_norm = jnp.sqrt(totals[0, 0])
    factor = jnp.minimum(1.0, clip_level / grad_norm)

    wide = 32
    spreads = (
        (1, 0, 0, ATTN_IN, D**-0.5),
        (2, 0, ATTN_IN, QG, (length / (4.0 * HEADS * HD)) ** 0.5),
        (0, 0, ATTN_IN + QG, 2 * FFG, D**-0.5),
        (0, 2 * FFG, ATTN_IN + QG + 2 * FFG, FFG, FF**-0.5),
    )
    layer = call_update(
        functools.partial(layer_update_kernel, spreads),
        factor,
        (g_ff, g_in, g_out),
        [
            pl.BlockSpec((wide, g_ff.shape[1]), lambda i: (i, 0)),
            pl.BlockSpec((wide, ATTN_IN), lambda i: (i, 0)),
            pl.BlockSpec((wide, QG), lambda i: (i, 0)),
        ],
        w_layer,
        mom_layer,
        avg_layer,
        wide,
        "layer_update",
    )
    g_head_a, *layer = lax.optimization_barrier((g_head_a, *layer))
    vocab = []
    steps = rows // 2 // (wide // 2)
    for first, g_head in ((0, g_head_a), (steps, g_head_b)):
        vocab = call_update(
            functools.partial(vocab_update_kernel, part),
            factor,
            (g_head, g_embed),
            [
                pl.BlockSpec((n_ctx, wide // 2, part), lambda i: (0, i, 0)),
                pl.BlockSpec((wide // 2, EMB_W), lambda i, first=first: (first + i, 0)),
            ],
            w_vocab,
            mom_vocab,
            avg_vocab,
            wide // 2,
            "vocab_update",
            (first, steps),
            vocab,
        )
    grad = factor * grad_gain
    gains_moment = momentum_rate * mom_gains + grad
    gains_new = gains - BASE * 0.1 * (grad + momentum_rate * gains_moment)
    gains_average = average_rate * avg_gains + (1.0 - average_rate) * gains_new
    return (
        *layer,
        *vocab,
        gains_new,
        gains_moment,
        gains_average,
        gains_new.astype(bf16),
        loss,
        grad_norm,
    )


def solution(mesh):
    token, split, gain = P("ctx"), P("ctx", "head"), P("ctx", None)
    in_specs = (token, token, token, P()) + (split, split, gain) * 3
    out_specs = (split,) * 8 + (gain,) * 4 + (P(), P())
    return jax.shard_map(local, mesh=mesh, in_specs=in_specs, out_specs=out_specs, check_vma=False)
```
